32 devices in a mesh: dp: 4 (over z), ctx: 8 (over y, x, core).
Axes of the slice: x: 2, y: 2, z: 4, core: 2. Of those that a mesh axis runs over, the one named last changes fastest.
Arguments:
- layer_in: bfloat16 [4, 4096, 2048], P('dp', 'ctx'), may hold values from -6 to 6
- positions: int32 [4, 4096], P('dp', 'ctx'), may hold values from 0 to 4095, as said below
- attn_gain: bfloat16 [2048], P(('dp', 'ctx')), may hold values from 0.5 to 1.5
- query_proj: bfloat16 [2048, 2048], P(('dp', 'ctx')), may hold values from -0.125 to 0.125
- key_proj: bfloat16 [2048, 256], P(('dp', 'ctx')), may hold values from -0.125 to 0.125
- value_proj: bfloat16 [2048, 256], P(('dp', 'ctx')), may hold values from -0.125 to 0.125
- merge_proj: bfloat16 [2048, 2048], P(('dp', 'ctx')), may hold values from -1 to 1
- ffn_gain: bfloat16 [2048], P(('dp', 'ctx')), may hold values from 0.5 to 1.5
- gate_proj: bfloat16 [2048, 5632], P(('dp', 'ctx')), may hold values from -0.125 to 0.125
- up_proj: bfloat16 [2048, 5632], P(('dp', 'ctx')), may hold values from -0.125 to 0.125
- down_proj: bfloat16 [5632, 2048], P(('dp', 'ctx')), may hold values from -0.078125 to 0.078125
- out_grad: bfloat16 [4, 4096, 2048], P('dp', 'ctx'), may hold values from -6 to 6
Outputs:
- layer_out: bfloat16 [4, 4096, 2048], P('dp', 'ctx')
- input_grad: bfloat16 [4, 4096, 2048], P('dp', 'ctx')
- attngain_grad: float32 [2048], P(('dp', 'ctx'))
- query_grad: float32 [2048, 2048], P(('dp', 'ctx'))
- key_grad: float32 [2048, 256], P(('dp', 'ctx'))
- value_grad: float32 [2048, 256], P(('dp', 'ctx'))
- merge_grad: float32 [2048, 2048], P(('dp', 'ctx'))
- ffngain_grad: float32 [2048], P(('dp', 'ctx'))
- gate_grad: float32 [2048, 5632], P(('dp', 'ctx'))
- up_grad: float32 [2048, 5632], P(('dp', 'ctx'))
- down_grad: float32 [5632, 2048], P(('dp', 'ctx'))
The draws below stay inside these ranges and needn't reach their ends.
Inputs may be any that keep to these rules, and one draw needn't show every extreme that they name: Each sequence's row holds every position 0 to 4095 once, in runs of 256 consecutive increasing positions that start at multiples of 256; the order of the runs is drawn per sequence.
All inputs are finite; a program needn't handle non-finite values.
Results may differ from the reference program's by a relative error of at most 0.02.
Values may be sent and summed in bfloat16 or wider, within the bound.
A program may use at most 384 MiB of HBM per device.

```python
import jax
import jax.numpy as jnp
from jax import lax

D = 2048
H = 32
KV = 4
HD = 64
FF = 5632
LENGTH = 4096
RUN = 256
SEQUENCES = 4


def draw_positions(key, part):
    keys = jax.random.split(key, SEQUENCES)
    runs = LENGTH // RUN

    def one_order(single):
        return jax.random.permutation(single, runs)
    orders = jax.vmap(one_order)(keys).astype(jnp.int32)
    offsets = jnp.arange(RUN, dtype=jnp.int32)
    placed = orders[:, :, None] * RUN + offsets[None, None, :]
    return placed.reshape(SEQUENCES, LENGTH)


def block_scale(stream_key, extent, shards, smallest, high):
    def one(position, blocks):
        steps = jax.random.uniform(jax.random.fold_in(jax.random.fold_in(stream_key, 6), position), (blocks,), jnp.float32, smallest / len(shards), high / len(shards))
        return jnp.repeat(jnp.exp(steps), extent[position] // blocks).reshape((-1,) + (1,) * (len(extent) - position - 1))

    loudness = one(*shards[0])
    for cut in shards[1:]:
        loudness = loudness * one(*cut)
    return loudness


def noise(own_key, shape, spread, most, cuts=(), held_as=jnp.bfloat16):
    entries = jax.random.normal(own_key, shape, jnp.float32) * spread
    if len(cuts) > 0:
        entries = block_scale(own_key, shape, cuts, -0.22, 0.18) * entries
    return jnp.clip(entries, min=-most, max=most).astype(held_as)


def setup_inputs(seed: int = 0) -> dict:
    key_list = jax.random.split(jax.random.key(seed), 13)
    layer_in = noise(key_list[0], (SEQUENCES, LENGTH, D), 1.0, 6.0, ((0, 4), (1, 8)))
    positions = draw_positions(jax.random.fold_in(key_list[12], 71), 0)
    attn_gain = jnp.clip(1.0 + 0.1 * jax.random.normal(key_list[2], (D,), jnp.float32), 0.5, 1.5).astype(jnp.bfloat16)
    query_proj = noise(key_list[3], (D, H * HD), D ** -0.5, 0.125, ((0, 32),))
    key_proj = noise(key_list[4], (D, KV * HD), D ** -0.5, 0.125, ((0, 32),))
    value_proj = noise(key_list[5], (D, KV * HD), D ** -0.5, 0.125, ((0, 32),))
    merge_proj = noise(key_list[6], (H * HD, D), (H * HD // 64) ** -0.5, 1.0, ((0, 32),))
    ffn_gain = jnp.clip(1.0 + 0.1 * jax.random.normal(key_list[7], (D,), jnp.float32), 0.5, 1.5).astype(jnp.bfloat16)
    gate_proj = noise(key_list[8], (D, FF), D ** -0.5, 0.125, ((0, 32),))
    up_proj = noise(key_list[9], (D, FF), D ** -0.5, 0.125, ((0, 32),))
    down_proj = noise(key_list[10], (FF, D), FF ** -0.5, 0.078125, ((0, 32),))
    out_grad = noise(key_list[11], (SEQUENCES, LENGTH, D), 1.0, 6.0, ((0, 4), (1, 8)))
    return {"layer_in": layer_in, "positions": positions, "attn_gain": attn_gain, "query_proj": query_proj, "key_proj": key_proj, "value_proj": value_proj, "merge_proj": merge_proj, "ffn_gain": ffn_gain, "gate_proj": gate_proj, "up_proj": up_proj, "down_proj": down_proj, "out_grad": out_grad}


EPS = 1e-05
NEG = -1e+30
HIGH = lax.Precision.HIGHEST

@jax.custom_vjp
def low(v):
    return lax.optimization_barrier(v.astype(jnp.bfloat16)).astype(jnp.float32)

@jax.custom_vjp
def low_back(v):
    return v

def low_keep(v):
    return (low(v), None)

def low_pass(kept, grad):
    return (grad,)

def back_keep(v):
    return (v, None)

def back_low(kept, grad):
    return (low(grad),)
low.defvjp(low_keep, low_pass)
low_back.defvjp(back_keep, back_low)

def matmul(left, right):
    return jnp.dot(left, right, preferred_element_type=jnp.float32, precision=HIGH)

def normalize(rows):
    return rows * lax.rsqrt(lax.optimization_barrier(jnp.mean(rows * rows, -1, keepdims=True)) + EPS)

def rotate(values, seq_pos):
    half = HD // 2
    freq = 10000.0 ** (-(jnp.arange(half, dtype=jnp.float32) * 2.0 / HD))
    turned = seq_pos.astype(jnp.float32)[:, None] * freq[None, :]
    cosine = jnp.cos(turned)[:, None, :]
    sine = jnp.sin(turned)[:, None, :]
    first = values[..., :half]
    second = values[..., half:]
    return jnp.concatenate([first * cosine - second * sine, second * cosine + first * sine], -1)

def attention(queries, keys, values, seq_pos):
    length = queries.shape[0]
    qblock = min(512, length)
    groups = H // KV
    scale = HD ** (-0.5)
    query_blocks = queries.reshape(length // qblock, qblock, KV, groups, HD)
    pos_blocks = seq_pos.reshape(length // qblock, qblock)

    def one_block(pair):
        query_part, query_pos = pair
        scores = jnp.einsum('qhgd,khd->hgqk', query_part, keys, precision=HIGH) * scale
        scores = low_back(scores)
        allowed = query_pos[:, None] >= seq_pos[None, :]
        scores = jnp.where(allowed, scores, NEG)
        top = lax.optimization_barrier(jnp.max(scores, -1, keepdims=True))
        weights = jnp.exp(scores - top)
        weights = weights / lax.optimization_barrier(jnp.sum(weights, -1, keepdims=True))
        mixed = jnp.einsum('hgqk,khd->qhgd', low(weights), values, precision=HIGH)
        return mixed.reshape(qblock, H * HD)
    outputs = lax.map(jax.checkpoint(one_block), (query_blocks, pos_blocks))
    return outputs.reshape(length, H * HD)

def forward(rows, seq_pos, attn_gain, query_proj, key_proj, value_proj, merge_proj, ffn_gain, gate_proj, up_proj, down_proj):
    length = rows.shape[0]
    first_in = low(normalize(rows) * attn_gain)
    queries = low_back(matmul(first_in, query_proj))
    keys = low_back(matmul(first_in, key_proj))
    values = low_back(matmul(first_in, value_proj))
    queries = low(rotate(queries.reshape(length, H, HD), seq_pos))
    keys = low(rotate(keys.reshape(length, KV, HD), seq_pos))
    values = low(values.reshape(length, KV, HD))
    mixed = low(low_back(attention(queries, keys, values, seq_pos)))
    middle = rows + low_back(matmul(mixed, merge_proj))
    second_in = low(normalize(middle) * ffn_gain)
    gate = low_back(matmul(second_in, gate_proj))
    lift = low_back(matmul(second_in, up_proj))
    hidden = low(jax.nn.silu(gate) * lift)
    return middle + matmul(hidden, down_proj)

def reference(layer_in, positions, attn_gain, query_proj, key_proj, value_proj, merge_proj, ffn_gain, gate_proj, up_proj, down_proj, out_grad):
    weights = tuple((item.astype(jnp.float32) for item in (attn_gain, query_proj, key_proj, value_proj, merge_proj, ffn_gain, gate_proj, up_proj, down_proj)))

    def one_sequence(totals, inputs):
        rows_in, seq_pos, seq_grad = inputs

        def local(rows, *params):
            return forward(rows, seq_pos, *params)
        result, back = jax.vjp(local, rows_in.astype(jnp.float32), *weights)
        grads = back(seq_grad.astype(jnp.float32))
        totals = tuple((total + grad for total, grad in zip(totals, grads[1:])))
        return (totals, (result.astype(jnp.bfloat16), grads[0].astype(jnp.bfloat16)))
    start = tuple((jnp.zeros(item.shape, jnp.float32) for item in weights))
    totals, produced = lax.scan(one_sequence, start, (layer_in, positions, out_grad))
    return (produced[0], produced[1], totals[0], totals[1], totals[2], totals[3], totals[4], totals[5], totals[6], totals[7], totals[8])
```

```python
import functools

import jax
import jax.numpy as jnp
from jax import lax
from jax.experimental import pallas as pl
from jax.experimental.pallas import tpu as pltpu
from jax.sharding import PartitionSpec as P

HD = 64
EPS = 1e-05
WIDE = 128
MASKED = -1e30
SCALE = HD**-0.5
LOG2E = 1.4426950408889634
TO_LOG2 = SCALE * LOG2E
BOTH = ("dp", "ctx")
F32 = jnp.float32
BF16 = jnp.bfloat16
NT = (((1,), (1,)), ((), ()))
NN = (((1,), (0,)), ((), ()))


def mm(left, right, dims):
    return lax.dot_general(left, right, dims, preferred_element_type=F32)


def later_in_run(keys, rows):
    run = rows // 2
    key = lax.broadcasted_iota(jnp.int32, (keys, rows), 0)
    query = lax.broadcasted_iota(jnp.int32, (keys, rows), 1)
    return (key > query) & ((key // run) == (query // run))


def attend_kernel(own_ref, qx_ref, kx_ref, vt_ref, o_ref, lse_ref, turned, *, pair):
    heads, rows, _ = qx_ref.shape
    kv_heads, length, _ = kx_ref.shape
    groups = heads // kv_heads
    own = own_ref[0]
    blocks = length // rows

    def scores(head, group, start):
        return mm(kx_ref[group, pl.ds(start, rows), :], qx_ref[head], NT) * TO_LOG2

    def weigh(probs, group, start):
        return mm(vt_ref[group, :, pl.ds(start, rows)], probs.astype(BF16), NN)

    def some_heads(index, _):
        members = [index * pair + i for i in range(pair)]
        group = members[0] // groups
        start = pl.multiple_of(own * rows, rows)
        blocked = later_in_run(rows, rows)
        state = []
        for head in members:
            s = jnp.where(blocked, MASKED, scores(head, group, start))
            top = jnp.max(s, 0, keepdims=True)
            state.append((top, weigh(jnp.exp2(s - top), group, start)))

        def step(j, state):
            start = pl.multiple_of(lax.rem(own + j, blocks) * rows, rows)
            raw = [scores(head, group, start) for head in members]
            result = []
            for (top, total), s in zip(state, raw):
                new_top = jnp.maximum(top, jnp.max(s, 0, keepdims=True))
                probs = jnp.exp2(s - new_top)
                result.append(
                    (new_top, total * jnp.exp2(top - new_top) + weigh(probs, group, start))
                )
            return result

        state = lax.fori_loop(1, blocks, step, state, unroll=True)
        for i, (head, (top, total)) in enumerate(zip(members, state)):
            weight_sum = total[HD : HD + 1, :]
            turned[i * HD : (i + 1) * HD, :] = total[:HD] / weight_sum
            lse_ref[pl.ds(head, 1), :] = top + jnp.log2(weight_sum)
        column = pl.multiple_of(index * (pair * HD), pair * HD)
        o_ref[:, pl.ds(column, pair * HD)] = turned[...].T
        return 0

    lax.fori_loop(0, heads // pair, some_heads, 0)


def attend(own, qx, kx, vt):
    heads, rows, _ = qx.shape
    length = kx.shape[1]
    pair = 2
    return pl.pallas_call(
        functools.partial(attend_kernel, pair=pair),
        out_shape=(
            jax.ShapeDtypeStruct((rows, heads * HD), F32),
            jax.ShapeDtypeStruct((heads, rows), F32),
        ),
        in_specs=[pl.BlockSpec(memory_space=pltpu.SMEM)]
        + [pl.BlockSpec(memory_space=pltpu.VMEM)] * 3,
        out_specs=(pl.BlockSpec(memory_space=pltpu.VMEM),) * 2,
        scratch_shapes=[pltpu.VMEM((pair * HD, rows), F32)],
        compiler_params=pltpu.CompilerParams(vmem_limit_bytes=48 << 20),
        cost_estimate=pl.CostEstimate(
            flops=16 * heads * rows * length * HD,
            bytes_accessed=2 * (qx.size + kx.size + vt.size) + 4 * rows * heads * HD,
            transcendentals=heads * rows * length,
        ),
        name="attend",
    )(own, qx, kx, vt)


def attend_back_kernel(own_ref, qx_ref, gx_ref, kx_ref, kt_ref, vx_ref, dq_ref, dkv_ref, *, pair):
    heads, rows, _ = qx_ref.shape
    kv_heads, length, _ = kx_ref.shape
    groups = heads // kv_heads
    own = own_ref[0]
    blocks = length // rows

    def kv_head(group, _):
        def block(index, diagonal):
            start = pl.multiple_of(index * rows, rows)

            def some_heads(i, sums):
                key_sum, value_sum = sums
                members = [group * groups + i * pair + t for t in range(pair)]
                key = kx_ref[group, pl.ds(start, rows), :]
                value = vx_ref[group, pl.ds(start, rows), :]
                key_turned = kt_ref[group, :, pl.ds(start, rows)]
                probs = [jnp.exp2(mm(key, qx_ref[h], NT) * TO_LOG2) for h in members]
                if diagonal:
                    blocked = later_in_run(rows, rows)
                    probs = [jnp.where(blocked, 0.0, p) for p in probs]
                slopes = [mm(value, gx_ref[h], NT) for h in members]
                grads = [(p * s).astype(BF16) for p, s in zip(probs, slopes)]
                for h, p, g in zip(members, probs, grads):
                    value_sum = value_sum + mm(p.astype(BF16), gx_ref[h], NN)
                    key_sum = key_sum + mm(g, qx_ref[h], NN)
                    term = mm(key_turned, g, NN)
                    dq_ref[h] = term if diagonal else dq_ref[h] + term
                return key_sum, value_sum

            zero = jnp.zeros((rows, WIDE), F32)
            key_sum, value_sum = lax.fori_loop(0, groups // pair, some_heads, (zero, zero))
            joined = jnp.concatenate([key_sum[:, :HD] * SCALE, value_sum[:, :HD]], 1)
            column = pl.multiple_of(group * WIDE, WIDE)
            dkv_ref[pl.ds(start, rows), pl.ds(column, WIDE)] = joined.astype(BF16)

        block(own, True)

        def rest(j, _):
            block(lax.rem(own + j, blocks), False)
            return 0

        lax.fori_loop(1, blocks, rest, 0)
        return 0

    lax.fori_loop(0, kv_heads, kv_head, 0)


def attend_back(own, qx, gx, kx, kt, vx):
    heads, rows, _ = qx.shape
    kv_heads, length, _ = kx.shape
    return pl.pallas_call(
        functools.partial(attend_back_kernel, pair=4),
        out_shape=(
            jax.ShapeDtypeStruct((heads, HD, rows), F32),
            jax.ShapeDtypeStruct((length, kv_heads * WIDE), BF16),
        ),
        in_specs=[pl.BlockSpec(memory_space=pltpu.SMEM)]
        + [pl.BlockSpec(memory_space=pltpu.VMEM)] * 5,
        out_specs=(pl.BlockSpec(memory_space=pltpu.VMEM),) * 2,
        compiler_params=pltpu.CompilerParams(vmem_limit_bytes=56 << 20),
        cost_estimate=pl.CostEstimate(
            flops=40 * heads * rows * length * HD,
            bytes_accessed=2 * (qx.size + gx.size + kx.size + kt.size + vx.size)
            + 4 * rows * heads * HD
            + 2 * length * kv_heads * WIDE,
            transcendentals=heads * rows * length,
        ),
        name="attend_back",
    )(own, qx, gx, kx, kt, vx)


def angles(positions, head_dim):
    half = head_dim // 2
    freq = 10000.0 ** (-(jnp.arange(half, dtype=F32) * 2.0 / head_dim))
    turned = positions.astype(F32)[..., None] * freq
    return (jnp.cos(turned)[:, None, :], jnp.sin(turned)[:, None, :])


def rotate(values, cosine, sine):
    half = values.shape[-1] // 2
    first = values[..., :half]
    second = values[..., half:]
    return jnp.concatenate([first * cosine - second * sine, second * cosine + first * sine], -1)


def normalize(rows):
    factor = lax.rsqrt(jnp.mean(rows * rows, -1, keepdims=True) + EPS)
    return (rows * factor, factor)


def norm_back(upstream, normed, factor, gain):
    scaled = upstream * gain
    inner = jnp.mean(scaled * normed, -1, keepdims=True)
    return (factor * (scaled - normed * inner), jnp.sum(upstream * normed, 0))


def rounded(values):
    return lax.reduce_precision(values, 8, 7)


def three_parts(values):
    high = rounded(values)
    middle = rounded(values - high)
    low = values - high - middle
    return jnp.stack([high, middle, low], -1).astype(BF16)


def widen(main, extra):
    pad = WIDE - main.shape[-1] - extra.shape[-1]
    return jnp.concatenate(
        [main, extra, jnp.zeros(main.shape[:-1] + (pad,), main.dtype)], -1
    )


def gather(piece):
    return lax.all_gather(piece, BOTH, axis=0, tiled=True)


def ctx_major(columns, n_dp, n_ctx):
    rows, width = columns.shape
    return (
        columns.reshape(rows, n_dp, n_ctx, width // (n_dp * n_ctx))
        .transpose(0, 2, 1, 3)
        .reshape(rows, width)
    )


def scatter(term):
    part = lax.psum_scatter(term, "ctx", scatter_dimension=0, tiled=True)
    return lax.psum_scatter(part, "dp", scatter_dimension=0, tiled=True).astype(F32)


def outer(left, right):
    return lax.dot_general(
        left, right, (((0,), (0,)), ((), ())), preferred_element_type=F32
    ).astype(BF16)


def body(
    n_dp,
    n_ctx,
    layer_in,
    positions,
    attn_gain,
    query_proj,
    key_proj,
    value_proj,
    merge_proj,
    ffn_gain,
    gate_proj,
    up_proj,
    down_proj,
    out_grad,
):
    _, rows, model = layer_in.shape
    kv_width = key_proj.shape[1]
    kv_heads = kv_width // HD
    width = query_proj.shape[1]
    heads = width // HD
    run = rows // 2
    positions = positions[0]
    own = lax.axis_index("ctx")
    own_ref = own.astype(jnp.int32).reshape(1)
    gains = jnp.stack([attn_gain, ffn_gain], -1)
    first_weights = gather(
        jnp.concatenate(
            [query_proj, key_proj, value_proj, widen(gains, gains[:, :0])], 1
        )
    )
    all_pos = lax.all_gather(positions, "ctx", axis=0, tiled=True)
    merge_all = gather(merge_proj)
    gate_all = gather(gate_proj)
    up_all = gather(up_proj)
    down_all = gather(down_proj)
    attn_all = first_weights[:, : width + 2 * kv_width]
    gain_one = first_weights[:, width + 2 * kv_width].astype(F32)
    gain_two = first_weights[:, width + 2 * kv_width + 1].astype(F32)

    cosine, sine = angles(positions, HD)
    rows_in = layer_in.reshape(rows, model).astype(F32)
    normed_one, factor_one = normalize(rows_in)
    first_in = (normed_one * gain_one).astype(BF16)
    raw = mm(first_in, attn_all, NN)
    queries = rotate(raw[:, :width].reshape(rows, heads, HD), cosine, sine).astype(BF16)
    keys = rotate(raw[:, width : width + kv_width].reshape(rows, kv_heads, HD), cosine, sine)
    keys = keys.astype(BF16).reshape(rows, kv_width)
    values = raw[:, width + kv_width :].astype(BF16)
    all_kv = lax.all_gather(jnp.concatenate([keys, values], 1), "ctx", axis=0, tiled=True)
    length = all_kv.shape[0]
    all_keys = all_kv[:, :kv_width].reshape(length, kv_heads, HD)
    all_values = all_kv[:, kv_width:].reshape(length, kv_heads, HD)

    run_starts = positions[::run]
    hidden_keys = all_pos[:, None] >= run_starts[None, :] + run
    bias = jnp.where(hidden_keys, MASKED, 0.0).astype(BF16)
    ones = jnp.ones((length, 3), BF16)
    key_extra = jnp.concatenate([bias, ones], 1)[None]
    kx = widen(
        all_keys.transpose(1, 0, 2), jnp.broadcast_to(key_extra, (kv_heads, length, 5))
    )
    kt = all_keys.transpose(1, 2, 0)
    vx = widen(
        all_values.transpose(1, 0, 2), jnp.broadcast_to(ones[None], (kv_heads, length, 3))
    )
    vt = jnp.concatenate(
        [
            all_values.transpose(1, 2, 0),
            jnp.ones((kv_heads, 1, length), BF16),
            jnp.zeros((kv_heads, 15, length), BF16),
        ],
        1,
    )
    queries = queries.transpose(1, 0, 2)
    in_run = (jnp.arange(rows)[:, None] // run == jnp.arange(2)[None, :]).astype(BF16)
    in_run = jnp.broadcast_to(in_run[None], (heads, rows, 2))
    attended, log_sum = attend(own_ref, widen(queries, in_run), kx, vt)

    mixed = attended.astype(BF16)
    middle = rows_in + mm(mixed, merge_all, NN)
    normed_two, factor_two = normalize(middle)
    second_in = (normed_two * gain_two).astype(BF16)
    gate = mm(second_in, gate_all, NN)
    lift = mm(second_in, up_all, NN)
    sigma = jax.nn.sigmoid(gate)
    activated = gate * sigma
    hidden = (activated * lift).astype(BF16)
    result = middle + mm(hidden, down_all, NN)
    layer_out = result.astype(BF16).reshape(layer_in.shape)

    grad_rows = out_grad.reshape(rows, model)
    down_share = scatter(outer(ctx_major(hidden, n_dp, n_ctx), grad_rows))
    grad_hidden = mm(grad_rows, down_all, NT)
    grad_gate = (grad_hidden * lift * sigma * (1.0 + gate * (1.0 - sigma))).astype(BF16)
    grad_lift = (grad_hidden * activated).astype(BF16)
    second_major = ctx_major(second_in, n_dp, n_ctx)
    gate_share = scatter(outer(second_major, grad_gate))
    up_share = scatter(outer(second_major, grad_lift))
    grad_second = mm(grad_gate, gate_all, NT) + mm(grad_lift, up_all, NT)
    grad_norm_two, gain_two_term = norm_back(grad_second, normed_two, factor_two, gain_two)
    grad_middle = grad_rows.astype(F32) + grad_norm_two
    grad_branch = grad_middle.astype(BF16)
    merge_share = scatter(outer(ctx_major(mixed, n_dp, n_ctx), grad_branch))
    grad_mixed = mm(grad_branch, merge_all, NT).astype(BF16)
    delta = jnp.sum((grad_mixed.astype(F32) * attended).reshape(rows, heads, HD), -1)
    grad_heads = grad_mixed.reshape(rows, heads, HD).transpose(1, 0, 2)
    gx = widen(grad_heads, three_parts(-delta.T))
    qx = widen(queries, jnp.concatenate([in_run, three_parts(log_sum * (-1.0 / TO_LOG2))], -1))
    dq, dkv = attend_back(own_ref, qx, gx, kx, kt, vx)
    dkv = lax.psum_scatter(dkv, "ctx", scatter_dimension=0, tiled=True).astype(F32)
    dkv = dkv.reshape(rows, kv_heads, 2, HD)
    grad_query = rotate(dq.transpose(2, 0, 1) * SCALE, cosine, -sine)
    grad_query = grad_query.reshape(rows, width).astype(BF16)
    grad_key = rotate(dkv[:, :, 0], cosine, -sine).reshape(rows, kv_width).astype(BF16)
    grad_value = dkv[:, :, 1].reshape(rows, kv_width).astype(BF16)
    grads = jnp.concatenate([grad_query, grad_key, grad_value], 1)
    grad_first = mm(grads, attn_all, NT)
    grad_norm_one, gain_one_term = norm_back(grad_first, normed_one, factor_one, gain_one)
    input_grad = (grad_middle + grad_norm_one).astype(BF16).reshape(layer_in.shape)
    gain_terms = jnp.stack([gain_one_term, gain_two_term], -1)
    gain_terms = ctx_major(gain_terms.T, n_dp, n_ctx).T.astype(BF16)
    first_major = ctx_major(first_in, n_dp, n_ctx)
    first_share = scatter(
        jnp.concatenate([outer(first_major, grads), widen(gain_terms, gain_terms[:, :0])], 1)
    )
    edge = width + kv_width
    return (
        layer_out,
        input_grad,
        first_share[:, edge + kv_width],
        first_share[:, :width],
        first_share[:, width:edge],
        first_share[:, edge : edge + kv_width],
        merge_share,
        first_share[:, edge + kv_width + 1],
        gate_share,
        up_share,
        down_share,
    )


def solution(mesh):
    acts = P("dp", "ctx", None)
    rows = P(BOTH, None)
    flat = P(BOTH)
    return jax.shard_map(
        functools.partial(body, mesh.shape["dp"], mesh.shape["ctx"]),
        mesh=mesh,
        in_specs=(acts, P("dp", "ctx"), flat, rows, rows, rows, rows, flat, rows, rows, rows, acts),
        out_specs=(acts, acts, flat, rows, rows, rows, rows, flat, rows, rows, rows),
        check_vma=False,
    )
```

```python
import functools

import jax
import jax.numpy as jnp
import numpy as np
from jax import lax
from jax.experimental import pallas as pl
from jax.experimental.pallas import tpu as pltpu
from jax.sharding import PartitionSpec as P

HD = 64
EPS = 1e-05
WIDE = 128
MASKED = -1e30
SCALE = HD**-0.5
LOG2E = 1.4426950408889634
TO_LOG2 = SCALE * LOG2E
F32 = jnp.float32
BF16 = jnp.bfloat16
NT = (((1,), (1,)), ((), ()))
NN = (((1,), (0,)), ((), ()))


def mm(left, right, dims):
    return lax.dot_general(left, right, dims, preferred_element_type=F32)


def same_run_later(keys, rows):
    run = rows // 2
    key = lax.broadcasted_iota(jnp.int32, (keys, rows), 0)
    query = lax.broadcasted_iota(jnp.int32, (keys, rows), 1)
    return (key > query) & ((key // run) == (query // run))


def split_heads(pair_ref, which, low_ref, high_ref):
    both = pair_ref[...]
    turned = pltpu.roll(both.astype(F32), HD, 1).astype(BF16)
    lane = lax.broadcasted_iota(jnp.int32, both.shape, 1)
    zero = jnp.zeros_like(both)
    first, second = (both, turned) if which == 0 else (turned, both)
    low_ref[...] = jnp.where(lane < HD, first, zero)
    high_ref[...] = jnp.where(lane < HD, zero, second)


def biased(scores, bias_ref, block, rows):
    run = rows // 2
    start = pl.multiple_of(block * rows, rows)
    parts = [
        scores[i * run : (i + 1) * run] + bias_ref[pl.ds(block * 2 + i, 1), :]
        for i in range(2)
    ]
    return jnp.concatenate(parts, 0)


def attend_kernel(own_ref, bias_ref, q_ref, kp_ref, vt_ref, o_ref, lse_ref, low, high, vx, turned, *, which, unroll):
    rows, width = q_ref.shape
    length = kp_ref.shape[0]
    own = own_ref[0]
    blocks = length // rows
    split_heads(kp_ref, which, low, high)
    vx[:HD, :] = vt_ref[...]
    top_row = lax.broadcasted_iota(jnp.int32, (16, length), 0) == 0
    vx[HD:, :] = top_row.astype(F32).astype(BF16)

    def scores(key, pair, block):
        start = pl.multiple_of(block * rows, rows)
        column = pl.multiple_of(pair * WIDE, WIDE)
        s = mm(key[pl.ds(start, rows), :], q_ref[:, pl.ds(column, WIDE)], NT) * TO_LOG2
        return biased(s, bias_ref, block, rows)

    def weigh(probs, block):
        start = pl.multiple_of(block * rows, rows)
        return mm(vx[:, pl.ds(start, rows)], probs.astype(BF16), NN)

    def one_pair(pair, _):
        blocked = same_run_later(rows, rows)
        state = []
        for key in (low, high):
            s = jnp.where(blocked, MASKED, scores(key, pair, own))
            top = jnp.max(s, 0, keepdims=True)
            state.append((top, weigh(jnp.exp2(s - top), own)))

        def step(j, state):
            block = lax.rem(own + j, blocks)
            raw = [scores(key, pair, block) for key in (low, high)]
            result = []
            for (top, total), s in zip(state, raw):
                new_top = jnp.maximum(top, jnp.max(s, 0, keepdims=True))
                probs = jnp.exp2(s - new_top)
                result.append((new_top, total * jnp.exp2(top - new_top) + weigh(probs, block)))
            return result

        state = lax.fori_loop(1, blocks, step, state, unroll=unroll)
        for i, (top, total) in enumerate(state):
            weight_sum = total[HD : HD + 1, :]
            turned[i * HD : (i + 1) * HD, :] = total[:HD] / weight_sum
            lse_ref[pl.ds(pair * 2 + i, 1), :] = top + jnp.log2(weight_sum)
        column = pl.multiple_of(pair * WIDE, WIDE)
        o_ref[:, pl.ds(column, WIDE)] = turned[...].T
        return 0

    lax.fori_loop(0, width // WIDE, one_pair, 0)


def attend(group, own, bias, q, kv, vt, unroll=True):
    rows, width = q.shape
    length = kv.shape[0]
    kv_heads = vt.shape[0] // HD
    mine = width // kv_heads
    heads = mine // HD
    return pl.pallas_call(
        functools.partial(attend_kernel, which=group % 2, unroll=unroll),
        grid=(1,),
        out_shape=(
            jax.ShapeDtypeStruct((rows, mine), F32),
            jax.ShapeDtypeStruct((heads, rows), F32),
        ),
        in_specs=[
            pl.BlockSpec(memory_space=pltpu.SMEM),
            pl.BlockSpec(bias.shape, lambda i: (0, 0)),
            pl.BlockSpec((rows, mine), lambda i: (0, group)),
            pl.BlockSpec((length, WIDE), lambda i: (0, group // 2)),
            pl.BlockSpec((HD, length), lambda i: (group, 0)),
        ],
        out_specs=(
            pl.BlockSpec((rows, mine), lambda i: (0, 0)),
            pl.BlockSpec((heads, rows), lambda i: (0, 0)),
        ),
        scratch_shapes=[
            pltpu.VMEM((length, WIDE), BF16),
            pltpu.VMEM((length, WIDE), BF16),
            pltpu.VMEM((HD + 16, length), BF16),
            pltpu.VMEM((WIDE, rows), F32),
        ],
        compiler_params=pltpu.CompilerParams(vmem_limit_bytes=40 << 20),
        cost_estimate=pl.CostEstimate(
            flops=16 * heads * rows * length * HD,
            bytes_accessed=2 * (rows * mine + 2 * length * WIDE) + 4 * rows * mine,
            transcendentals=heads * rows * length,
        ),
        name="attend",
    )(own, bias, q, kv, vt)


def attend_back_kernel(
    own_ref, bias_ref, lse_ref, o_ref, q_ref, g_ref, kp_ref, vp_ref, kt_ref,
    dq_ref, dkv_ref, k_low, k_high, v_low, v_high, dqt, delta_ref, *, which, unroll
):
    rows, width = q_ref.shape
    length = kp_ref.shape[0]
    own = own_ref[0]
    blocks = length // rows
    pairs = width // WIDE
    split_heads(kp_ref, which, k_low, k_high)
    split_heads(vp_ref, which, v_low, v_high)
    row = lax.broadcasted_iota(jnp.int32, (16, WIDE), 0)
    lane = lax.broadcasted_iota(jnp.int32, (16, WIDE), 1)
    chosen = (row == lane // HD).astype(F32).astype(BF16)
    for pair in range(pairs):
        column = pl.ds(pair * WIDE, WIDE)
        product = g_ref[:, column].astype(F32) * o_ref[:, column]
        main = product.astype(BF16)
        rest = (product - main.astype(F32)).astype(BF16)
        both = mm(chosen, main, NT) + mm(chosen, rest, NT)
        delta_ref[2 * pair : 2 * pair + 2, :] = both[:2]

    def block(index, diagonal):
        start = pl.multiple_of(index * rows, rows)

        def some_heads(i, sums):
            sums = list(sums)
            work = []
            for t in range(unroll):
                pair = i * unroll + t
                column = pl.multiple_of(pair * WIDE, WIDE)
                query = q_ref[:, pl.ds(column, WIDE)]
                grad = g_ref[:, pl.ds(column, WIDE)]
                for side, (key, value) in enumerate(((k_low, v_low), (k_high, v_high))):
                    head = pair * 2 + side
                    shift = -lse_ref[pl.ds(head, 1), :]
                    run = rows // 2
                    s = mm(key[pl.ds(start, rows), :], query, NT) * TO_LOG2
                    s = jnp.concatenate(
                        [
                            s[r * run : (r + 1) * run]
                            + (bias_ref[pl.ds(index * 2 + r, 1), :] + shift)
                            for r in range(2)
                        ],
                        0,
                    )
                    p = jnp.exp2(s)
                    if diagonal:
                        p = jnp.where(same_run_later(rows, rows), 0.0, p)
                    slope = mm(value[pl.ds(start, rows), :], grad, NT)
                    d = (p * (slope - delta_ref[pl.ds(head, 1), :])).astype(BF16)
                    work.append((side, pair, query, grad, p.astype(BF16), d))
            for side, pair, query, grad, p, d in work:
                sums[side] = sums[side] + mm(d, query, NN)
                sums[2 + side] = sums[2 + side] + mm(p, grad, NN)
                term = mm(kt_ref[:, pl.ds(start, rows)], d, NN)
                row = pl.multiple_of(pair * WIDE + side * HD, HD)
                if diagonal:
                    dqt[pl.ds(row, HD), :] = term
                else:
                    dqt[pl.ds(row, HD), :] += term
            return tuple(sums)

        zero = jnp.zeros((rows, WIDE), F32)
        sums = lax.fori_loop(0, pairs // unroll, some_heads, (zero,) * 4)
        lane = lax.broadcasted_iota(jnp.int32, (rows, WIDE), 1)
        key_sum = sums[0] + pltpu.roll(sums[1], HD, 1)
        value_sum = pltpu.roll(sums[2], HD, 1) + sums[3]
        dkv_ref[pl.ds(start, rows), :] = jnp.where(
            lane < HD, key_sum * SCALE, value_sum
        ).astype(BF16)

    block(own, True)

    def rest(j, _):
        block(lax.rem(own + j, blocks), False)
        return 0

    lax.fori_loop(1, blocks, rest, 0)
    for pair in range(pairs):
        dq_ref[:, pair * WIDE : (pair + 1) * WIDE] = (
            dqt[pair * WIDE : (pair + 1) * WIDE, :] * SCALE
        ).T


def attend_back(group, own, bias, lse, out, q, g, kv, kt, unroll=2):
    rows, width = q.shape
    length = kv.shape[0]
    kv_heads = kt.shape[0] // HD
    mine = width // kv_heads
    heads = mine // HD
    return pl.pallas_call(
        functools.partial(attend_back_kernel, which=group % 2, unroll=unroll),
        grid=(1,),
        out_shape=(
            jax.ShapeDtypeStruct((rows, mine), F32),
            jax.ShapeDtypeStruct((length, WIDE), BF16),
        ),
        in_specs=[
            pl.BlockSpec(memory_space=pltpu.SMEM),
            pl.BlockSpec(bias.shape, lambda i: (0, 0)),
            pl.BlockSpec((heads, rows), lambda i: (0, 0)),
            pl.BlockSpec((rows, mine), lambda i: (0, 0)),
            pl.BlockSpec((rows, mine), lambda i: (0, group)),
            pl.BlockSpec((rows, mine), lambda i: (0, group)),
            pl.BlockSpec((length, WIDE), lambda i: (0, group // 2)),
            pl.BlockSpec((length, WIDE), lambda i: (0, kv_heads // 2 + group // 2)),
            pl.BlockSpec((HD, length), lambda i: (group, 0)),
        ],
        out_specs=(
            pl.BlockSpec((rows, mine), lambda i: (0, 0)),
            pl.BlockSpec((length, WIDE), lambda i: (0, 0)),
        ),
        scratch_shapes=[pltpu.VMEM((length, WIDE), BF16)] * 4
        + [pltpu.VMEM((mine, rows), F32), pltpu.VMEM((heads, rows), F32)],
        compiler_params=pltpu.CompilerParams(vmem_limit_bytes=48 << 20),
        cost_estimate=pl.CostEstimate(
            flops=40 * heads * rows * length * HD,
            bytes_accessed=2 * (2 * rows * mine + 4 * length * WIDE) + 4 * rows * mine,
            transcendentals=heads * rows * length,
        ),
        name="attend_back",
    )(own, bias, lse, out, q, g, kv, kv, kt)


def turn_pairs(x, cosine, sine):
    lane = lax.broadcasted_iota(jnp.int32, x.shape, 1)
    swapped = jnp.where(
        lane % HD < HD // 2, pltpu.roll(x, WIDE - HD // 2, 1), pltpu.roll(x, HD // 2, 1)
    )
    return x * cosine + swapped * sine


def rotate_kernel(cos_ref, sin_ref, raw_ref, q_ref, kv_ref, *, kv_width):
    cosine, sine = cos_ref[...], sin_ref[...]
    width = q_ref.shape[1]
    for at in range(0, width, WIDE):
        q_ref[:, at : at + WIDE] = turn_pairs(raw_ref[:, at : at + WIDE], cosine, sine).astype(BF16)
    for at in range(0, kv_width, WIDE):
        column = slice(width + at, width + at + WIDE)
        kv_ref[:, at : at + WIDE] = turn_pairs(raw_ref[:, column], cosine, sine).astype(BF16)
    kv_ref[:, kv_width:] = raw_ref[:, width + kv_width :].astype(BF16)


def rotated(raw, cosine, sine, kv_width):
    rows, total = raw.shape
    return pl.pallas_call(
        functools.partial(rotate_kernel, kv_width=kv_width),
        out_shape=(
            jax.ShapeDtypeStruct((rows, total - 2 * kv_width), BF16),
            jax.ShapeDtypeStruct((rows, 2 * kv_width), BF16),
        ),
        in_specs=[pl.BlockSpec(memory_space=pltpu.VMEM)] * 3,
        out_specs=(pl.BlockSpec(memory_space=pltpu.VMEM),) * 2,
        compiler_params=pltpu.CompilerParams(vmem_limit_bytes=32 << 20),
        cost_estimate=pl.CostEstimate(
            flops=8 * raw.size, bytes_accessed=6 * raw.size, transcendentals=0
        ),
        name="rotated",
    )(cosine, sine, raw)


def unrotate_kernel(cos_ref, sin_ref, *refs, kv_heads):
    cosine, sine = cos_ref[...], -sin_ref[...]
    dqs, dkvs, out_ref = refs[:kv_heads], refs[kv_heads : 2 * kv_heads], refs[-1]
    mine = dqs[0].shape[1]
    lane = lax.broadcasted_iota(jnp.int32, cosine.shape, 1)
    for group in range(kv_heads):
        for at in range(0, mine, WIDE):
            turned = turn_pairs(dqs[group][:, at : at + WIDE], cosine, sine)
            out_ref[:, group * mine + at : group * mine + at + WIDE] = turned.astype(BF16)
    base = kv_heads * mine
    for i in range(kv_heads // 2):
        first, second = dkvs[2 * i][...].astype(F32), dkvs[2 * i + 1][...].astype(F32)
        keys = jnp.where(lane < HD, first, pltpu.roll(second, HD, 1))
        values = jnp.where(lane < HD, pltpu.roll(first, HD, 1), second)
        at = base + i * WIDE
        out_ref[:, at : at + WIDE] = turn_pairs(keys, cosine, sine).astype(BF16)
        at = base + kv_heads * HD + i * WIDE
        out_ref[:, at : at + WIDE] = values.astype(BF16)


def unrotated(dqs, dkvs, cosine, sine):
    rows, mine = dqs[0].shape
    kv_heads = len(dqs)
    total = kv_heads * (mine + 2 * HD)
    return pl.pallas_call(
        functools.partial(unrotate_kernel, kv_heads=kv_heads),
        out_shape=jax.ShapeDtypeStruct((rows, total), BF16),
        in_specs=[pl.BlockSpec(memory_space=pltpu.VMEM)] * (2 + 2 * kv_heads),
        out_specs=pl.BlockSpec(memory_space=pltpu.VMEM),
        compiler_params=pltpu.CompilerParams(vmem_limit_bytes=32 << 20),
        cost_estimate=pl.CostEstimate(
            flops=8 * rows * total, bytes_accessed=6 * rows * total, transcendentals=0
        ),
        name="unrotated",
    )(cosine, sine, *dqs, *dkvs)


BOTH = ("dp", "ctx")


class Grid:
    def __init__(self, n_dp, n_ctx):
        self.n_dp, self.n_a, self.n_b = n_dp, 2, n_ctx // 4
        self.n_ctx = n_ctx
        self.own = lax.axis_index("ctx").astype(jnp.int32)
        self.a = self.own // (2 * self.n_b)
        self.b = (self.own // 2) % self.n_b
        self.c = self.own % 2

    def size(self, axis):
        return {"a": self.n_a, "b": self.n_b, "c": 2}[axis]

    def next(self, values, axis):
        pairs = []
        for i in range(self.n_ctx):
            a, b, c = i // (2 * self.n_b), (i // 2) % self.n_b, i % 2
            if axis == "a":
                a = (a + 1) % self.n_a
            elif axis == "b":
                b = (b + 1) % self.n_b
            else:
                c = 1 - c
            pairs.append((i, (a * self.n_b + b) * 2 + c))
        return lax.ppermute(values, "ctx", pairs)

    def block_order(self, half_axes, core_major):
        half = self.n_dp // 2
        rows = []
        for core in range(2):
            for h, (first, second) in enumerate(half_axes):
                for i in range(self.size(first)):
                    for j in range(self.size(second)):
                        for d in range(half):
                            near = {first: i, second: j}
                            rows.append((core, h, near["a"], near["b"], h * half + d))
        rows = np.array(rows, np.int32)
        a = (self.a - rows[:, 2]) % self.n_a
        b = (self.b - rows[:, 3]) % self.n_b
        c = (self.c - rows[:, 0]) % 2
        return ((rows[:, 4] * self.n_a + a) * self.n_b + b) * 2 + c


HALVES = (("b", "a"), ("a", "b"))


def turn_kernel(order_ref, x_ref, o_ref, held, *, blk):
    tokens, width = x_ref.shape
    for i in range(width // WIDE):
        held[i * WIDE : (i + 1) * WIDE, :] = x_ref[:, i * WIDE : (i + 1) * WIDE].T

    def move(i, _):
        source = pl.multiple_of(order_ref[i] * blk, blk)
        target = pl.multiple_of(i * blk, blk)
        o_ref[pl.ds(target, blk), :] = held[pl.ds(source, blk), :]
        return 0

    lax.fori_loop(0, width // blk, move, 0)


def turned(x, order):
    tokens, width = x.shape
    blk = width // order.shape[0]
    if blk % 16:
        blocks = jnp.take(x.T.reshape(order.shape[0], blk, tokens), order, axis=0)
        return blocks.reshape(width, tokens)
    return pl.pallas_call(
        functools.partial(turn_kernel, blk=blk),
        out_shape=jax.ShapeDtypeStruct((width, tokens), x.dtype),
        in_specs=[
            pl.BlockSpec(memory_space=pltpu.SMEM),
            pl.BlockSpec(memory_space=pltpu.VMEM),
        ],
        out_specs=pl.BlockSpec(memory_space=pltpu.VMEM),
        scratch_shapes=[pltpu.VMEM((width, tokens), x.dtype)],
        compiler_params=pltpu.CompilerParams(vmem_limit_bytes=32 << 20),
        cost_estimate=pl.CostEstimate(flops=0, bytes_accessed=4 * x.size, transcendentals=0),
        name="turned",
    )(order, x)


def reduce_term(grid, left, right, extra=None):
    rows = left.shape[0]
    mine = rows // 2

    def term(start, size):
        part = mm(left[start : start + size], right, NN)
        if extra is not None:
            part = jnp.concatenate([part, extra[start : start + size].astype(F32)], 1)
        return part

    (arrived,) = yield [grid.next(term(mine, mine).astype(BF16), "c")]
    held = []
    for h, axes in enumerate(HALVES):
        start = h * (mine // 2)
        count = grid.size(axes[0])
        size = mine // 2 // count
        held.append(
            [
                (term(at, size) + arrived[at : at + size].astype(F32)).astype(BF16)
                for at in range(start, start + count * size, size)
            ]
        )
    for step in range(2):
        totals = [None, None]
        counts = [grid.size(axes[step]) for axes in HALVES]
        for k in range(1, max(counts)):
            live = [h for h in range(2) if k < counts[h]]
            sent = [
                grid.next(held[h][1] if k == 1 else totals[h], HALVES[h][step]) for h in live
            ]
            came = yield sent
            for h, part in zip(live, came):
                own = held[h][(k + 1) % counts[h]]
                totals[h] = (part.astype(F32) + own.astype(F32)).astype(BF16)
        if step == 0:
            held = []
            for h, total in enumerate(totals):
                count = grid.size(HALVES[h][1])
                size = total.shape[0] // count
                held.append([total[j * size : (j + 1) * size] for j in range(count)])
    joined = jnp.concatenate(totals, 0)
    (share,) = yield [lax.psum_scatter(joined, "dp", scatter_dimension=0, tiled=True)]
    return share.astype(F32)


def place_kernel(order_ref, *refs, sources, slots):
    pieces = refs[: -(3 + 1)]
    out_ref, held, in_sem, out_sem = refs[-4:]
    count = len(sources)

    def fetch(i):
        piece, place = sources[i]
        return pltpu.make_async_copy(
            pieces[piece].at[place], held.at[i % slots], in_sem.at[i % slots]
        )

    def store(i):
        return pltpu.make_async_copy(
            held.at[i % slots], out_ref.at[order_ref[i]], out_sem.at[i % slots]
        )

    ahead = slots // 2
    for i in range(min(ahead, count)):
        fetch(i).start()
    for i in range(count):
        fetch(i).wait()
        store(i).start()
        later = i + ahead
        if later < count:
            if later >= slots:
                store(later - slots).wait()
            fetch(later).start()
    for i in range(max(0, count - slots), count):
        store(i).wait()


def placed(order, pieces):
    blk, width = pieces[0].shape[-2:]
    flat = [p.reshape((-1, blk, width)) for p in pieces]
    sources = [(n, j) for n, p in enumerate(flat) for j in range(p.shape[0])]
    slots = 8
    whole = pl.pallas_call(
        functools.partial(place_kernel, sources=sources, slots=slots),
        out_shape=jax.ShapeDtypeStruct((len(sources), blk, width), flat[0].dtype),
        in_specs=[pl.BlockSpec(memory_space=pltpu.SMEM)]
        + [pl.BlockSpec(memory_space=pl.ANY)] * len(flat),
        out_specs=pl.BlockSpec(memory_space=pl.ANY),
        scratch_shapes=[
            pltpu.VMEM((slots, blk, width), flat[0].dtype),
            pltpu.SemaphoreType.DMA((slots,)),
            pltpu.SemaphoreType.DMA((slots,)),
        ],
        compiler_params=pltpu.CompilerParams(vmem_limit_bytes=16 << 20),
        cost_estimate=pl.CostEstimate(
            flops=0, bytes_accessed=4 * len(sources) * blk * width, transcendentals=0
        ),
        name="placed",
    )(order, *flat)
    return whole.reshape(len(sources) * blk, width)


def gather_weight(grid, weight, order):
    (column,) = yield [lax.all_gather(weight, "dp", axis=0)]
    half = grid.n_dp // 2
    parts = [column[:half], column[half:]]
    steps = [[parts[0]], [parts[1]]]
    for stage in (1, 0):
        counts = [grid.size(axes[stage]) for axes in HALVES]
        for k in range(1, max(counts)):
            live = [h for h in range(2) if k < counts[h]]
            came = yield [grid.next(steps[h][-1], HALVES[h][stage]) for h in live]
            for h, part in zip(live, came):
                steps[h].append(part)
        if stage == 1:
            steps = [[jnp.stack(s)] for s in steps]
    near = steps[0] + steps[1]
    far = yield [grid.next(piece, "c") for piece in near]
    return placed(order, near + list(far))


class Chain:
    def __init__(self, generator):
        self.generator, self.done, self.result = generator, False, None
        self.flight = next(generator)

    def advance(self, arrived):
        try:
            self.flight = self.generator.send(arrived)
        except StopIteration as stop:
            self.done, self.result, self.flight = True, stop.value, []


def meet(main, *chains):
    chains = [c for c in chains if not c.done]
    main, flights = lax.optimization_barrier((main, [list(c.flight) for c in chains]))
    for chain, flight in zip(chains, flights):
        chain.advance(flight)
    return main


def finish(chain):
    while not chain.done:
        chain.advance(chain.flight)
    return chain.result


def angles(positions):
    lane = jnp.arange(WIDE)
    freq = 10000.0 ** (-((lane % (HD // 2)).astype(F32) * 2.0 / HD))
    turn = positions.astype(F32)[:, None] * freq[None, :]
    sign = jnp.where(lane % HD < HD // 2, -1.0, 1.0)
    return jnp.cos(turn), jnp.sin(turn) * sign[None, :]


def normalize(rows):
    factor = lax.rsqrt(jnp.mean(rows * rows, -1, keepdims=True) + EPS)
    return (rows * factor, factor)


def norm_back(upstream, normed, factor, gain):
    scaled = upstream * gain
    inner = jnp.mean(scaled * normed, -1, keepdims=True)
    return (factor * (scaled - normed * inner), jnp.sum(upstream * normed, 0))


def body(
    n_dp,
    n_ctx,
    layer_in,
    positions,
    attn_gain,
    query_proj,
    key_proj,
    value_proj,
    merge_proj,
    ffn_gain,
    gate_proj,
    up_proj,
    down_proj,
    out_grad,
):
    _, rows, model = layer_in.shape
    kv_width = key_proj.shape[1]
    kv_heads = kv_width // HD
    width = query_proj.shape[1]
    heads = width // HD
    run = rows // 2
    positions = positions[0]
    grid = Grid(n_dp, n_ctx)
    own = grid.own.reshape(1)
    order = grid.block_order(HALVES, True)

    gains = jnp.stack([attn_gain, ffn_gain], -1)
    gains = jnp.concatenate([gains, jnp.zeros((gains.shape[0], WIDE - 2), BF16)], 1)
    packed = jnp.concatenate([query_proj, key_proj, value_proj, gains], 1)
    first_chain = Chain(gather_weight(grid, packed, order))
    (gate_proj,) = meet((gate_proj,))
    gate_chain = Chain(gather_weight(grid, gate_proj, order))
    merge_chain = Chain(gather_weight(grid, merge_proj, order))
    up_chain = Chain(gather_weight(grid, up_proj, order))
    down_chain = Chain(gather_weight(grid, down_proj, order))
    all_pos = lax.all_gather(positions[::run], "ctx", axis=0, tiled=True)
    cosine, sine = angles(positions)
    rows_in = layer_in.reshape(rows, model).astype(F32)
    normed_one, factor_one = normalize(rows_in)
    first_weights = finish(first_chain)
    attn_all = first_weights[:, : width + 2 * kv_width]
    gain_one = first_weights[:, width + 2 * kv_width].astype(F32)
    gain_two = first_weights[:, width + 2 * kv_width + 1].astype(F32)

    first_in = (normed_one * gain_one).astype(BF16)
    raw = mm(first_in, attn_all, NN)
    raw = meet(raw, gate_chain)
    queries, own_kv = rotated(raw, cosine, sine, kv_width)
    all_kv = lax.all_gather(own_kv, "ctx", axis=0, tiled=True)
    turned_kv = all_kv.T
    kt, vt = turned_kv[:kv_width], turned_kv[kv_width:]
    later = all_pos[:, None] > jnp.repeat(positions[::run], run)[None, :]
    bias = jnp.where(later, MASKED, 0.0).astype(F32)

    queries, vt = meet((queries, vt), gate_chain, merge_chain)
    plan = (
        (merge_chain,),
        (gate_chain, up_chain),
        (merge_chain, up_chain),
        (gate_chain, merge_chain, down_chain),
    )
    outs, log_sums = [], []
    for group in range(kv_heads):
        out, log_sum = attend(group, own, bias, queries, all_kv, vt)
        queries, out = meet((queries, out), *plan[group % 4])
        outs.append(out)
        log_sums.append(log_sum)
    mixed = jnp.concatenate([out.astype(BF16) for out in outs], 1)
    merge_all = finish(merge_chain)
    gate_all = finish(gate_chain)
    middle = rows_in + mm(mixed, merge_all, NN)
    middle = meet(middle, up_chain)
    normed_two, factor_two = normalize(middle)
    second_in = (normed_two * gain_two).astype(BF16)
    gate = mm(second_in, gate_all, NN)
    gate = meet(gate, up_chain, down_chain)
    up_all = finish(up_chain)
    lift = mm(second_in, up_all, NN)
    sigma = jax.nn.sigmoid(gate)
    activated = gate * sigma
    hidden = (activated * lift).astype(BF16)
    hidden = meet(hidden, down_chain)
    down_all = finish(down_chain)
    grad_rows = out_grad.reshape(rows, model)

    down_chain = Chain(reduce_term(grid, turned(hidden, order), grad_rows))
    result = middle + mm(hidden, down_all, NN)
    layer_out = result.astype(BF16).reshape(layer_in.shape)
    grad_hidden = mm(grad_rows, down_all, NT)
    grad_gate = (grad_hidden * lift * sigma * (1.0 + gate * (1.0 - sigma))).astype(BF16)
    grad_lift = (grad_hidden * activated).astype(BF16)
    grad_gate, grad_lift, layer_out = meet((grad_gate, grad_lift, layer_out), down_chain)
    second_turned = turned(second_in, order)
    gate_chain = Chain(reduce_term(grid, second_turned, grad_gate))
    up_chain = Chain(reduce_term(grid, second_turned, grad_lift))
    grad_second = mm(grad_gate, gate_all, NT) + mm(grad_lift, up_all, NT)
    grad_second = meet(grad_second, gate_chain, up_chain)
    grad_norm_two, gain_two_term = norm_back(grad_second, normed_two, factor_two, gain_two)
    grad_middle = grad_rows.astype(F32) + grad_norm_two
    grad_branch = grad_middle.astype(BF16)
    merge_chain = Chain(reduce_term(grid, turned(mixed, order), grad_branch))
    grad_mixed = mm(grad_branch, merge_all, NT).astype(BF16)
    grad_mixed = meet(grad_mixed, down_chain, merge_chain)
    plan = (
        (down_chain, gate_chain),
        (up_chain, gate_chain, merge_chain),
        (up_chain, merge_chain),
        (),
    )
    dqs, dkvs = [], []
    for group in range(kv_heads):
        dq, dkv = attend_back(
            group, own, bias, log_sums[group], outs[group], queries, grad_mixed, all_kv, kt
        )
        dq, grad_mixed, dkv = meet((dq, grad_mixed, dkv), *plan[group % 4])
        dqs.append(dq)
        dkvs.append(lax.psum_scatter(dkv, "ctx", scatter_dimension=0, tiled=True))
    first_turned = turned(first_in, order)
    grads = unrotated(dqs, dkvs, cosine, sine)
    grad_first = mm(grads, attn_all, NT)
    grad_norm_one, gain_one_term = norm_back(grad_first, normed_one, factor_one, gain_one)
    gain_terms = jnp.stack([gain_one_term, gain_two_term], 0)
    gain_terms = jnp.concatenate([gain_terms, jnp.zeros((WIDE - 2, model), F32)], 0)
    first_chain = Chain(
        reduce_term(grid, first_turned, grads, turned(gain_terms.astype(BF16), order))
    )
    input_grad = (grad_middle + grad_norm_one).astype(BF16).reshape(layer_in.shape)
    first_share = finish(first_chain)
    merge_share, gate_share = finish(merge_chain), finish(gate_chain)
    up_share, down_share = finish(up_chain), finish(down_chain)
    edge = width + kv_width
    return (
        layer_out,
        input_grad,
        first_share[:, edge + kv_width],
        first_share[:, :width],
        first_share[:, width:edge],
        first_share[:, edge : edge + kv_width],
        merge_share,
        first_share[:, edge + kv_width + 1],
        gate_share,
        up_share,
        down_share,
    )


def solution(mesh):
    acts = P("dp", "ctx", None)
    rows = P(BOTH, None)
    flat = P(BOTH)
    return jax.shard_map(
        functools.partial(body, mesh.shape["dp"], mesh.shape["ctx"]),
        mesh=mesh,
        in_specs=(acts, P("dp", "ctx"), flat, rows, rows, rows, rows, flat, rows, rows, rows, acts),
        out_specs=(acts, acts, flat, rows, rows, rows, rows, flat, rows, rows, rows),
        check_vma=False,
    )
```

```python
import functools

import jax
import jax.numpy as jnp
import numpy as np
from jax import lax
from jax.experimental import pallas as pl
from jax.experimental.pallas import tpu as pltpu
from jax.sharding import PartitionSpec as P

HD = 64
EPS = 1e-05
WIDE = 128
MASKED = -1e30
SCALE = HD**-0.5
LOG2E = 1.4426950408889634
TO_LOG2 = SCALE * LOG2E
F32 = jnp.float32
BF16 = jnp.bfloat16
NT = (((1,), (1,)), ((), ()))
NN = (((1,), (0,)), ((), ()))


def mm(left, right, dims):
    return lax.dot_general(left, right, dims, preferred_element_type=F32)


def same_run_later(keys, rows):
    run = rows // 2
    key = lax.broadcasted_iota(jnp.int32, (keys, rows), 0)
    query = lax.broadcasted_iota(jnp.int32, (keys, rows), 1)
    return (key > query) & ((key // run) == (query // run))


def split_heads(pair_ref, which, low_ref, high_ref):
    both = pair_ref[...]
    turned = pltpu.roll(both.astype(F32), HD, 1).astype(BF16)
    lane = lax.broadcasted_iota(jnp.int32, both.shape, 1)
    zero = jnp.zeros_like(both)
    first, second = (both, turned) if which == 0 else (turned, both)
    low_ref[...] = jnp.where(lane < HD, first, zero)
    high_ref[...] = jnp.where(lane < HD, zero, second)


def biased(scores, bias_ref, block, rows):
    run = rows // 2
    start = pl.multiple_of(block * rows, rows)
    parts = [
        scores[i * run : (i + 1) * run] + bias_ref[pl.ds(block * 2 + i, 1), :]
        for i in range(2)
    ]
    return jnp.concatenate(parts, 0)


def attend_kernel(
    bias_ref, q_ref, kp_ref, vt_ref, o_ref, lse_ref, low, high, vx, turned, *, which, places
):
    rows, width = q_ref.shape
    length = kp_ref.shape[0]
    blocks = length // rows
    split_heads(kp_ref, which, low, high)
    vx[:HD, :] = vt_ref[...]
    top_row = lax.broadcasted_iota(jnp.int32, (16, length), 0) == 0
    vx[HD:, :] = top_row.astype(F32).astype(BF16)

    def scores(key, pair, block):
        start = pl.multiple_of(block * rows, rows)
        column = pl.multiple_of(pair * WIDE, WIDE)
        s = mm(key[pl.ds(start, rows), :], q_ref[:, pl.ds(column, WIDE)], NT) * TO_LOG2
        return biased(s, bias_ref, block, rows)

    def weigh(probs, block):
        start = places[block] * rows
        return mm(vx[:, start : start + rows], probs.astype(BF16), NN)

    def one_pair(pair, _):
        blocked = same_run_later(rows, rows)
        state = []
        for key in (low, high):
            s = jnp.where(blocked, MASKED, scores(key, pair, 0))
            top = jnp.max(s, 0, keepdims=True)
            state.append((top, weigh(jnp.exp2(s - top), 0)))

        def step(block, state):
            raw = [scores(key, pair, block) for key in (low, high)]
            result = []
            for (top, total), s in zip(state, raw):
                new_top = jnp.maximum(top, jnp.max(s, 0, keepdims=True))
                probs = jnp.exp2(s - new_top)
                result.append((new_top, total * jnp.exp2(top - new_top) + weigh(probs, block)))
            return result

        for block in range(1, blocks):
            state = step(block, state)
        for i, (top, total) in enumerate(state):
            weight_sum = total[HD : HD + 1, :]
            turned[i * HD : (i + 1) * HD, :] = total[:HD] / weight_sum
            lse_ref[pl.ds(pair * 2 + i, 1), :] = top + jnp.log2(weight_sum)
        column = pl.multiple_of(pair * WIDE, WIDE)
        o_ref[:, pl.ds(column, WIDE)] = turned[...].T
        return 0

    lax.fori_loop(0, width // WIDE, one_pair, 0)


def attend(group, places, bias, q, keys, vt):
    rows, width = q.shape
    length = keys.shape[0]
    kv_heads = vt.shape[0] // HD
    mine = width // kv_heads
    heads = mine // HD
    return pl.pallas_call(
        functools.partial(attend_kernel, which=group % 2, places=places),
        grid=(1,),
        out_shape=(
            jax.ShapeDtypeStruct((rows, mine), F32),
            jax.ShapeDtypeStruct((heads, rows), F32),
        ),
        in_specs=[
            pl.BlockSpec(bias.shape, lambda i: (0, 0)),
            pl.BlockSpec((rows, mine), lambda i: (0, group)),
            pl.BlockSpec((length, WIDE), lambda i: (0, group // 2)),
            pl.BlockSpec((HD, length), lambda i: (group, 0)),
        ],
        out_specs=(
            pl.BlockSpec((rows, mine), lambda i: (0, 0)),
            pl.BlockSpec((heads, rows), lambda i: (0, 0)),
        ),
        scratch_shapes=[
            pltpu.VMEM((length, WIDE), BF16),
            pltpu.VMEM((length, WIDE), BF16),
            pltpu.VMEM((HD + 16, length), BF16),
            pltpu.VMEM((WIDE, rows), F32),
        ],
        compiler_params=pltpu.CompilerParams(vmem_limit_bytes=40 << 20),
        cost_estimate=pl.CostEstimate(
            flops=16 * heads * rows * length * HD,
            bytes_accessed=2 * (rows * mine + 2 * length * WIDE) + 4 * rows * mine,
            transcendentals=heads * rows * length,
        ),
        name="attend",
    )(bias, q, keys, vt)


def attend_back_kernel(
    order_ref, place_ref, bias_ref, lse_ref, o_ref, q_ref, g_ref, kp_ref, vp_ref, kt_ref,
    dq_ref, dkv_ref, k_low, k_high, v_low, v_high, dqt, delta_ref, *, which, unroll
):
    rows, width = q_ref.shape
    length = kp_ref.shape[0]
    blocks = length // rows
    pairs = width // WIDE
    split_heads(kp_ref, which, k_low, k_high)
    split_heads(vp_ref, which, v_low, v_high)
    row = lax.broadcasted_iota(jnp.int32, (16, WIDE), 0)
    lane = lax.broadcasted_iota(jnp.int32, (16, WIDE), 1)
    chosen = (row == lane // HD).astype(F32).astype(BF16)
    for pair in range(pairs):
        column = pl.ds(pair * WIDE, WIDE)
        product = g_ref[:, column].astype(F32) * o_ref[:, column]
        main = product.astype(BF16)
        rest = (product - main.astype(F32)).astype(BF16)
        both = mm(chosen, main, NT) + mm(chosen, rest, NT)
        delta_ref[2 * pair : 2 * pair + 2, :] = both[:2]

    def block(index, diagonal):
        start = pl.multiple_of(index * rows, rows)
        value_start = pl.multiple_of(place_ref[index] * rows, rows)

        def some_heads(i, sums):
            sums = list(sums)
            work = []
            for t in range(unroll):
                pair = i * unroll + t
                column = pl.multiple_of(pair * WIDE, WIDE)
                query = q_ref[:, pl.ds(column, WIDE)]
                grad = g_ref[:, pl.ds(column, WIDE)]
                for side, (key, value) in enumerate(((k_low, v_low), (k_high, v_high))):
                    head = pair * 2 + side
                    shift = -lse_ref[pl.ds(head, 1), :]
                    run = rows // 2
                    s = mm(key[pl.ds(start, rows), :], query, NT) * TO_LOG2
                    s = jnp.concatenate(
                        [
                            s[r * run : (r + 1) * run]
                            + (bias_ref[pl.ds(index * 2 + r, 1), :] + shift)
                            for r in range(2)
                        ],
                        0,
                    )
                    p = jnp.exp2(s)
                    if diagonal:
                        p = jnp.where(same_run_later(rows, rows), 0.0, p)
                    slope = mm(value[pl.ds(value_start, rows), :], grad, NT)
                    d = (p * (slope - delta_ref[pl.ds(head, 1), :])).astype(BF16)
                    work.append((side, pair, query, grad, p.astype(BF16), d))
            for side, pair, query, grad, p, d in work:
                sums[side] = sums[side] + mm(d, query, NN)
                sums[2 + side] = sums[2 + side] + mm(p, grad, NN)
                term = mm(kt_ref[:, pl.ds(start, rows)], d, NN)
                row = pl.multiple_of(pair * WIDE + side * HD, HD)
                if diagonal:
                    dqt[pl.ds(row, HD), :] = term
                else:
                    dqt[pl.ds(row, HD), :] += term
            return tuple(sums)

        zero = jnp.zeros((rows, WIDE), F32)
        sums = lax.fori_loop(0, pairs // unroll, some_heads, (zero,) * 4)
        lane = lax.broadcasted_iota(jnp.int32, (rows, WIDE), 1)
        key_sum = sums[0] + pltpu.roll(sums[1], HD, 1)
        value_sum = pltpu.roll(sums[2], HD, 1) + sums[3]
        place = pl.multiple_of(order_ref[index] * rows, rows)
        dkv_ref[pl.ds(place, rows), :] = jnp.where(
            lane < HD, key_sum * SCALE, value_sum
        ).astype(BF16)

    block(0, True)

    def rest(j, _):
        block(j, False)
        return 0

    lax.fori_loop(1, blocks, rest, 0)
    for pair in range(pairs):
        dq_ref[:, pair * WIDE : (pair + 1) * WIDE] = (
            dqt[pair * WIDE : (pair + 1) * WIDE, :] * SCALE
        ).T


def attend_back(group, order, places, bias, lse, out, q, g, keys, values, kt, unroll=2):
    rows, width = q.shape
    length = keys.shape[0]
    kv_heads = kt.shape[0] // HD
    mine = width // kv_heads
    heads = mine // HD
    return pl.pallas_call(
        functools.partial(attend_back_kernel, which=group % 2, unroll=unroll),
        grid=(1,),
        out_shape=(
            jax.ShapeDtypeStruct((rows, mine), F32),
            jax.ShapeDtypeStruct((length, WIDE), BF16),
        ),
        in_specs=[
            pl.BlockSpec(memory_space=pltpu.SMEM),
            pl.BlockSpec(memory_space=pltpu.SMEM),
            pl.BlockSpec(bias.shape, lambda i: (0, 0)),
            pl.BlockSpec((heads, rows), lambda i: (0, 0)),
            pl.BlockSpec((rows, mine), lambda i: (0, 0)),
            pl.BlockSpec((rows, mine), lambda i: (0, group)),
            pl.BlockSpec((rows, mine), lambda i: (0, group)),
            pl.BlockSpec((length, WIDE), lambda i: (0, group // 2)),
            pl.BlockSpec((length, WIDE), lambda i: (0, group // 2)),
            pl.BlockSpec((HD, length), lambda i: (group, 0)),
        ],
        out_specs=(
            pl.BlockSpec((rows, mine), lambda i: (0, 0)),
            pl.BlockSpec((length, WIDE), lambda i: (0, 0)),
        ),
        scratch_shapes=[pltpu.VMEM((length, WIDE), BF16)] * 4
        + [pltpu.VMEM((mine, rows), F32), pltpu.VMEM((heads, rows), F32)],
        compiler_params=pltpu.CompilerParams(vmem_limit_bytes=48 << 20),
        cost_estimate=pl.CostEstimate(
            flops=40 * heads * rows * length * HD,
            bytes_accessed=2 * (2 * rows * mine + 4 * length * WIDE) + 4 * rows * mine,
            transcendentals=heads * rows * length,
        ),
        name="attend_back",
    )(order, jnp.array(places, jnp.int32), bias, lse, out, q, g, keys, values, kt)


def turn_pairs(x, cosine, sine):
    lane = lax.broadcasted_iota(jnp.int32, x.shape, 1)
    swapped = jnp.where(
        lane % HD < HD // 2, pltpu.roll(x, WIDE - HD // 2, 1), pltpu.roll(x, HD // 2, 1)
    )
    return x * cosine + swapped * sine


def rotate_kernel(cos_ref, sin_ref, raw_ref, q_ref, kv_ref, *, kv_width):
    cosine, sine = cos_ref[...], sin_ref[...]
    width = q_ref.shape[1]
    for at in range(0, width, WIDE):
        q_ref[:, at : at + WIDE] = turn_pairs(raw_ref[:, at : at + WIDE], cosine, sine).astype(BF16)
    for at in range(0, kv_width, WIDE):
        column = slice(width + at, width + at + WIDE)
        kv_ref[:, at : at + WIDE] = turn_pairs(raw_ref[:, column], cosine, sine).astype(BF16)
    kv_ref[:, kv_width:] = raw_ref[:, width + kv_width :].astype(BF16)


def rotated(raw, cosine, sine, kv_width):
    rows, total = raw.shape
    return pl.pallas_call(
        functools.partial(rotate_kernel, kv_width=kv_width),
        out_shape=(
            jax.ShapeDtypeStruct((rows, total - 2 * kv_width), BF16),
            jax.ShapeDtypeStruct((rows, 2 * kv_width), BF16),
        ),
        in_specs=[pl.BlockSpec(memory_space=pltpu.VMEM)] * 3,
        out_specs=(pl.BlockSpec(memory_space=pltpu.VMEM),) * 2,
        compiler_params=pltpu.CompilerParams(vmem_limit_bytes=32 << 20),
        cost_estimate=pl.CostEstimate(
            flops=8 * raw.size, bytes_accessed=6 * raw.size, transcendentals=0
        ),
        name="rotated",
    )(cosine, sine, raw)


def unrotate_queries_kernel(cos_ref, sin_ref, *refs):
    cosine, sine = cos_ref[...], -sin_ref[...]
    out_ref = refs[-1]
    mine = refs[0].shape[1]
    for n, ref in enumerate(refs[:-1]):
        for at in range(0, mine, WIDE):
            turned = turn_pairs(ref[:, at : at + WIDE], cosine, sine)
            out_ref[:, n * mine + at : n * mine + at + WIDE] = turned.astype(BF16)


def unrotate_keys_kernel(cos_ref, sin_ref, *refs):
    cosine, sine = cos_ref[...], -sin_ref[...]
    out_ref = refs[-1]
    count = len(refs) - 1
    lane = lax.broadcasted_iota(jnp.int32, cosine.shape, 1)
    for i in range(count // 2):
        first, second = refs[2 * i][...].astype(F32), refs[2 * i + 1][...].astype(F32)
        keys = jnp.where(lane < HD, first, pltpu.roll(second, HD, 1))
        values = jnp.where(lane < HD, pltpu.roll(first, HD, 1), second)
        at = i * WIDE
        out_ref[:, at : at + WIDE] = turn_pairs(keys, cosine, sine).astype(BF16)
        at = count * HD + i * WIDE
        out_ref[:, at : at + WIDE] = values.astype(BF16)


def unrotated(kernel, parts, cosine, sine):
    rows, mine = parts[0].shape
    total = len(parts) * mine
    return pl.pallas_call(
        kernel,
        out_shape=jax.ShapeDtypeStruct((rows, total), BF16),
        in_specs=[pl.BlockSpec(memory_space=pltpu.VMEM)] * (2 + len(parts)),
        out_specs=pl.BlockSpec(memory_space=pltpu.VMEM),
        compiler_params=pltpu.CompilerParams(vmem_limit_bytes=32 << 20),
        cost_estimate=pl.CostEstimate(
            flops=8 * rows * total, bytes_accessed=6 * rows * total, transcendentals=0
        ),
        name="unrotated",
    )(cosine, sine, *parts)


BOTH = ("dp", "ctx")


class Grid:
    def __init__(self, n_dp, n_ctx):
        self.n_dp, self.n_a, self.n_b = n_dp, 2, n_ctx // 4
        self.n_ctx = n_ctx
        self.ring = [0, 1, 3, 2] if n_dp == 4 else list(range(n_dp))
        own = lax.axis_index("ctx").astype(jnp.int32)
        self.a = own // (2 * self.n_b)
        self.b = (own // 2) % self.n_b
        self.c = own % 2
        places = np.argsort(np.array(self.ring)).astype(np.int32)
        self.d = jnp.asarray(places)[lax.axis_index("dp")]

    def size(self, axis):
        return {"a": self.n_a, "b": self.n_b, "c": 2, "d": self.n_dp}[axis]

    def next(self, values, axis):
        if axis == "d":
            around = self.ring[1:] + self.ring[:1]
            return lax.ppermute(values, "dp", list(zip(self.ring, around)))
        pairs = []
        for i in range(self.n_ctx):
            a, b, c = i // (2 * self.n_b), (i // 2) % self.n_b, i % 2
            if axis == "a":
                a = (a + 1) % self.n_a
            elif axis == "b":
                b = (b + 1) % self.n_b
            else:
                c = 1 - c
            pairs.append((i, (a * self.n_b + b) * 2 + c))
        return lax.ppermute(values, "ctx", pairs)

    def natural(self, rows):
        rows = np.array(rows, np.int32)
        a = (self.a - rows[:, 2]) % self.n_a
        b = (self.b - rows[:, 3]) % self.n_b
        c = (self.c - rows[:, 0]) % 2
        return ((rows[:, 1] * self.n_a + a) * self.n_b + b) * 2 + c

    def block_order(self):
        half = self.n_dp // 2
        rows = []
        for core in range(2):
            for h, (first, second) in enumerate(HALVES):
                for i in range(self.size(first)):
                    for j in range(self.size(second)):
                        for d in range(half):
                            near = {first: i, second: j}
                            rows.append((core, h * half + d, near["a"], near["b"]))
        return self.natural(rows)

    def ring_order(self):
        rows, hops = [], []
        for core in range(2):
            for d in range(self.n_dp):
                for b in range(self.n_b):
                    for a in range(self.n_a):
                        rows.append((core, 0, a, b))
                        hops.append(d)
        place = jnp.asarray(np.array(self.ring, np.int32))[
            (self.d - np.array(hops, np.int32)) % self.n_dp
        ]
        return self.natural(rows) + place * self.n_ctx

    def ctx_order(self):
        rows = [
            (c, 0, a, b) for c in range(2) for b in range(self.n_b) for a in range(self.n_a)
        ]
        return self.natural(rows)

    def value_places(self):
        cells = [(c, b, a) for c in range(2) for b in range(self.n_b) for a in range(self.n_a)]
        return tuple((c * self.n_a + a) * self.n_b + b for c, b, a in cells)


HALVES = (("b", "a"), ("a", "b"))


def turn_kernel(order_ref, x_ref, o_ref, held, *, blk):
    tokens, width = x_ref.shape
    for i in range(width // WIDE):
        held[i * WIDE : (i + 1) * WIDE, :] = x_ref[:, i * WIDE : (i + 1) * WIDE].T

    def move(i, _):
        source = pl.multiple_of(order_ref[i] * blk, blk)
        target = pl.multiple_of(i * blk, blk)
        o_ref[pl.ds(target, blk), :] = held[pl.ds(source, blk), :]
        return 0

    lax.fori_loop(0, width // blk, move, 0)


def turned(x, order):
    tokens, width = x.shape
    blk = width // order.shape[0]
    if blk % 16:
        blocks = jnp.take(x.T.reshape(order.shape[0], blk, tokens), order, axis=0)
        return blocks.reshape(width, tokens)
    return pl.pallas_call(
        functools.partial(turn_kernel, blk=blk),
        out_shape=jax.ShapeDtypeStruct((width, tokens), x.dtype),
        in_specs=[
            pl.BlockSpec(memory_space=pltpu.SMEM),
            pl.BlockSpec(memory_space=pltpu.VMEM),
        ],
        out_specs=pl.BlockSpec(memory_space=pltpu.VMEM),
        scratch_shapes=[pltpu.VMEM((width, tokens), x.dtype)],
        compiler_params=pltpu.CompilerParams(vmem_limit_bytes=32 << 20),
        cost_estimate=pl.CostEstimate(flops=0, bytes_accessed=4 * x.size, transcendentals=0),
        name="turned",
    )(order, x)


def reduce_term(grid, left, right, extra=None):
    rows = left.shape[0]
    mine = rows // 2

    def term(start, size):
        part = mm(left[start : start + size], right, NN)
        if extra is not None:
            part = jnp.concatenate([part, extra[start : start + size].astype(F32)], 1)
        return part

    (arrived,) = yield [grid.next(term(mine, mine).astype(BF16), "c")]
    held = []
    for h, axes in enumerate(HALVES):
        start = h * (mine // 2)
        count = grid.size(axes[0])
        size = mine // 2 // count
        held.append(
            [
                (term(at, size) + arrived[at : at + size].astype(F32)).astype(BF16)
                for at in range(start, start + count * size, size)
            ]
        )
    for step in range(2):
        totals = [None, None]
        counts = [grid.size(axes[step]) for axes in HALVES]
        for k in range(1, max(counts)):
            live = [h for h in range(2) if k < counts[h]]
            sent = [
                grid.next(held[h][1] if k == 1 else totals[h], HALVES[h][step]) for h in live
            ]
            came = yield sent
            for h, part in zip(live, came):
                own = held[h][(k + 1) % counts[h]]
                totals[h] = (part.astype(F32) + own.astype(F32)).astype(BF16)
        if step == 0:
            held = []
            for h, total in enumerate(totals):
                count = grid.size(HALVES[h][1])
                size = total.shape[0] // count
                held.append([total[j * size : (j + 1) * size] for j in range(count)])
    joined = jnp.concatenate(totals, 0)
    (share,) = yield [lax.psum_scatter(joined, "dp", scatter_dimension=0, tiled=True)]
    return share.astype(F32)


def place_kernel(order_ref, *refs, sources, slots):
    pieces = refs[: -(3 + 1)]
    out_ref, held, in_sem, out_sem = refs[-4:]
    count = len(sources)

    def fetch(i):
        piece, place = sources[i]
        return pltpu.make_async_copy(
            pieces[piece].at[place], held.at[i % slots], in_sem.at[i % slots]
        )

    def store(i):
        return pltpu.make_async_copy(
            held.at[i % slots], out_ref.at[order_ref[i]], out_sem.at[i % slots]
        )

    ahead = slots // 2
    for i in range(min(ahead, count)):
        fetch(i).start()
    for i in range(count):
        fetch(i).wait()
        store(i).start()
        later = i + ahead
        if later < count:
            if later >= slots:
                store(later - slots).wait()
            fetch(later).start()
    for i in range(max(0, count - slots), count):
        store(i).wait()


def placed(order, pieces):
    blk, width = pieces[0].shape[-2:]
    flat = [p.reshape((-1, blk, width)) for p in pieces]
    sources = [(n, j) for n, p in enumerate(flat) for j in range(p.shape[0])]
    slots = 8
    whole = pl.pallas_call(
        functools.partial(place_kernel, sources=sources, slots=slots),
        out_shape=jax.ShapeDtypeStruct((len(sources), blk, width), flat[0].dtype),
        in_specs=[pl.BlockSpec(memory_space=pltpu.SMEM)]
        + [pl.BlockSpec(memory_space=pl.ANY)] * len(flat),
        out_specs=pl.BlockSpec(memory_space=pl.ANY),
        scratch_shapes=[
            pltpu.VMEM((slots, blk, width), flat[0].dtype),
            pltpu.SemaphoreType.DMA((slots,)),
            pltpu.SemaphoreType.DMA((slots,)),
        ],
        compiler_params=pltpu.CompilerParams(vmem_limit_bytes=16 << 20),
        cost_estimate=pl.CostEstimate(
            flops=0, bytes_accessed=4 * len(sources) * blk * width, transcendentals=0
        ),
        name="placed",
    )(order, *flat)
    return whole.reshape(len(sources) * blk, width)


def gather_weight(grid, weight, order):
    (column,) = yield [lax.all_gather(weight, "dp", axis=0)]
    half = grid.n_dp // 2
    parts = [column[:half], column[half:]]
    steps = [[parts[0]], [parts[1]]]
    for stage in (1, 0):
        counts = [grid.size(axes[stage]) for axes in HALVES]
        for k in range(1, max(counts)):
            live = [h for h in range(2) if k < counts[h]]
            came = yield [grid.next(steps[h][-1], HALVES[h][stage]) for h in live]
            for h, part in zip(live, came):
                steps[h].append(part)
        if stage == 1:
            steps = [[jnp.stack(s)] for s in steps]
    near = steps[0] + steps[1]
    far = yield [grid.next(piece, "c") for piece in near]
    return placed(order, near + list(far))


def gather_ring(grid, weight):
    part = weight
    for axis in ("a", "b"):
        steps = [part]
        for _ in range(grid.size(axis) - 1):
            (came,) = yield [grid.next(steps[-1], axis)]
            steps.append(came)
        part = jnp.stack(steps)
    near, far = [part], []
    for _ in range(grid.n_dp - 1):
        came, other = yield [grid.next(near[-1], "d"), grid.next(near[-1], "c")]
        near.append(came)
        far.append(other)
    (other,) = yield [grid.next(near[-1], "c")]
    return placed(grid.ring_order(), near + far + [other])


def reduce_ring(grid, left, right):
    mine = left.shape[0] // 2
    (arrived,) = yield [grid.next(mm(left[mine:], right, NN).astype(BF16), "c")]
    size = mine // grid.n_dp
    held = [
        (mm(left[at : at + size], right, NN) + arrived[at : at + size].astype(F32)).astype(BF16)
        for at in range(0, mine, size)
    ]
    for axis in ("d", "b", "a"):
        count = grid.size(axis)
        total = held[1]
        for k in range(1, count):
            (came,) = yield [grid.next(total, axis)]
            total = (came.astype(F32) + held[(k + 1) % count].astype(F32)).astype(BF16)
        following = {"d": grid.n_b, "b": grid.n_a, "a": 1}[axis]
        size = total.shape[0] // following
        held = [total[at : at + size] for at in range(0, total.shape[0], size)]
    return held[0].astype(F32)


def gather_keys(grid, own):
    width = own.shape[1] // 2
    steps = [[own[:, :width]], [own[:, width:]]]
    for stage in (1, 0):
        counts = [grid.size(axes[stage]) for axes in HALVES]
        for k in range(1, max(counts)):
            live = [h for h in range(2) if k < counts[h]]
            came = yield [grid.next(steps[h][-1], HALVES[h][stage]) for h in live]
            for h, part in zip(live, came):
                steps[h].append(part)
        steps = [[jnp.stack(s)] for s in steps]
    near = [s[0] for s in steps]
    far = yield [grid.next(part, "c") for part in near]
    return tuple(
        jnp.stack([one, two]).reshape(-1, width) for one, two in zip(near, far)
    )


class Chain:
    def __init__(self, generator):
        self.generator, self.done, self.result = generator, False, None
        self.flight = next(generator)

    def advance(self, arrived):
        try:
            self.flight = self.generator.send(arrived)
        except StopIteration as stop:
            self.done, self.result, self.flight = True, stop.value, []


def meet(main, *chains):
    chains = [c for c in chains if not c.done]
    main, flights = lax.optimization_barrier((main, [list(c.flight) for c in chains]))
    for chain, flight in zip(chains, flights):
        chain.advance(flight)
    return main


def finish(chain):
    while not chain.done:
        chain.advance(chain.flight)
    return chain.result


def angles(positions):
    lane = jnp.arange(WIDE)
    freq = 10000.0 ** (-((lane % (HD // 2)).astype(F32) * 2.0 / HD))
    turn = positions.astype(F32)[:, None] * freq[None, :]
    sign = jnp.where(lane % HD < HD // 2, -1.0, 1.0)
    return jnp.cos(turn), jnp.sin(turn) * sign[None, :]


def normalize(rows):
    factor = lax.rsqrt(jnp.mean(rows * rows, -1, keepdims=True) + EPS)
    return (rows * factor, factor)


def norm_back(upstream, normed, factor, gain):
    scaled = upstream * gain
    inner = jnp.mean(scaled * normed, -1, keepdims=True)
    return (factor * (scaled - normed * inner), jnp.sum(upstream * normed, 0))


def body(
    n_dp,
    n_ctx,
    layer_in,
    positions,
    attn_gain,
    query_proj,
    key_proj,
    value_proj,
    merge_proj,
    ffn_gain,
    gate_proj,
    up_proj,
    down_proj,
    out_grad,
):
    _, rows, model = layer_in.shape
    kv_width = key_proj.shape[1]
    kv_heads = kv_width // HD
    width = query_proj.shape[1]
    run = rows // 2
    positions = positions[0]
    grid = Grid(n_dp, n_ctx)
    order, ring_order, ctx_order = grid.block_order(), grid.ring_order(), grid.ctx_order()
    places = grid.value_places()

    gains = jnp.stack([attn_gain, ffn_gain], -1)
    gains = jnp.concatenate([gains, jnp.zeros((gains.shape[0], WIDE - 2), BF16)], 1)
    packed = jnp.concatenate([query_proj, key_proj, value_proj, gains], 1)
    first_chain = Chain(gather_weight(grid, packed, order))
    down_chain = Chain(gather_ring(grid, down_proj))
    all_pos = lax.all_gather(positions[::run], "ctx", axis=0, tiled=True)
    cosine, sine = angles(positions)
    rows_in = layer_in.reshape(rows, model).astype(F32)
    normed_one, factor_one = normalize(rows_in)
    all_pos, merge_proj, factor_one = meet((all_pos, merge_proj, factor_one), first_chain, down_chain)
    merge_chain = Chain(gather_weight(grid, merge_proj, order))
    gate_proj = meet(gate_proj, first_chain)
    gate_chain = Chain(gather_weight(grid, gate_proj, order))
    first_weights = finish(first_chain)
    attn_all = first_weights[:, : width + 2 * kv_width]
    gain_one = first_weights[:, width + 2 * kv_width].astype(F32)
    gain_two = first_weights[:, width + 2 * kv_width + 1].astype(F32)

    first_in = (normed_one * gain_one).astype(BF16)
    raw = mm(first_in, attn_all, NN)
    raw, up_proj = meet((raw, up_proj), merge_chain)
    up_chain = Chain(gather_weight(grid, up_proj, order))
    queries, own_kv = rotated(raw, cosine, sine, kv_width)
    kv_chain = Chain(gather_keys(grid, own_kv))
    later = all_pos.reshape(n_ctx, 2)[ctx_order].reshape(2 * n_ctx, 1)
    later = later > jnp.repeat(positions[::run], run)[None, :]
    bias = jnp.where(later, MASKED, 0.0).astype(F32)
    bias = meet(bias, kv_chain, gate_chain, merge_chain)
    bias = meet(bias, kv_chain)
    all_keys, all_values = finish(kv_chain)
    kt, vt = all_keys.T, all_values.T

    plan = (
        (gate_chain, merge_chain, up_chain, down_chain),
        (merge_chain,),
        (),
        (gate_chain, up_chain, down_chain),
    )
    outs, log_sums = [], []
    for group in range(kv_heads):
        out, log_sum = attend(group, places, bias, queries, all_keys, vt)
        queries, out = meet((queries, out), *plan[group % 4])
        outs.append(out)
        log_sums.append(log_sum)
    mixed = jnp.concatenate([out.astype(BF16) for out in outs], 1)
    merge_all = finish(merge_chain)
    middle = rows_in + mm(mixed, merge_all, NN)
    normed_two, factor_two = normalize(middle)
    second_in = (normed_two * gain_two).astype(BF16)
    second_in = meet(second_in, gate_chain)
    gate_all = finish(gate_chain)
    gate = mm(second_in, gate_all, NN)
    gate = meet(gate, up_chain, down_chain)
    up_all = finish(up_chain)
    lift = mm(second_in, up_all, NN)
    sigma = jax.nn.sigmoid(gate)
    activated = gate * sigma
    hidden = (activated * lift).astype(BF16)
    grad_rows = out_grad.reshape(rows, model)
    down_sum = Chain(reduce_ring(grid, turned(hidden, ring_order), grad_rows))
    hidden = meet(hidden, down_chain)
    down_all = finish(down_chain)
    result = middle + mm(hidden, down_all, NN)
    layer_out = result.astype(BF16).reshape(layer_in.shape)
    layer_out = meet(layer_out, down_sum)
    grad_hidden = mm(grad_rows, down_all, NT)
    grad_gate = (grad_hidden * lift * sigma * (1.0 + gate * (1.0 - sigma))).astype(BF16)
    grad_lift = (grad_hidden * activated).astype(BF16)
    second_turned = turned(second_in, order)
    gate_sum = Chain(reduce_term(grid, second_turned, grad_gate))
    up_sum = Chain(reduce_term(grid, second_turned, grad_lift))
    grad_second = mm(grad_gate, gate_all, NT) + mm(grad_lift, up_all, NT)
    grad_second = meet(grad_second, gate_sum, up_sum, down_sum)
    grad_norm_two, gain_two_term = norm_back(grad_second, normed_two, factor_two, gain_two)
    grad_middle = grad_rows.astype(F32) + grad_norm_two
    grad_branch = grad_middle.astype(BF16)
    merge_sum = Chain(reduce_term(grid, turned(mixed, order), grad_branch))
    grad_mixed = mm(grad_branch, merge_all, NT).astype(BF16)
    grad_mixed = meet(grad_mixed, merge_sum)
    first_turned = turned(first_in, order)
    plan = (
        (down_sum, gate_sum),
        (up_sum, merge_sum),
        (down_sum, gate_sum),
        (merge_sum, up_sum, down_sum),
    )
    dqs, shares, dkv_parts, early = [], [], [], None
    for group in range(kv_heads):
        dq, dkv = attend_back(
            group, ctx_order, places, bias, log_sums[group], outs[group], queries, grad_mixed,
            all_keys, all_values, kt,
        )
        flying = dkv_parts[-1:]
        (dq, grad_mixed, dkv, flying) = meet((dq, grad_mixed, dkv, flying), *plan[group % 4])
        dkv_parts[-1:] = flying
        dqs.append(dq)
        dkv_parts.append(lax.psum_scatter(dkv, "ctx", scatter_dimension=0, tiled=True))
        if group == kv_heads - 2:
            early_grads = unrotated(unrotate_queries_kernel, dqs, cosine, sine)
            early = Chain(reduce_term(grid, first_turned, early_grads))
            grad_mixed = meet(grad_mixed, early)
    split = early_grads.shape[1]
    late_grads = unrotated(unrotate_queries_kernel, dqs[-1:], cosine, sine)
    late = Chain(reduce_term(grid, first_turned, late_grads))
    grad_first = mm(early_grads, attn_all[:, :split], NT)
    grad_first = grad_first + mm(late_grads, attn_all[:, split:width], NT)
    grad_first, dkv_parts = meet((grad_first, dkv_parts), early, late, gate_sum, down_sum)
    kv_grads = unrotated(unrotate_keys_kernel, dkv_parts, cosine, sine)
    grad_first = grad_first + mm(kv_grads, attn_all[:, width:], NT)
    grad_norm_one, gain_one_term = norm_back(grad_first, normed_one, factor_one, gain_one)
    gain_terms = jnp.stack([gain_one_term, gain_two_term], 0)
    gain_terms = jnp.concatenate([gain_terms, jnp.zeros((WIDE - 2, model), F32)], 0)
    last = Chain(
        reduce_term(grid, first_turned, kv_grads, turned(gain_terms.astype(BF16), order))
    )
    input_grad = (grad_middle + grad_norm_one).astype(BF16).reshape(layer_in.shape)
    input_grad = meet(input_grad, last, early, late, merge_sum, up_sum)
    while not last.done:
        input_grad = meet(input_grad, last, early, late)
    early_share, late_share, last_share = finish(early), finish(late), finish(last)
    merge_share, gate_share = finish(merge_sum), finish(gate_sum)
    up_share, down_share = finish(up_sum), finish(down_sum)
    return (
        layer_out,
        input_grad,
        last_share[:, 2 * kv_width],
        jnp.concatenate([early_share, late_share], 1),
        last_share[:, :kv_width],
        last_share[:, kv_width : 2 * kv_width],
        merge_share,
        last_share[:, 2 * kv_width + 1],
        gate_share,
        up_share,
        down_share,
    )


def solution(mesh):
    acts = P("dp", "ctx", None)
    rows = P(BOTH, None)
    flat = P(BOTH)
    return jax.shard_map(
        functools.partial(body, mesh.shape["dp"], mesh.shape["ctx"]),
        mesh=mesh,
        in_specs=(acts, P("dp", "ctx"), flat, rows, rows, rows, rows, flat, rows, rows, rows, acts),
        out_specs=(acts, acts, flat, rows, rows, rows, rows, flat, rows, rows, rows),
        check_vma=False,
    )
```

```python
import functools

import jax
import jax.numpy as jnp
import numpy as np
from jax import lax
from jax.experimental import pallas as pl
from jax.experimental.pallas import tpu as pltpu
from jax.sharding import PartitionSpec as P

HD = 64
EPS = 1e-05
WIDE = 128
MASKED = -1e30
SCALE = HD**-0.5
LOG2E = 1.4426950408889634
TO_LOG2 = SCALE * LOG2E
BRIEF = pl.CostEstimate(flops=1 << 20, bytes_accessed=1 << 16, transcendentals=0)
F32 = jnp.float32
BF16 = jnp.bfloat16
NT = (((1,), (1,)), ((), ()))
NN = (((1,), (0,)), ((), ()))


def mm(left, right, dims):
    return lax.dot_general(left, right, dims, preferred_element_type=F32)


def same_run_later(keys, rows):
    run = rows // 2
    key = lax.broadcasted_iota(jnp.int32, (keys, rows), 0)
    query = lax.broadcasted_iota(jnp.int32, (keys, rows), 1)
    return (key > query) & ((key // run) == (query // run))


def split_heads(pair_ref, which, low_ref, high_ref):
    both = pair_ref[...]
    turned = pltpu.roll(both.astype(F32), HD, 1).astype(BF16)
    lane = lax.broadcasted_iota(jnp.int32, both.shape, 1)
    zero = jnp.zeros_like(both)
    first, second = (both, turned) if which == 0 else (turned, both)
    low_ref[...] = jnp.where(lane < HD, first, zero)
    high_ref[...] = jnp.where(lane < HD, zero, second)


def biased(scores, bias_ref, block, rows):
    run = rows // 2
    start = pl.multiple_of(block * rows, rows)
    parts = [
        scores[i * run : (i + 1) * run] + bias_ref[pl.ds(block * 2 + i, 1), :]
        for i in range(2)
    ]
    return jnp.concatenate(parts, 0)


def attend_kernel(
    bias_ref, q_ref, kp_ref, vt_ref, o_ref, lse_ref, low, high, vx, turned, *, which, places
):
    rows, width = q_ref.shape
    length = kp_ref.shape[0]
    blocks = length // rows
    split_heads(kp_ref, which, low, high)
    vx[:HD, :] = vt_ref[...]
    top_row = lax.broadcasted_iota(jnp.int32, (16, length), 0) == 0
    vx[HD:, :] = top_row.astype(F32).astype(BF16)

    def scores(key, pair, block):
        start = pl.multiple_of(block * rows, rows)
        column = pl.multiple_of(pair * WIDE, WIDE)
        s = mm(key[pl.ds(start, rows), :], q_ref[:, pl.ds(column, WIDE)], NT) * TO_LOG2
        return biased(s, bias_ref, block, rows)

    def weigh(probs, block):
        start = places[block] * rows
        return mm(vx[:, start : start + rows], probs.astype(BF16), NN)

    def one_pair(pair, _):
        blocked = same_run_later(rows, rows)
        state = []
        for key in (low, high):
            s = jnp.where(blocked, MASKED, scores(key, pair, 0))
            top = jnp.max(s, 0, keepdims=True)
            state.append((top, weigh(jnp.exp2(s - top), 0)))

        def step(block, state):
            raw = [scores(key, pair, block) for key in (low, high)]
            result = []
            for (top, total), s in zip(state, raw):
                new_top = jnp.maximum(top, jnp.max(s, 0, keepdims=True))
                probs = jnp.exp2(s - new_top)
                result.append((new_top, total * jnp.exp2(top - new_top) + weigh(probs, block)))
            return result

        for block in range(1, blocks):
            state = step(block, state)
        for i, (top, total) in enumerate(state):
            weight_sum = total[HD : HD + 1, :]
            turned[i * HD : (i + 1) * HD, :] = total[:HD] / weight_sum
            lse_ref[pl.ds(pair * 2 + i, 1), :] = top + jnp.log2(weight_sum)
        column = pl.multiple_of(pair * WIDE, WIDE)
        o_ref[:, pl.ds(column, WIDE)] = turned[...].T
        return 0

    lax.fori_loop(0, width // WIDE, one_pair, 0)


def attend(group, places, bias, q, keys, vt):
    rows, width = q.shape
    length = keys.shape[0]
    kv_heads = vt.shape[0] // HD
    mine = width // kv_heads
    heads = mine // HD
    return pl.pallas_call(
        functools.partial(attend_kernel, which=group % 2, places=places),
        grid=(1,),
        out_shape=(
            jax.ShapeDtypeStruct((rows, mine), F32),
            jax.ShapeDtypeStruct((heads, rows), F32),
        ),
        in_specs=[
            pl.BlockSpec(bias.shape, lambda i: (0, 0)),
            pl.BlockSpec((rows, mine), lambda i: (0, group)),
            pl.BlockSpec((length, WIDE), lambda i: (0, group // 2)),
            pl.BlockSpec((HD, length), lambda i: (group, 0)),
        ],
        out_specs=(
            pl.BlockSpec((rows, mine), lambda i: (0, 0)),
            pl.BlockSpec((heads, rows), lambda i: (0, 0)),
        ),
        scratch_shapes=[
            pltpu.VMEM((length, WIDE), BF16),
            pltpu.VMEM((length, WIDE), BF16),
            pltpu.VMEM((HD + 16, length), BF16),
            pltpu.VMEM((WIDE, rows), F32),
        ],
        compiler_params=pltpu.CompilerParams(vmem_limit_bytes=40 << 20),
        cost_estimate=BRIEF,
        name="attend",
    )(bias, q, keys, vt)


def attend_back_kernel(
    place_ref, bias_ref, lse_ref, o_ref, q_ref, g_ref, kp_ref, vp_ref, kt_ref,
    dq_ref, dkv_ref, k_low, k_high, v_low, v_high, dqt, delta_ref, *, which, unroll
):
    rows, width = q_ref.shape
    length = kp_ref.shape[0]
    blocks = length // rows
    pairs = width // WIDE
    split_heads(kp_ref, which, k_low, k_high)
    split_heads(vp_ref, which, v_low, v_high)
    row = lax.broadcasted_iota(jnp.int32, (16, WIDE), 0)
    lane = lax.broadcasted_iota(jnp.int32, (16, WIDE), 1)
    chosen = (row == lane // HD).astype(F32).astype(BF16)
    for pair in range(pairs):
        column = pl.ds(pair * WIDE, WIDE)
        product = g_ref[:, column].astype(F32) * o_ref[:, column]
        main = product.astype(BF16)
        rest = (product - main.astype(F32)).astype(BF16)
        both = mm(chosen, main, NT) + mm(chosen, rest, NT)
        delta_ref[2 * pair : 2 * pair + 2, :] = both[:2]

    def block(index, diagonal):
        start = pl.multiple_of(index * rows, rows)
        value_start = pl.multiple_of(place_ref[index] * rows, rows)

        def some_heads(i, sums):
            sums = list(sums)
            work = []
            for t in range(unroll):
                pair = i * unroll + t
                column = pl.multiple_of(pair * WIDE, WIDE)
                query = q_ref[:, pl.ds(column, WIDE)]
                grad = g_ref[:, pl.ds(column, WIDE)]
                for side, (key, value) in enumerate(((k_low, v_low), (k_high, v_high))):
                    head = pair * 2 + side
                    shift = -lse_ref[pl.ds(head, 1), :]
                    run = rows // 2
                    s = mm(key[pl.ds(start, rows), :], query, NT) * TO_LOG2
                    s = jnp.concatenate(
                        [
                            s[r * run : (r + 1) * run]
                            + (bias_ref[pl.ds(index * 2 + r, 1), :] + shift)
                            for r in range(2)
                        ],
                        0,
                    )
                    p = jnp.exp2(s)
                    if diagonal:
                        p = jnp.where(same_run_later(rows, rows), 0.0, p)
                    slope = mm(value[pl.ds(value_start, rows), :], grad, NT)
                    d = (p * (slope - delta_ref[pl.ds(head, 1), :])).astype(BF16)
                    work.append((side, pair, query, grad, p.astype(BF16), d))
            for side, pair, query, grad, p, d in work:
                sums[side] = sums[side] + mm(d, query, NN)
                sums[2 + side] = sums[2 + side] + mm(p, grad, NN)
                term = mm(kt_ref[:, pl.ds(start, rows)], d, NN)
                row = pl.multiple_of(pair * WIDE + side * HD, HD)
                if diagonal:
                    dqt[pl.ds(row, HD), :] = term
                else:
                    dqt[pl.ds(row, HD), :] += term
            return tuple(sums)

        zero = jnp.zeros((rows, WIDE), F32)
        sums = lax.fori_loop(0, pairs // unroll, some_heads, (zero,) * 4)
        lane = lax.broadcasted_iota(jnp.int32, (rows, WIDE), 1)
        key_sum = sums[0] + pltpu.roll(sums[1], HD, 1)
        value_sum = pltpu.roll(sums[2], HD, 1) + sums[3]
        dkv_ref[pl.ds(start, rows), :] = jnp.where(
            lane < HD, key_sum * SCALE, value_sum
        ).astype(BF16)

    block(0, True)

    def rest(j, _):
        block(j, False)
        return 0

    lax.fori_loop(1, blocks, rest, 0)
    for pair in range(pairs):
        dq_ref[:, pair * WIDE : (pair + 1) * WIDE] = (
            dqt[pair * WIDE : (pair + 1) * WIDE, :] * SCALE
        ).T


def attend_back(group, places, bias, lse, out, q, g, keys, values, kt, unroll=2):
    rows, width = q.shape
    length = keys.shape[0]
    kv_heads = kt.shape[0] // HD
    mine = width // kv_heads
    heads = mine // HD
    return pl.pallas_call(
        functools.partial(attend_back_kernel, which=group % 2, unroll=unroll),
        grid=(1,),
        out_shape=(
            jax.ShapeDtypeStruct((rows, mine), F32),
            jax.ShapeDtypeStruct((length, WIDE), BF16),
        ),
        in_specs=[
            pl.BlockSpec(memory_space=pltpu.SMEM),
            pl.BlockSpec(bias.shape, lambda i: (0, 0)),
            pl.BlockSpec((heads, rows), lambda i: (0, 0)),
            pl.BlockSpec((rows, mine), lambda i: (0, 0)),
            pl.BlockSpec((rows, mine), lambda i: (0, group)),
            pl.BlockSpec((rows, mine), lambda i: (0, group)),
            pl.BlockSpec((length, WIDE), lambda i: (0, group // 2)),
            pl.BlockSpec((length, WIDE), lambda i: (0, group // 2)),
            pl.BlockSpec((HD, length), lambda i: (group, 0)),
        ],
        out_specs=(
            pl.BlockSpec((rows, mine), lambda i: (0, 0)),
            pl.BlockSpec((length, WIDE), lambda i: (0, 0)),
        ),
        scratch_shapes=[pltpu.VMEM((length, WIDE), BF16)] * 4
        + [pltpu.VMEM((mine, rows), F32), pltpu.VMEM((heads, rows), F32)],
        compiler_params=pltpu.CompilerParams(vmem_limit_bytes=48 << 20),
        cost_estimate=BRIEF,
        name="attend_back",
    )(jnp.array(places, jnp.int32), bias, lse, out, q, g, keys, values, kt)


def turn_pairs(x, cosine, sine):
    lane = lax.broadcasted_iota(jnp.int32, x.shape, 1)
    swapped = jnp.where(
        lane % HD < HD // 2, pltpu.roll(x, WIDE - HD // 2, 1), pltpu.roll(x, HD // 2, 1)
    )
    return x * cosine + swapped * sine


def rotate_kernel(cos_ref, sin_ref, raw_ref, q_ref, kv_ref, *, kv_width):
    cosine, sine = cos_ref[...], sin_ref[...]
    width = q_ref.shape[1]
    for at in range(0, width, WIDE):
        q_ref[:, at : at + WIDE] = turn_pairs(raw_ref[:, at : at + WIDE], cosine, sine).astype(BF16)
    for at in range(0, kv_width, WIDE):
        column = slice(width + at, width + at + WIDE)
        kv_ref[:, at : at + WIDE] = turn_pairs(raw_ref[:, column], cosine, sine).astype(BF16)
    kv_ref[:, kv_width:] = raw_ref[:, width + kv_width :].astype(BF16)


def rotated(raw, cosine, sine, kv_width):
    rows, total = raw.shape
    return pl.pallas_call(
        functools.partial(rotate_kernel, kv_width=kv_width),
        out_shape=(
            jax.ShapeDtypeStruct((rows, total - 2 * kv_width), BF16),
            jax.ShapeDtypeStruct((rows, 2 * kv_width), BF16),
        ),
        in_specs=[pl.BlockSpec(memory_space=pltpu.VMEM)] * 3,
        out_specs=(pl.BlockSpec(memory_space=pltpu.VMEM),) * 2,
        compiler_params=pltpu.CompilerParams(vmem_limit_bytes=32 << 20),
        cost_estimate=pl.CostEstimate(
            flops=8 * raw.size, bytes_accessed=6 * raw.size, transcendentals=0
        ),
        name="rotated",
    )(cosine, sine, raw)


def unrotate_queries_kernel(cos_ref, sin_ref, *refs):
    cosine, sine = cos_ref[...], -sin_ref[...]
    out_ref = refs[-1]
    mine = refs[0].shape[1]
    for n, ref in enumerate(refs[:-1]):
        for at in range(0, mine, WIDE):
            turned = turn_pairs(ref[:, at : at + WIDE], cosine, sine)
            out_ref[:, n * mine + at : n * mine + at + WIDE] = turned.astype(BF16)


def unrotate_keys_kernel(cos_ref, sin_ref, *refs):
    cosine, sine = cos_ref[...], -sin_ref[...]
    out_ref = refs[-1]
    count = len(refs) - 1
    lane = lax.broadcasted_iota(jnp.int32, cosine.shape, 1)
    for i in range(count // 2):
        first, second = refs[2 * i][...].astype(F32), refs[2 * i + 1][...].astype(F32)
        keys = jnp.where(lane < HD, first, pltpu.roll(second, HD, 1))
        values = jnp.where(lane < HD, pltpu.roll(first, HD, 1), second)
        at = i * WIDE
        out_ref[:, at : at + WIDE] = turn_pairs(keys, cosine, sine).astype(BF16)
        at = count * HD + i * WIDE
        out_ref[:, at : at + WIDE] = values.astype(BF16)


def unrotated(kernel, parts, cosine, sine):
    rows, mine = parts[0].shape
    total = len(parts) * mine
    return pl.pallas_call(
        kernel,
        out_shape=jax.ShapeDtypeStruct((rows, total), BF16),
        in_specs=[pl.BlockSpec(memory_space=pltpu.VMEM)] * (2 + len(parts)),
        out_specs=pl.BlockSpec(memory_space=pltpu.VMEM),
        compiler_params=pltpu.CompilerParams(vmem_limit_bytes=32 << 20),
        cost_estimate=pl.CostEstimate(
            flops=8 * rows * total, bytes_accessed=6 * rows * total, transcendentals=0
        ),
        name="unrotated",
    )(cosine, sine, *parts)


BOTH = ("dp", "ctx")


class Grid:
    def __init__(self, n_dp, n_ctx):
        self.n_dp, self.n_a, self.n_b = n_dp, 2, n_ctx // 4
        self.n_ctx = n_ctx
        self.ring = [0, 1, 3, 2] if n_dp == 4 else list(range(n_dp))
        own = lax.axis_index("ctx").astype(jnp.int32)
        self.a = own // (2 * self.n_b)
        self.b = (own // 2) % self.n_b
        self.c = own % 2
        places = np.argsort(np.array(self.ring)).astype(np.int32)
        self.d = jnp.asarray(places)[lax.axis_index("dp")]

    def size(self, axis):
        return {"a": self.n_a, "b": self.n_b, "c": 2, "d": self.n_dp}[axis]

    def next(self, values, axis):
        if axis == "d":
            around = self.ring[1:] + self.ring[:1]
            return lax.ppermute(values, "dp", list(zip(self.ring, around)))
        pairs = []
        for i in range(self.n_ctx):
            a, b, c = i // (2 * self.n_b), (i // 2) % self.n_b, i % 2
            if axis == "a":
                a = (a + 1) % self.n_a
            elif axis == "b":
                b = (b + 1) % self.n_b
            else:
                c = 1 - c
            pairs.append((i, (a * self.n_b + b) * 2 + c))
        return lax.ppermute(values, "ctx", pairs)

    def natural(self, rows):
        rows = np.array(rows, np.int32)
        a = (self.a - rows[:, 2]) % self.n_a
        b = (self.b - rows[:, 3]) % self.n_b
        c = (self.c - rows[:, 0]) % 2
        return ((rows[:, 1] * self.n_a + a) * self.n_b + b) * 2 + c

    def block_order(self, around):
        half = self.n_dp // 2
        rows, hops = [], []
        for core in range(2):
            for h, (first, second) in enumerate(HALVES):
                for i in range(self.size(first)):
                    for j in range(self.size(second)):
                        for d in range(half):
                            near = {first: i, second: j}
                            at = h * half + d
                            rows.append((core, 0 if around else at, near["a"], near["b"]))
                            hops.append(at)
        return self.natural(rows) + (self.around(hops) * self.n_ctx if around else 0)

    def around(self, hops):
        ring = jnp.asarray(np.array(self.ring, np.int32))
        return ring[(self.d - np.array(hops, np.int32)) % self.n_dp]

    def ring_order(self):
        rows, hops = [], []
        for core in range(2):
            for d in range(self.n_dp):
                for b in range(self.n_b):
                    for a in range(self.n_a):
                        rows.append((core, 0, a, b))
                        hops.append(d)
        return self.natural(rows) + self.around(hops) * self.n_ctx

    def ctx_order(self):
        rows = [
            (c, 0, a, b) for c in range(2) for b in range(self.n_b) for a in range(self.n_a)
        ]
        return self.natural(rows)

    def value_places(self):
        cells = [(c, b, a) for c in range(2) for b in range(self.n_b) for a in range(self.n_a)]
        return tuple((c * self.n_a + a) * self.n_b + b for c, b, a in cells)


HALVES = (("b", "a"), ("a", "b"))


def turn_kernel(order_ref, x_ref, o_ref, held, *, blk):
    tokens, width = x_ref.shape
    for i in range(width // WIDE):
        held[i * WIDE : (i + 1) * WIDE, :] = x_ref[:, i * WIDE : (i + 1) * WIDE].T

    def move(i, _):
        source = pl.multiple_of(order_ref[i] * blk, blk)
        target = pl.multiple_of(i * blk, blk)
        o_ref[pl.ds(target, blk), :] = held[pl.ds(source, blk), :]
        return 0

    lax.fori_loop(0, width // blk, move, 0)


def turned(x, order):
    tokens, width = x.shape
    blk = width // order.shape[0]
    if blk % 16:
        blocks = jnp.take(x.T.reshape(order.shape[0], blk, tokens), order, axis=0)
        return blocks.reshape(width, tokens)
    return pl.pallas_call(
        functools.partial(turn_kernel, blk=blk),
        out_shape=jax.ShapeDtypeStruct((width, tokens), x.dtype),
        in_specs=[
            pl.BlockSpec(memory_space=pltpu.SMEM),
            pl.BlockSpec(memory_space=pltpu.VMEM),
        ],
        out_specs=pl.BlockSpec(memory_space=pltpu.VMEM),
        scratch_shapes=[pltpu.VMEM((width, tokens), x.dtype)],
        compiler_params=pltpu.CompilerParams(vmem_limit_bytes=32 << 20),
        cost_estimate=pl.CostEstimate(flops=0, bytes_accessed=4 * x.size, transcendentals=0),
        name="turned",
    )(order, x)


def reduce_term(grid, left, right, extra=None, around=False):
    rows = left.shape[0]
    mine = rows // 2

    def term(start, size):
        part = mm(left[start : start + size], right, NN)
        if extra is not None:
            part = jnp.concatenate([part, extra[start : start + size].astype(F32)], 1)
        return part

    (arrived,) = yield [grid.next(term(mine, mine).astype(BF16), "c")]
    held = []
    for h, axes in enumerate(HALVES):
        start = h * (mine // 2)
        count = grid.size(axes[0])
        size = mine // 2 // count
        held.append(
            [
                (term(at, size) + arrived[at : at + size].astype(F32)).astype(BF16)
                for at in range(start, start + count * size, size)
            ]
        )
    for step in range(2):
        totals = [None, None]
        counts = [grid.size(axes[step]) for axes in HALVES]
        for k in range(1, max(counts)):
            live = [h for h in range(2) if k < counts[h]]
            sent = [
                grid.next(held[h][1] if k == 1 else totals[h], HALVES[h][step]) for h in live
            ]
            came = yield sent
            for h, part in zip(live, came):
                own = held[h][(k + 1) % counts[h]]
                totals[h] = (part.astype(F32) + own.astype(F32)).astype(BF16)
        if step == 0:
            held = []
            for h, total in enumerate(totals):
                count = grid.size(HALVES[h][1])
                size = total.shape[0] // count
                held.append([total[j * size : (j + 1) * size] for j in range(count)])
    if not around:
        joined = jnp.concatenate(totals, 0)
        (share,) = yield [lax.psum_scatter(joined, "dp", scatter_dimension=0, tiled=True)]
        return share.astype(F32)
    half = grid.n_dp // 2
    size = totals[0].shape[0] // half
    held = [t[at : at + size] for t in totals for at in range(0, half * size, size)]
    total = held[1]
    for k in range(1, grid.n_dp):
        (came,) = yield [grid.next(total, "d")]
        total = came.astype(F32) + held[(k + 1) % grid.n_dp].astype(F32)
        total = total if k == grid.n_dp - 1 else total.astype(BF16)
    return total


def place_kernel(order_ref, *refs, sources, slots):
    pieces = refs[: -(3 + 1)]
    out_ref, held, in_sem, out_sem = refs[-4:]
    count = len(sources)

    def fetch(i):
        piece, place = sources[i]
        return pltpu.make_async_copy(
            pieces[piece].at[place], held.at[i % slots], in_sem.at[i % slots]
        )

    def store(i):
        return pltpu.make_async_copy(
            held.at[i % slots], out_ref.at[order_ref[i]], out_sem.at[i % slots]
        )

    ahead = slots // 2
    for i in range(min(ahead, count)):
        fetch(i).start()
    for i in range(count):
        fetch(i).wait()
        store(i).start()
        later = i + ahead
        if later < count:
            if later >= slots:
                store(later - slots).wait()
            fetch(later).start()
    for i in range(max(0, count - slots), count):
        store(i).wait()


def placed(order, pieces):
    blk, width = pieces[0].shape[-2:]
    flat = [p.reshape((-1, blk, width)) for p in pieces]
    sources = [(n, j) for n, p in enumerate(flat) for j in range(p.shape[0])]
    slots = 8
    whole = pl.pallas_call(
        functools.partial(place_kernel, sources=sources, slots=slots),
        out_shape=jax.ShapeDtypeStruct((len(sources), blk, width), flat[0].dtype),
        in_specs=[pl.BlockSpec(memory_space=pltpu.SMEM)]
        + [pl.BlockSpec(memory_space=pl.ANY)] * len(flat),
        out_specs=pl.BlockSpec(memory_space=pl.ANY),
        scratch_shapes=[
            pltpu.VMEM((slots, blk, width), flat[0].dtype),
            pltpu.SemaphoreType.DMA((slots,)),
            pltpu.SemaphoreType.DMA((slots,)),
        ],
        compiler_params=pltpu.CompilerParams(vmem_limit_bytes=16 << 20),
        cost_estimate=pl.CostEstimate(
            flops=0, bytes_accessed=4 * len(sources) * blk * width, transcendentals=0
        ),
        name="placed",
    )(order, *flat)
    return whole.reshape(len(sources) * blk, width)


def gather_weight(grid, weight, around=False):
    half = grid.n_dp // 2
    if around:
        column = [weight]
        for _ in range(grid.n_dp - 1):
            (came,) = yield [grid.next(column[-1], "d")]
            column.append(came)
        parts = [jnp.stack(column[:half]), jnp.stack(column[half:])]
    else:
        (column,) = yield [lax.all_gather(weight, "dp", axis=0)]
        parts = [column[:half], column[half:]]
    steps = [[parts[0]], [parts[1]]]
    for stage in (1, 0):
        counts = [grid.size(axes[stage]) for axes in HALVES]
        for k in range(1, max(counts)):
            live = [h for h in range(2) if k < counts[h]]
            came = yield [grid.next(steps[h][-1], HALVES[h][stage]) for h in live]
            for h, part in zip(live, came):
                steps[h].append(part)
        if stage == 1:
            steps = [[jnp.stack(s)] for s in steps]
    near = jnp.concatenate([p.reshape((-1,) + p.shape[-2:]) for p in steps[0] + steps[1]], 0)
    (far,) = yield [grid.next(near, "c")]
    return placed(grid.block_order(around), [near, far])


def gather_ring(grid, weight):
    part = weight
    for axis in ("a", "b"):
        steps = [part]
        for _ in range(grid.size(axis) - 1):
            (came,) = yield [grid.next(steps[-1], axis)]
            steps.append(came)
        part = jnp.stack(steps)
    near, far = [part], []
    waiting = [part]
    for k in range(grid.n_dp - 1):
        sent = [grid.next(near[-1], "d")]
        early = k == grid.n_dp - 2
        if early:
            sent.append(grid.next(jnp.stack(waiting[:-1]), "c"))
            waiting = waiting[-1:]
        came = yield sent
        if early:
            far.append(came[1])
        near.append(came[0])
        waiting.append(came[0])
    (other,) = yield [grid.next(jnp.stack(waiting), "c")]
    return placed(grid.ring_order(), near + far + [other])


def reduce_ring(grid, left, right):
    mine = left.shape[0] // 2
    (arrived,) = yield [grid.next(mm(left[mine:], right, NN).astype(BF16), "c")]
    size = mine // grid.n_dp
    held = [
        (mm(left[at : at + size], right, NN) + arrived[at : at + size].astype(F32)).astype(BF16)
        for at in range(0, mine, size)
    ]
    for axis in ("d", "b", "a"):
        count = grid.size(axis)
        total = held[1]
        for k in range(1, count):
            (came,) = yield [grid.next(total, axis)]
            total = (came.astype(F32) + held[(k + 1) % count].astype(F32)).astype(BF16)
        following = {"d": grid.n_b, "b": grid.n_a, "a": 1}[axis]
        size = total.shape[0] // following
        held = [total[at : at + size] for at in range(0, total.shape[0], size)]
    return held[0].astype(F32)


def gather_keys(grid, own):
    width = own.shape[1] // 2
    steps = [[own[:, :width]], [own[:, width:]]]
    for stage in (1, 0):
        counts = [grid.size(axes[stage]) for axes in HALVES]
        for k in range(1, max(counts)):
            live = [h for h in range(2) if k < counts[h]]
            came = yield [grid.next(steps[h][-1], HALVES[h][stage]) for h in live]
            for h, part in zip(live, came):
                steps[h].append(part)
        steps = [[jnp.stack(s)] for s in steps]
    near = [s[0] for s in steps]
    far = yield [grid.next(part, "c") for part in near]
    return tuple(
        jnp.stack([one, two]).reshape(-1, width) for one, two in zip(near, far)
    )


def reduce_keys(grid, terms):
    mine = terms.shape[0] // 2
    (came,) = yield [grid.next(terms[mine:], "c")]
    total = (terms[:mine].astype(F32) + came.astype(F32)).astype(BF16)
    for axis in ("b", "a"):
        count = grid.size(axis)
        size = total.shape[0] // count
        held = [total[at : at + size] for at in range(0, count * size, size)]
        total = held[1]
        for k in range(1, count):
            (came,) = yield [grid.next(total, axis)]
            total = (came.astype(F32) + held[(k + 1) % count].astype(F32)).astype(BF16)
    return total


class Chain:
    def __init__(self, generator):
        self.generator, self.done, self.result = generator, False, None
        self.flight = next(generator)

    def advance(self, arrived):
        try:
            self.flight = self.generator.send(arrived)
        except StopIteration as stop:
            self.done, self.result, self.flight = True, stop.value, []


def meet(main, *chains):
    chains = [c for c in chains if not c.done]
    main, flights = lax.optimization_barrier((main, [list(c.flight) for c in chains]))
    for chain, flight in zip(chains, flights):
        chain.advance(flight)
    return main


def settle(main, *chains):
    main, flights = lax.optimization_barrier((main, [list(c.flight) for c in chains]))
    for chain, flight in zip(chains, flights):
        chain.flight = flight
    return main


def finish(chain):
    while not chain.done:
        chain.advance(chain.flight)
    return chain.result


def angles(positions):
    lane = jnp.arange(WIDE)
    freq = 10000.0 ** (-((lane % (HD // 2)).astype(F32) * 2.0 / HD))
    turn = positions.astype(F32)[:, None] * freq[None, :]
    sign = jnp.where(lane % HD < HD // 2, -1.0, 1.0)
    return jnp.cos(turn), jnp.sin(turn) * sign[None, :]


def normalize(rows):
    factor = lax.rsqrt(jnp.mean(rows * rows, -1, keepdims=True) + EPS)
    return (rows * factor, factor)


def norm_back(upstream, normed, factor, gain):
    scaled = upstream * gain
    inner = jnp.mean(scaled * normed, -1, keepdims=True)
    return (factor * (scaled - normed * inner), jnp.sum(upstream * normed, 0))


def body(
    n_dp,
    n_ctx,
    layer_in,
    positions,
    attn_gain,
    query_proj,
    key_proj,
    value_proj,
    merge_proj,
    ffn_gain,
    gate_proj,
    up_proj,
    down_proj,
    out_grad,
):
    _, rows, model = layer_in.shape
    kv_width = key_proj.shape[1]
    kv_heads = kv_width // HD
    width = query_proj.shape[1]
    run = rows // 2
    positions = positions[0]
    grid = Grid(n_dp, n_ctx)
    order, sum_order = grid.block_order(False), grid.block_order(True)
    ring_order, ctx_order = grid.ring_order(), grid.ctx_order()
    places = grid.value_places()

    gains = jnp.stack([attn_gain, ffn_gain], -1)
    gains = jnp.concatenate([gains, jnp.zeros((gains.shape[0], WIDE - 2), BF16)], 1)
    packed = jnp.concatenate([query_proj, key_proj, value_proj, gains], 1)
    down_chain = Chain(gather_weight(grid, down_proj))
    first_chain = Chain(gather_weight(grid, packed, True))
    up_chain = Chain(gather_ring(grid, up_proj))
    all_pos = lax.all_gather(positions[::run], "ctx", axis=0, tiled=True)
    cosine, sine = angles(positions)
    rows_in = layer_in.reshape(rows, model).astype(F32)
    normed_one, factor_one = normalize(rows_in)
    all_pos, gate_proj = meet((all_pos, gate_proj), first_chain, up_chain)
    gate_chain = Chain(gather_weight(grid, gate_proj))
    factor_one, merge_proj = meet((factor_one, merge_proj), first_chain)
    merge_chain = Chain(gather_weight(grid, merge_proj))
    cosine, sine = meet((cosine, sine), first_chain)
    cosine = meet(cosine, first_chain, down_chain)
    first_weights = finish(first_chain)
    first_weights = meet(first_weights, down_chain, up_chain)
    first_weights = settle(first_weights, gate_chain)
    attn_all = first_weights[:, : width + 2 * kv_width]
    gain_one = first_weights[:, width + 2 * kv_width].astype(F32)
    gain_two = first_weights[:, width + 2 * kv_width + 1].astype(F32)

    first_in = (normed_one * gain_one).astype(BF16)
    raw = mm(first_in, attn_all, NN)
    queries, own_kv = rotated(raw, cosine, sine, kv_width)
    kv_chain = Chain(gather_keys(grid, own_kv))
    later = all_pos.reshape(n_ctx, 2)[ctx_order].reshape(2 * n_ctx, 1)
    later = later > jnp.repeat(positions[::run], run)[None, :]
    bias = jnp.where(later, MASKED, 0.0).astype(F32)
    bias = meet(bias, kv_chain)
    bias = meet(bias, kv_chain)
    bias = settle(bias, merge_chain)
    bias = meet(bias, kv_chain, gate_chain)
    all_keys, all_values = finish(kv_chain)
    kt, vt = all_keys.T, all_values.T

    grad_rows = out_grad.reshape(rows, model)
    plan = (
        (down_chain, gate_chain, up_chain),
        (down_chain, merge_chain),
        (gate_chain, merge_chain, up_chain),
        (gate_chain, merge_chain),
    )
    outs, log_sums = [], []
    for group in range(kv_heads):
        out, log_sum = attend(group, places, bias, queries, all_keys, vt)
        queries, out, grad_rows = meet((queries, out, grad_rows), *plan[group % 4])
        if group == 1:
            down_all = finish(down_chain)
            grad_hidden = mm(grad_rows, down_all, NT)
            queries, grad_hidden = lax.optimization_barrier((queries, grad_hidden))
        outs.append(out)
        log_sums.append(log_sum)
    mixed = jnp.concatenate([out.astype(BF16) for out in outs], 1)
    gate_all, merge_all = finish(gate_chain), finish(merge_chain)
    middle = rows_in + mm(mixed, merge_all, NN)
    normed_two, factor_two = normalize(middle)
    second_in = (normed_two * gain_two).astype(BF16)
    gate = mm(second_in, gate_all, NN)
    gate = meet(gate, up_chain)
    up_all = finish(up_chain)
    lift = mm(second_in, up_all, NN)
    sigma = jax.nn.sigmoid(gate)
    activated = gate * sigma
    hidden = (activated * lift).astype(BF16)
    grad_gate = (grad_hidden * lift * sigma * (1.0 + gate * (1.0 - sigma))).astype(BF16)
    grad_lift = (grad_hidden * activated).astype(BF16)
    hidden, grad_gate, grad_lift = lax.optimization_barrier((hidden, grad_gate, grad_lift))
    second_turned = turned(second_in, order)
    gate_sum = Chain(reduce_term(grid, second_turned, grad_gate))
    up_sum = Chain(reduce_term(grid, second_turned, grad_lift))
    down_sum = Chain(reduce_ring(grid, turned(hidden, ring_order), grad_rows))
    grad_second = mm(grad_gate, gate_all, NT)
    grad_second, grad_lift, hidden = meet((grad_second, grad_lift, hidden), gate_sum)
    grad_second = grad_second + mm(grad_lift, up_all, NT)
    result = middle + mm(hidden, down_all, NN)
    layer_out = result.astype(BF16).reshape(layer_in.shape)
    grad_norm_two, gain_two_term = norm_back(grad_second, normed_two, factor_two, gain_two)
    grad_middle = grad_rows.astype(F32) + grad_norm_two
    grad_branch = grad_middle.astype(BF16)
    grad_mixed = mm(grad_branch, merge_all, NT).astype(BF16)
    grad_mixed, layer_out, grad_branch = meet(
        (grad_mixed, layer_out, grad_branch), down_sum, up_sum
    )
    first_turned = turned(first_in, sum_order)
    mixed_turned = turned(mixed, order)

    dqs, dkvs = [], []
    for group in range(kv_heads):
        dq, dkv = attend_back(
            group, places, bias, log_sums[group], outs[group], queries, grad_mixed,
            all_keys, all_values, kt,
        )
        dqs.append(dq)
        dkvs.append(dkv)
        if group == kv_heads - 4:
            grad_mixed, dkv, grad_branch = meet(
                (grad_mixed, dkv, grad_branch), gate_sum, down_sum
            )
        elif group == kv_heads - 3:
            grad_mixed, dkv, grad_branch = meet(
                (grad_mixed, dkv, grad_branch), gate_sum, up_sum, down_sum
            )
            merge_sum = Chain(reduce_term(grid, mixed_turned, grad_branch))
        elif group == kv_heads - 2:
            early_grads = unrotated(unrotate_queries_kernel, dqs, cosine, sine)
            grad_mixed, early_grads, dkvs = meet(
                (grad_mixed, early_grads, dkvs), up_sum, merge_sum, down_sum
            )
            early = Chain(reduce_term(grid, first_turned, early_grads, around=True))
            keys_sum = Chain(reduce_keys(grid, jnp.concatenate(dkvs, 1)))
    dq, dkv = meet((dq, dkv), gate_sum, merge_sum, down_sum, early, keys_sum)
    last_keys = Chain(reduce_keys(grid, dkv))
    late_grads = unrotated(unrotate_queries_kernel, dqs[-1:], cosine, sine)
    split = early_grads.shape[1]
    grad_first = mm(early_grads, attn_all[:, :split], NT)
    grad_first = meet(grad_first, last_keys, keys_sum)
    grad_first = grad_first + mm(late_grads, attn_all[:, split:width], NT)
    late = Chain(reduce_term(grid, first_turned, late_grads, around=True))
    grad_first = meet(grad_first, last_keys, keys_sum, early, merge_sum)
    grad_first = meet(grad_first, last_keys, up_sum, down_sum)
    wide = finish(keys_sum)
    dkv_parts = [wide[:, at : at + WIDE] for at in range(0, wide.shape[1], WIDE)]
    dkv_parts.append(finish(last_keys))
    kv_grads = unrotated(unrotate_keys_kernel, dkv_parts, cosine, sine)
    grad_first = grad_first + mm(kv_grads, attn_all[:, width:], NT)
    grad_norm_one, gain_one_term = norm_back(grad_first, normed_one, factor_one, gain_one)
    gain_terms = jnp.stack([gain_one_term, gain_two_term], 0)
    gain_terms = jnp.concatenate([gain_terms, jnp.zeros((WIDE - 2, model), F32)], 0)
    gain_terms = meet(gain_terms, early, late, down_sum)
    gain_columns = turned(gain_terms.astype(BF16), sum_order)
    last = Chain(reduce_term(grid, first_turned, kv_grads, gain_columns, around=True))
    input_grad = (grad_middle + grad_norm_one).astype(BF16).reshape(layer_in.shape)
    waiting = (last, late, early, down_sum)
    while not all(c.done for c in waiting):
        input_grad = meet(input_grad, *waiting)
    early_share, late_share, last_share = finish(early), finish(late), finish(last)
    merge_share, gate_share = finish(merge_sum), finish(gate_sum)
    up_share, down_share = finish(up_sum), finish(down_sum)
    return (
        layer_out,
        input_grad,
        last_share[:, 2 * kv_width],
        jnp.concatenate([early_share, late_share], 1),
        last_share[:, :kv_width],
        last_share[:, kv_width : 2 * kv_width],
        merge_share,
        last_share[:, 2 * kv_width + 1],
        gate_share,
        up_share,
        down_share,
    )


def solution(mesh):
    acts = P("dp", "ctx", None)
    rows = P(BOTH, None)
    flat = P(BOTH)
    return jax.shard_map(
        functools.partial(body, mesh.shape["dp"], mesh.shape["ctx"]),
        mesh=mesh,
        in_specs=(acts, P("dp", "ctx"), flat, rows, rows, rows, rows, flat, rows, rows, rows, acts),
        out_specs=(acts, acts, flat, rows, rows, rows, rows, flat, rows, rows, rows),
        check_vma=False,
    )
```

```python
import functools

import jax
import jax.numpy as jnp
import numpy as np
from jax import lax
from jax.experimental import pallas as pl
from jax.experimental.pallas import tpu as pltpu
from jax.sharding import PartitionSpec as P

HD = 64
EPS = 1e-05
WIDE = 128
MASKED = -1e30
SCALE = HD**-0.5
LOG2E = 1.4426950408889634
TO_LOG2 = SCALE * LOG2E
BRIEF = pl.CostEstimate(flops=1 << 20, bytes_accessed=1 << 16, transcendentals=0)
F32 = jnp.float32
BF16 = jnp.bfloat16
NT = (((1,), (1,)), ((), ()))
NN = (((1,), (0,)), ((), ()))


def mm(left, right, dims):
    return lax.dot_general(left, right, dims, preferred_element_type=F32)


def same_run_later(keys, rows):
    run = rows // 2
    key = lax.broadcasted_iota(jnp.int32, (keys, rows), 0)
    query = lax.broadcasted_iota(jnp.int32, (keys, rows), 1)
    return (key > query) & ((key // run) == (query // run))


def split_heads(pair_ref, which, low_ref, high_ref):
    both = pair_ref[...]
    turned = pltpu.roll(both.astype(F32), HD, 1).astype(BF16)
    lane = lax.broadcasted_iota(jnp.int32, both.shape, 1)
    zero = jnp.zeros_like(both)
    first, second = (both, turned) if which == 0 else (turned, both)
    low_ref[...] = jnp.where(lane < HD, first, zero)
    high_ref[...] = jnp.where(lane < HD, zero, second)


def biased(scores, bias_ref, block, rows):
    run = rows // 2
    start = pl.multiple_of(block * rows, rows)
    parts = [
        scores[i * run : (i + 1) * run] + bias_ref[pl.ds(block * 2 + i, 1), :]
        for i in range(2)
    ]
    return jnp.concatenate(parts, 0)


def attend_kernel(
    bias_ref, q_ref, kp_ref, vt_ref, o_ref, lse_ref, low, high, vx, turned, *, which, places
):
    rows, width = q_ref.shape
    length = kp_ref.shape[0]
    blocks = length // rows
    split_heads(kp_ref, which, low, high)
    vx[:HD, :] = vt_ref[...]
    top_row = lax.broadcasted_iota(jnp.int32, (16, length), 0) == 0
    vx[HD:, :] = top_row.astype(F32).astype(BF16)

    def scores(key, pair, block):
        start = pl.multiple_of(block * rows, rows)
        column = pl.multiple_of(pair * WIDE, WIDE)
        s = mm(key[pl.ds(start, rows), :], q_ref[:, pl.ds(column, WIDE)], NT) * TO_LOG2
        return biased(s, bias_ref, block, rows)

    def weigh(probs, block):
        start = places[block] * rows
        return mm(vx[:, start : start + rows], probs.astype(BF16), NN)

    def one_pair(pair, _):
        blocked = same_run_later(rows, rows)
        state = []
        for key in (low, high):
            s = jnp.where(blocked, MASKED, scores(key, pair, 0))
            top = jnp.max(s, 0, keepdims=True)
            state.append((top, weigh(jnp.exp2(s - top), 0)))

        def step(block, state):
            raw = [scores(key, pair, block) for key in (low, high)]
            result = []
            for (top, total), s in zip(state, raw):
                new_top = jnp.maximum(top, jnp.max(s, 0, keepdims=True))
                probs = jnp.exp2(s - new_top)
                result.append((new_top, total * jnp.exp2(top - new_top) + weigh(probs, block)))
            return result

        for block in range(1, blocks):
            state = step(block, state)
        for i, (top, total) in enumerate(state):
            weight_sum = total[HD : HD + 1, :]
            turned[i * HD : (i + 1) * HD, :] = total[:HD] / weight_sum
            lse_ref[pl.ds(pair * 2 + i, 1), :] = top + jnp.log2(weight_sum)
        column = pl.multiple_of(pair * WIDE, WIDE)
        o_ref[:, pl.ds(column, WIDE)] = turned[...].T
        return 0

    lax.fori_loop(0, width // WIDE, one_pair, 0)


def attend(group, places, bias, q, keys, vt):
    rows, width = q.shape
    length = keys.shape[0]
    kv_heads = vt.shape[0] // HD
    mine = width // kv_heads
    heads = mine // HD
    return pl.pallas_call(
        functools.partial(attend_kernel, which=group % 2, places=places),
        grid=(1,),
        out_shape=(
            jax.ShapeDtypeStruct((rows, mine), F32),
            jax.ShapeDtypeStruct((heads, rows), F32),
        ),
        in_specs=[
            pl.BlockSpec(bias.shape, lambda i: (0, 0)),
            pl.BlockSpec((rows, mine), lambda i: (0, group)),
            pl.BlockSpec((length, WIDE), lambda i: (0, group // 2)),
            pl.BlockSpec((HD, length), lambda i: (group, 0)),
        ],
        out_specs=(
            pl.BlockSpec((rows, mine), lambda i: (0, 0)),
            pl.BlockSpec((heads, rows), lambda i: (0, 0)),
        ),
        scratch_shapes=[
            pltpu.VMEM((length, WIDE), BF16),
            pltpu.VMEM((length, WIDE), BF16),
            pltpu.VMEM((HD + 16, length), BF16),
            pltpu.VMEM((WIDE, rows), F32),
        ],
        compiler_params=pltpu.CompilerParams(vmem_limit_bytes=40 << 20),
        cost_estimate=BRIEF,
        name="attend",
    )(bias, q, keys, vt)


def attend_back_kernel(
    place_ref, bias_ref, lse_ref, o_ref, q_ref, g_ref, kp_ref, vp_ref, kt_ref,
    dq_ref, dkv_ref, k_low, k_high, v_low, v_high, dqt, delta_ref, *, which, unroll
):
    rows, width = q_ref.shape
    length = kp_ref.shape[0]
    blocks = length // rows
    pairs = width // WIDE
    split_heads(kp_ref, which, k_low, k_high)
    split_heads(vp_ref, which, v_low, v_high)
    row = lax.broadcasted_iota(jnp.int32, (16, WIDE), 0)
    lane = lax.broadcasted_iota(jnp.int32, (16, WIDE), 1)
    chosen = (row == lane // HD).astype(F32).astype(BF16)
    for pair in range(pairs):
        column = pl.ds(pair * WIDE, WIDE)
        product = g_ref[:, column].astype(F32) * o_ref[:, column]
        main = product.astype(BF16)
        rest = (product - main.astype(F32)).astype(BF16)
        both = mm(chosen, main, NT) + mm(chosen, rest, NT)
        delta_ref[2 * pair : 2 * pair + 2, :] = both[:2]

    def block(index, diagonal):
        start = pl.multiple_of(index * rows, rows)
        value_start = pl.multiple_of(place_ref[index] * rows, rows)

        def some_heads(i, sums):
            sums = list(sums)
            work = []
            for t in range(unroll):
                pair = i * unroll + t
                column = pl.multiple_of(pair * WIDE, WIDE)
                query = q_ref[:, pl.ds(column, WIDE)]
                grad = g_ref[:, pl.ds(column, WIDE)]
                for side, (key, value) in enumerate(((k_low, v_low), (k_high, v_high))):
                    head = pair * 2 + side
                    shift = -lse_ref[pl.ds(head, 1), :]
                    run = rows // 2
                    s = mm(key[pl.ds(start, rows), :], query, NT) * TO_LOG2
                    s = jnp.concatenate(
                        [
                            s[r * run : (r + 1) * run]
                            + (bias_ref[pl.ds(index * 2 + r, 1), :] + shift)
                            for r in range(2)
                        ],
                        0,
                    )
                    p = jnp.exp2(s)
                    if diagonal:
                        p = jnp.where(same_run_later(rows, rows), 0.0, p)
                    slope = mm(value[pl.ds(value_start, rows), :], grad, NT)
                    d = (p * (slope - delta_ref[pl.ds(head, 1), :])).astype(BF16)
                    work.append((side, pair, query, grad, p.astype(BF16), d))
            for side, pair, query, grad, p, d in work:
                sums[side] = sums[side] + mm(d, query, NN)
                sums[2 + side] = sums[2 + side] + mm(p, grad, NN)
                term = mm(kt_ref[:, pl.ds(start, rows)], d, NN)
                row = pl.multiple_of(pair * WIDE + side * HD, HD)
                if diagonal:
                    dqt[pl.ds(row, HD), :] = term
                else:
                    dqt[pl.ds(row, HD), :] += term
            return tuple(sums)

        zero = jnp.zeros((rows, WIDE), F32)
        sums = lax.fori_loop(0, pairs // unroll, some_heads, (zero,) * 4)
        lane = lax.broadcasted_iota(jnp.int32, (rows, WIDE), 1)
        key_sum = sums[0] + pltpu.roll(sums[1], HD, 1)
        value_sum = pltpu.roll(sums[2], HD, 1) + sums[3]
        dkv_ref[pl.ds(start, rows), :] = jnp.where(
            lane < HD, key_sum * SCALE, value_sum
        ).astype(BF16)

    block(0, True)

    def rest(j, _):
        block(j, False)
        return 0

    lax.fori_loop(1, blocks, rest, 0)
    for pair in range(pairs):
        dq_ref[:, pair * WIDE : (pair + 1) * WIDE] = (
            dqt[pair * WIDE : (pair + 1) * WIDE, :] * SCALE
        ).T


def attend_back(group, places, bias, lse, out, q, g, keys, values, kt, unroll=2):
    rows, width = q.shape
    length = keys.shape[0]
    kv_heads = kt.shape[0] // HD
    mine = width // kv_heads
    heads = mine // HD
    return pl.pallas_call(
        functools.partial(attend_back_kernel, which=group % 2, unroll=unroll),
        grid=(1,),
        out_shape=(
            jax.ShapeDtypeStruct((rows, mine), F32),
            jax.ShapeDtypeStruct((length, WIDE), BF16),
        ),
        in_specs=[
            pl.BlockSpec(memory_space=pltpu.SMEM),
            pl.BlockSpec(bias.shape, lambda i: (0, 0)),
            pl.BlockSpec((heads, rows), lambda i: (0, 0)),
            pl.BlockSpec((rows, mine), lambda i: (0, 0)),
            pl.BlockSpec((rows, mine), lambda i: (0, group)),
            pl.BlockSpec((rows, mine), lambda i: (0, group)),
            pl.BlockSpec((length, WIDE), lambda i: (0, group // 2)),
            pl.BlockSpec((length, WIDE), lambda i: (0, group // 2)),
            pl.BlockSpec((HD, length), lambda i: (group, 0)),
        ],
        out_specs=(
            pl.BlockSpec((rows, mine), lambda i: (0, 0)),
            pl.BlockSpec((length, WIDE), lambda i: (0, 0)),
        ),
        scratch_shapes=[pltpu.VMEM((length, WIDE), BF16)] * 4
        + [pltpu.VMEM((mine, rows), F32), pltpu.VMEM((heads, rows), F32)],
        compiler_params=pltpu.CompilerParams(vmem_limit_bytes=48 << 20),
        cost_estimate=BRIEF,
        name="attend_back",
    )(jnp.array(places, jnp.int32), bias, lse, out, q, g, keys, values, kt)


def turn_pairs(x, cosine, sine):
    lane = lax.broadcasted_iota(jnp.int32, x.shape, 1)
    swapped = jnp.where(
        lane % HD < HD // 2, pltpu.roll(x, WIDE - HD // 2, 1), pltpu.roll(x, HD // 2, 1)
    )
    return x * cosine + swapped * sine


def rotate_kernel(cos_ref, sin_ref, raw_ref, q_ref, kv_ref, *, kv_width):
    cosine, sine = cos_ref[...], sin_ref[...]
    width = q_ref.shape[1]
    for at in range(0, width, WIDE):
        q_ref[:, at : at + WIDE] = turn_pairs(raw_ref[:, at : at + WIDE], cosine, sine).astype(BF16)
    for at in range(0, kv_width, WIDE):
        column = slice(width + at, width + at + WIDE)
        kv_ref[:, at : at + WIDE] = turn_pairs(raw_ref[:, column], cosine, sine).astype(BF16)
    kv_ref[:, kv_width:] = raw_ref[:, width + kv_width :].astype(BF16)


def rotated(raw, cosine, sine, kv_width):
    rows, total = raw.shape
    return pl.pallas_call(
        functools.partial(rotate_kernel, kv_width=kv_width),
        out_shape=(
            jax.ShapeDtypeStruct((rows, total - 2 * kv_width), BF16),
            jax.ShapeDtypeStruct((rows, 2 * kv_width), BF16),
        ),
        in_specs=[pl.BlockSpec(memory_space=pltpu.VMEM)] * 3,
        out_specs=(pl.BlockSpec(memory_space=pltpu.VMEM),) * 2,
        compiler_params=pltpu.CompilerParams(vmem_limit_bytes=32 << 20),
        cost_estimate=pl.CostEstimate(
            flops=8 * raw.size, bytes_accessed=6 * raw.size, transcendentals=0
        ),
        name="rotated",
    )(cosine, sine, raw)


def unrotate_queries_kernel(cos_ref, sin_ref, *refs):
    cosine, sine = cos_ref[...], -sin_ref[...]
    out_ref = refs[-1]
    mine = refs[0].shape[1]
    for n, ref in enumerate(refs[:-1]):
        for at in range(0, mine, WIDE):
            turned = turn_pairs(ref[:, at : at + WIDE], cosine, sine)
            out_ref[:, n * mine + at : n * mine + at + WIDE] = turned.astype(BF16)


def unrotate_keys_kernel(cos_ref, sin_ref, *refs):
    cosine, sine = cos_ref[...], -sin_ref[...]
    out_ref = refs[-1]
    count = len(refs) - 1
    lane = lax.broadcasted_iota(jnp.int32, cosine.shape, 1)
    for i in range(count // 2):
        first, second = refs[2 * i][...].astype(F32), refs[2 * i + 1][...].astype(F32)
        keys = jnp.where(lane < HD, first, pltpu.roll(second, HD, 1))
        values = jnp.where(lane < HD, pltpu.roll(first, HD, 1), second)
        at = i * WIDE
        out_ref[:, at : at + WIDE] = turn_pairs(keys, cosine, sine).astype(BF16)
        at = count * HD + i * WIDE
        out_ref[:, at : at + WIDE] = values.astype(BF16)


def unrotated(kernel, parts, cosine, sine):
    rows, mine = parts[0].shape
    total = len(parts) * mine
    return pl.pallas_call(
        kernel,
        out_shape=jax.ShapeDtypeStruct((rows, total), BF16),
        in_specs=[pl.BlockSpec(memory_space=pltpu.VMEM)] * (2 + len(parts)),
        out_specs=pl.BlockSpec(memory_space=pltpu.VMEM),
        compiler_params=pltpu.CompilerParams(vmem_limit_bytes=32 << 20),
        cost_estimate=pl.CostEstimate(
            flops=8 * rows * total, bytes_accessed=6 * rows * total, transcendentals=0
        ),
        name="unrotated",
    )(cosine, sine, *parts)


BOTH = ("dp", "ctx")


class Grid:
    def __init__(self, n_dp, n_ctx):
        self.n_dp, self.n_a, self.n_b = n_dp, 2, n_ctx // 4
        self.n_ctx = n_ctx
        self.ring = [0, 1, 3, 2] if n_dp == 4 else list(range(n_dp))
        own = lax.axis_index("ctx").astype(jnp.int32)
        self.a = own // (2 * self.n_b)
        self.b = (own // 2) % self.n_b
        self.c = own % 2
        places = np.argsort(np.array(self.ring)).astype(np.int32)
        self.d = jnp.asarray(places)[lax.axis_index("dp")]

    def size(self, axis):
        return {"a": self.n_a, "b": self.n_b, "c": 2, "d": self.n_dp}[axis]

    def next(self, values, axis):
        if axis == "d":
            around = self.ring[1:] + self.ring[:1]
            return lax.ppermute(values, "dp", list(zip(self.ring, around)))
        pairs = []
        for i in range(self.n_ctx):
            a, b, c = i // (2 * self.n_b), (i // 2) % self.n_b, i % 2
            if axis == "a":
                a = (a + 1) % self.n_a
            elif axis == "b":
                b = (b + 1) % self.n_b
            else:
                c = 1 - c
            pairs.append((i, (a * self.n_b + b) * 2 + c))
        return lax.ppermute(values, "ctx", pairs)

    def natural(self, rows):
        rows = np.array(rows, np.int32)
        a = (self.a - rows[:, 2]) % self.n_a
        b = (self.b - rows[:, 3]) % self.n_b
        c = (self.c - rows[:, 0]) % 2
        return ((rows[:, 1] * self.n_a + a) * self.n_b + b) * 2 + c

    def block_order(self, around):
        half = self.n_dp // 2
        rows, hops = [], []
        for core in range(2):
            for h, (first, second) in enumerate(HALVES):
                for i in range(self.size(first)):
                    for j in range(self.size(second)):
                        for d in range(half):
                            near = {first: i, second: j}
                            at = h * half + d
                            rows.append((core, 0 if around else at, near["a"], near["b"]))
                            hops.append(at)
        return self.natural(rows) + (self.around(hops) * self.n_ctx if around else 0)

    def around(self, hops):
        ring = jnp.asarray(np.array(self.ring, np.int32))
        return ring[(self.d - np.array(hops, np.int32)) % self.n_dp]

    def ring_order(self):
        rows, hops = [], []
        for core in range(2):
            for d in range(self.n_dp):
                for b in range(self.n_b):
                    for a in range(self.n_a):
                        rows.append((core, 0, a, b))
                        hops.append(d)
        return self.natural(rows) + self.around(hops) * self.n_ctx

    def ctx_order(self):
        rows = [
            (c, 0, a, b) for c in range(2) for b in range(self.n_b) for a in range(self.n_a)
        ]
        return self.natural(rows)

    def value_places(self):
        cells = [(c, b, a) for c in range(2) for b in range(self.n_b) for a in range(self.n_a)]
        return tuple((c * self.n_a + a) * self.n_b + b for c, b, a in cells)


HALVES = (("b", "a"), ("a", "b"))


def turn_kernel(order_ref, x_ref, o_ref, held, *, blk):
    tokens, width = x_ref.shape
    for i in range(width // WIDE):
        held[i * WIDE : (i + 1) * WIDE, :] = x_ref[:, i * WIDE : (i + 1) * WIDE].T

    def move(i, _):
        source = pl.multiple_of(order_ref[i] * blk, blk)
        target = pl.multiple_of(i * blk, blk)
        o_ref[pl.ds(target, blk), :] = held[pl.ds(source, blk), :]
        return 0

    lax.fori_loop(0, width // blk, move, 0)


def turned(x, order):
    tokens, width = x.shape
    blk = width // order.shape[0]
    if blk % 16:
        blocks = jnp.take(x.T.reshape(order.shape[0], blk, tokens), order, axis=0)
        return blocks.reshape(width, tokens)
    return pl.pallas_call(
        functools.partial(turn_kernel, blk=blk),
        out_shape=jax.ShapeDtypeStruct((width, tokens), x.dtype),
        in_specs=[
            pl.BlockSpec(memory_space=pltpu.SMEM),
            pl.BlockSpec(memory_space=pltpu.VMEM),
        ],
        out_specs=pl.BlockSpec(memory_space=pltpu.VMEM),
        scratch_shapes=[pltpu.VMEM((width, tokens), x.dtype)],
        compiler_params=pltpu.CompilerParams(vmem_limit_bytes=32 << 20),
        cost_estimate=pl.CostEstimate(flops=0, bytes_accessed=4 * x.size, transcendentals=0),
        name="turned",
    )(order, x)


def reduce_term(grid, left, right, extra=None, around=False):
    rows = left.shape[0]
    mine = rows // 2

    def term(start, size):
        part = mm(left[start : start + size], right, NN)
        if extra is not None:
            part = jnp.concatenate([part, extra[start : start + size].astype(F32)], 1)
        return part

    (arrived,) = yield [grid.next(term(mine, mine).astype(BF16), "c")]
    held = []
    for h, axes in enumerate(HALVES):
        start = h * (mine // 2)
        count = grid.size(axes[0])
        size = mine // 2 // count
        held.append(
            [
                (term(at, size) + arrived[at : at + size].astype(F32)).astype(BF16)
                for at in range(start, start + count * size, size)
            ]
        )
    for step in range(2):
        totals = [None, None]
        counts = [grid.size(axes[step]) for axes in HALVES]
        for k in range(1, max(counts)):
            live = [h for h in range(2) if k < counts[h]]
            sent = [
                grid.next(held[h][1] if k == 1 else totals[h], HALVES[h][step]) for h in live
            ]
            came = yield sent
            for h, part in zip(live, came):
                own = held[h][(k + 1) % counts[h]]
                totals[h] = (part.astype(F32) + own.astype(F32)).astype(BF16)
        if step == 0:
            held = []
            for h, total in enumerate(totals):
                count = grid.size(HALVES[h][1])
                size = total.shape[0] // count
                held.append([total[j * size : (j + 1) * size] for j in range(count)])
    if not around:
        joined = jnp.concatenate(totals, 0)
        (share,) = yield [lax.psum_scatter(joined, "dp", scatter_dimension=0, tiled=True)]
        return share.astype(F32)
    half = grid.n_dp // 2
    size = totals[0].shape[0] // half
    held = [t[at : at + size] for t in totals for at in range(0, half * size, size)]
    total = held[1]
    for k in range(1, grid.n_dp):
        (came,) = yield [grid.next(total, "d")]
        total = came.astype(F32) + held[(k + 1) % grid.n_dp].astype(F32)
        total = total if k == grid.n_dp - 1 else total.astype(BF16)
    return total


def place_kernel(order_ref, *refs, sources, slots):
    pieces = refs[: -(3 + 1)]
    out_ref, held, in_sem, out_sem = refs[-4:]
    count = len(sources)

    def fetch(i):
        piece, place = sources[i]
        return pltpu.make_async_copy(
            pieces[piece].at[place], held.at[i % slots], in_sem.at[i % slots]
        )

    def store(i):
        return pltpu.make_async_copy(
            held.at[i % slots], out_ref.at[order_ref[i]], out_sem.at[i % slots]
        )

    ahead = slots // 2
    for i in range(min(ahead, count)):
        fetch(i).start()
    for i in range(count):
        fetch(i).wait()
        store(i).start()
        later = i + ahead
        if later < count:
            if later >= slots:
                store(later - slots).wait()
            fetch(later).start()
    for i in range(max(0, count - slots), count):
        store(i).wait()


def placed(order, pieces):
    blk, width = pieces[0].shape[-2:]
    flat = [p.reshape((-1, blk, width)) for p in pieces]
    sources = [(n, j) for n, p in enumerate(flat) for j in range(p.shape[0])]
    slots = 8
    whole = pl.pallas_call(
        functools.partial(place_kernel, sources=sources, slots=slots),
        out_shape=jax.ShapeDtypeStruct((len(sources), blk, width), flat[0].dtype),
        in_specs=[pl.BlockSpec(memory_space=pltpu.SMEM)]
        + [pl.BlockSpec(memory_space=pl.ANY)] * len(flat),
        out_specs=pl.BlockSpec(memory_space=pl.ANY),
        scratch_shapes=[
            pltpu.VMEM((slots, blk, width), flat[0].dtype),
            pltpu.SemaphoreType.DMA((slots,)),
            pltpu.SemaphoreType.DMA((slots,)),
        ],
        compiler_params=pltpu.CompilerParams(vmem_limit_bytes=16 << 20),
        cost_estimate=pl.CostEstimate(
            flops=0, bytes_accessed=4 * len(sources) * blk * width, transcendentals=0
        ),
        name="placed",
    )(order, *flat)
    return whole.reshape(len(sources) * blk, width)


def gather_weight(grid, weight, around=False):
    half = grid.n_dp // 2
    if around:
        column = [weight]
        for _ in range(grid.n_dp - 1):
            (came,) = yield [grid.next(column[-1], "d")]
            column.append(came)
        parts = [jnp.stack(column[:half]), jnp.stack(column[half:])]
    else:
        (column,) = yield [lax.all_gather(weight, "dp", axis=0)]
        parts = [column[:half], column[half:]]
    steps = [[parts[0]], [parts[1]]]
    for stage in (1, 0):
        counts = [grid.size(axes[stage]) for axes in HALVES]
        for k in range(1, max(counts)):
            live = [h for h in range(2) if k < counts[h]]
            came = yield [grid.next(steps[h][-1], HALVES[h][stage]) for h in live]
            for h, part in zip(live, came):
                steps[h].append(part)
        if stage == 1:
            steps = [[jnp.stack(s)] for s in steps]
    near = jnp.concatenate([p.reshape((-1,) + p.shape[-2:]) for p in steps[0] + steps[1]], 0)
    (far,) = yield [grid.next(near, "c")]
    return placed(grid.block_order(around), [near, far])


def gather_ring(grid, weight):
    part = weight
    for axis in ("a", "b"):
        steps = [part]
        for _ in range(grid.size(axis) - 1):
            (came,) = yield [grid.next(steps[-1], axis)]
            steps.append(came)
        part = jnp.stack(steps)
    near, far = [part], []
    waiting = [part]
    for k in range(grid.n_dp - 1):
        sent = [grid.next(near[-1], "d")]
        early = k == grid.n_dp - 2
        if early:
            sent.append(grid.next(jnp.stack(waiting[:-1]), "c"))
            waiting = waiting[-1:]
        came = yield sent
        if early:
            far.append(came[1])
        near.append(came[0])
        waiting.append(came[0])
    (other,) = yield [grid.next(jnp.stack(waiting), "c")]
    return placed(grid.ring_order(), near + far + [other])


def reduce_ring(grid, left, right):
    mine = left.shape[0] // 2
    (arrived,) = yield [grid.next(mm(left[mine:], right, NN).astype(BF16), "c")]
    size = mine // grid.n_dp
    held = [
        (mm(left[at : at + size], right, NN) + arrived[at : at + size].astype(F32)).astype(BF16)
        for at in range(0, mine, size)
    ]
    for axis in ("d", "b", "a"):
        count = grid.size(axis)
        total = held[1]
        for k in range(1, count):
            (came,) = yield [grid.next(total, axis)]
            total = (came.astype(F32) + held[(k + 1) % count].astype(F32)).astype(BF16)
        following = {"d": grid.n_b, "b": grid.n_a, "a": 1}[axis]
        size = total.shape[0] // following
        held = [total[at : at + size] for at in range(0, total.shape[0], size)]
    return held[0].astype(F32)


def gather_keys(grid, own):
    width = own.shape[1] // 2
    steps = [[own[:, :width]], [own[:, width:]]]
    for stage in (1, 0):
        counts = [grid.size(axes[stage]) for axes in HALVES]
        for k in range(1, max(counts)):
            live = [h for h in range(2) if k < counts[h]]
            came = yield [grid.next(steps[h][-1], HALVES[h][stage]) for h in live]
            for h, part in zip(live, came):
                steps[h].append(part)
        steps = [[jnp.stack(s)] for s in steps]
    near = [s[0] for s in steps]
    far = yield [grid.next(part, "c") for part in near]
    return tuple(
        jnp.stack([one, two]).reshape(-1, width) for one, two in zip(near, far)
    )


def reduce_keys(grid, terms):
    mine = terms.shape[0] // 2
    (came,) = yield [grid.next(terms[mine:], "c")]
    total = (terms[:mine].astype(F32) + came.astype(F32)).astype(BF16)
    for axis in ("b", "a"):
        count = grid.size(axis)
        size = total.shape[0] // count
        held = [total[at : at + size] for at in range(0, count * size, size)]
        total = held[1]
        for k in range(1, count):
            (came,) = yield [grid.next(total, axis)]
            total = (came.astype(F32) + held[(k + 1) % count].astype(F32)).astype(BF16)
    return total


class Chain:
    def __init__(self, generator):
        self.generator, self.done, self.result = generator, False, None
        self.flight = next(generator)

    def advance(self, arrived):
        try:
            self.flight = self.generator.send(arrived)
        except StopIteration as stop:
            self.done, self.result, self.flight = True, stop.value, []


def meet(main, *chains):
    chains = [c for c in chains if not c.done]
    main, flights = lax.optimization_barrier((main, [list(c.flight) for c in chains]))
    for chain, flight in zip(chains, flights):
        chain.advance(flight)
    return main


def settle(main, *chains):
    main, flights = lax.optimization_barrier((main, [list(c.flight) for c in chains]))
    for chain, flight in zip(chains, flights):
        chain.flight = flight
    return main


def finish(chain):
    while not chain.done:
        chain.advance(chain.flight)
    return chain.result


def angles(positions):
    lane = jnp.arange(WIDE)
    freq = 10000.0 ** (-((lane % (HD // 2)).astype(F32) * 2.0 / HD))
    turn = positions.astype(F32)[:, None] * freq[None, :]
    sign = jnp.where(lane % HD < HD // 2, -1.0, 1.0)
    return jnp.cos(turn), jnp.sin(turn) * sign[None, :]


def normalize(rows):
    factor = lax.rsqrt(jnp.mean(rows * rows, -1, keepdims=True) + EPS)
    return (rows * factor, factor)


def norm_back(upstream, normed, factor, gain):
    scaled = upstream * gain
    inner = jnp.mean(scaled * normed, -1, keepdims=True)
    return (factor * (scaled - normed * inner), jnp.sum(upstream * normed, 0))


def body(
    n_dp,
    n_ctx,
    layer_in,
    positions,
    attn_gain,
    query_proj,
    key_proj,
    value_proj,
    merge_proj,
    ffn_gain,
    gate_proj,
    up_proj,
    down_proj,
    out_grad,
):
    _, rows, model = layer_in.shape
    kv_width = key_proj.shape[1]
    kv_heads = kv_width // HD
    width = query_proj.shape[1]
    run = rows // 2
    positions = positions[0]
    grid = Grid(n_dp, n_ctx)
    order = grid.block_order(False)
    ring_order, ctx_order = grid.ring_order(), grid.ctx_order()
    places = grid.value_places()

    gains = jnp.stack([attn_gain, ffn_gain], -1)
    gains = jnp.concatenate([gains, jnp.zeros((gains.shape[0], WIDE - 2), BF16)], 1)
    packed = jnp.concatenate([query_proj, key_proj, value_proj, gains], 1)
    packed, down_proj, gate_proj, merge_proj = lax.optimization_barrier(
        (packed, down_proj, gate_proj, merge_proj)
    )
    first_chain = Chain(gather_weight(grid, packed))
    down_chain = Chain(gather_weight(grid, down_proj))
    gate_chain = Chain(gather_weight(grid, gate_proj))
    merge_chain = Chain(gather_weight(grid, merge_proj))
    up_chain = Chain(gather_ring(grid, up_proj))
    all_pos = lax.all_gather(positions[::run], "ctx", axis=0, tiled=True)
    cosine, sine = angles(positions)
    rows_in = layer_in.reshape(rows, model).astype(F32)
    normed_one, factor_one = normalize(rows_in)
    all_pos, factor_one, cosine = meet((all_pos, factor_one, cosine), first_chain, up_chain)
    first_weights = finish(first_chain)
    attn_all = first_weights[:, : width + 2 * kv_width]
    gain_one = first_weights[:, width + 2 * kv_width].astype(F32)
    gain_two = first_weights[:, width + 2 * kv_width + 1].astype(F32)

    first_in = (normed_one * gain_one).astype(BF16)
    first_in = meet(first_in, down_chain)
    raw = mm(first_in, attn_all, NN)
    queries, own_kv = rotated(raw, cosine, sine, kv_width)
    kv_chain = Chain(gather_keys(grid, own_kv))
    later = all_pos.reshape(n_ctx, 2)[ctx_order].reshape(2 * n_ctx, 1)
    later = later > jnp.repeat(positions[::run], run)[None, :]
    bias = jnp.where(later, MASKED, 0.0).astype(F32)
    bias = meet(bias, kv_chain, down_chain, up_chain)
    bias = meet(bias, kv_chain)
    bias = meet(bias, kv_chain, gate_chain)
    all_keys, all_values = finish(kv_chain)
    kt, vt = all_keys.T, all_values.T

    grad_rows = out_grad.reshape(rows, model)
    plan = (
        (),
        (down_chain, gate_chain, up_chain),
        (down_chain, merge_chain),
        (gate_chain, merge_chain, up_chain),
    )
    outs, log_sums = [], []
    for group in range(kv_heads):
        out, log_sum = attend(group, places, bias, queries, all_keys, vt)
        queries, out, grad_rows = meet((queries, out, grad_rows), *plan[group % 4])
        if group == 2:
            down_all = finish(down_chain)
            grad_hidden = mm(grad_rows, down_all, NT)
            queries, grad_hidden = lax.optimization_barrier((queries, grad_hidden))
        outs.append(out)
        log_sums.append(log_sum)
    mixed = jnp.concatenate([out.astype(BF16) for out in outs], 1)
    mixed = meet(mixed, gate_chain, merge_chain)
    gate_all, merge_all = finish(gate_chain), finish(merge_chain)
    middle = rows_in + mm(mixed, merge_all, NN)
    normed_two, factor_two = normalize(middle)
    second_in = (normed_two * gain_two).astype(BF16)
    second_in = meet(second_in, up_chain)
    gate = mm(second_in, gate_all, NN)
    up_all = finish(up_chain)
    lift = mm(second_in, up_all, NN)
    sigma = jax.nn.sigmoid(gate)
    activated = gate * sigma
    hidden = (activated * lift).astype(BF16)
    grad_gate = (grad_hidden * lift * sigma * (1.0 + gate * (1.0 - sigma))).astype(BF16)
    grad_lift = (grad_hidden * activated).astype(BF16)
    hidden, grad_gate, grad_lift = lax.optimization_barrier((hidden, grad_gate, grad_lift))
    second_turned = turned(second_in, order)
    gate_sum = Chain(reduce_term(grid, second_turned, grad_gate))
    up_sum = Chain(reduce_term(grid, second_turned, grad_lift))
    down_sum = Chain(reduce_ring(grid, turned(hidden, ring_order), grad_rows))
    grad_second = mm(grad_gate, gate_all, NT)
    grad_second, grad_lift = meet((grad_second, grad_lift), gate_sum)
    grad_second = grad_second + mm(grad_lift, up_all, NT)
    grad_norm_two, gain_two_term = norm_back(grad_second, normed_two, factor_two, gain_two)
    grad_middle = grad_rows.astype(F32) + grad_norm_two
    grad_branch = grad_middle.astype(BF16)
    grad_mixed = mm(grad_branch, merge_all, NT).astype(BF16)
    grad_mixed, grad_branch = meet((grad_mixed, grad_branch), down_sum, up_sum)
    first_turned = turned(first_in, order)
    mixed_turned = turned(mixed, order)

    dqs, dkvs = [], []
    for group in range(kv_heads):
        dq, dkv = attend_back(
            group, places, bias, log_sums[group], outs[group], queries, grad_mixed,
            all_keys, all_values, kt,
        )
        dqs.append(dq)
        dkvs.append(dkv)
        if group == kv_heads - 4:
            grad_mixed, dkv = meet((grad_mixed, dkv), gate_sum, down_sum)
        elif group == kv_heads - 3:
            grad_mixed, dkv, grad_branch = meet((grad_mixed, dkv, grad_branch), gate_sum, up_sum)
            merge_sum = Chain(reduce_term(grid, mixed_turned, grad_branch))
        elif group == kv_heads - 2:
            grad_mixed, dkvs = meet((grad_mixed, dkvs), up_sum, merge_sum, gate_sum)
            keys_sum = Chain(reduce_keys(grid, jnp.concatenate(dkvs, 1)))
    dqs, dkv, hidden = meet((dqs, dkv, hidden), merge_sum, keys_sum, up_sum)
    last_keys = Chain(reduce_keys(grid, dkv))
    query_grads = unrotated(unrotate_queries_kernel, dqs, cosine, sine)
    query_sum = Chain(reduce_term(grid, first_turned, query_grads))
    grad_first = mm(query_grads, attn_all[:, :width], NT)
    grad_first, hidden = meet(
        (grad_first, hidden), last_keys, keys_sum, query_sum, merge_sum, down_sum
    )
    result = middle + mm(hidden, down_all, NN)
    layer_out = result.astype(BF16).reshape(layer_in.shape)
    grad_first = meet(grad_first, last_keys, keys_sum)
    grad_first, layer_out = meet((grad_first, layer_out), last_keys, query_sum)
    wide = finish(keys_sum)
    dkv_parts = [wide[:, at : at + WIDE] for at in range(0, wide.shape[1], WIDE)]
    dkv_parts.append(finish(last_keys))
    kv_grads = unrotated(unrotate_keys_kernel, dkv_parts, cosine, sine)
    grad_first = grad_first + mm(kv_grads, attn_all[:, width:], NT)
    grad_norm_one, gain_one_term = norm_back(grad_first, normed_one, factor_one, gain_one)
    gain_terms = jnp.stack([gain_one_term, gain_two_term], 0)
    gain_terms = jnp.concatenate([gain_terms, jnp.zeros((WIDE - 2, model), F32)], 0)
    gain_columns = turned(gain_terms.astype(BF16), order)
    last = Chain(reduce_term(grid, first_turned, kv_grads, gain_columns))
    input_grad = (grad_middle + grad_norm_one).astype(BF16).reshape(layer_in.shape)
    input_grad = meet(input_grad, last, query_sum)
    input_grad = meet(input_grad, last, down_sum)
    input_grad = meet(input_grad, last, down_sum)
    query_share, last_share = finish(query_sum), finish(last)
    merge_share, gate_share = finish(merge_sum), finish(gate_sum)
    up_share, down_share = finish(up_sum), finish(down_sum)
    return (
        layer_out,
        input_grad,
        last_share[:, 2 * kv_width],
        query_share,
        last_share[:, :kv_width],
        last_share[:, kv_width : 2 * kv_width],
        merge_share,
        last_share[:, 2 * kv_width + 1],
        gate_share,
        up_share,
        down_share,
    )


def solution(mesh):
    acts = P("dp", "ctx", None)
    rows = P(BOTH, None)
    flat = P(BOTH)
    return jax.shard_map(
        functools.partial(body, mesh.shape["dp"], mesh.shape["ctx"]),
        mesh=mesh,
        in_specs=(acts, P("dp", "ctx"), flat, rows, rows, rows, rows, flat, rows, rows, rows, acts),
        out_specs=(acts, acts, flat, rows, rows, rows, rows, flat, rows, rows, rows),
        check_vma=False,
    )
```

```python
import functools

import jax
import jax.numpy as jnp
import numpy as np
from jax import lax
from jax.experimental import pallas as pl
from jax.experimental.pallas import tpu as pltpu
from jax.sharding import PartitionSpec as P

HD = 64
EPS = 1e-05
WIDE = 128
MASKED = -1e30
SCALE = HD**-0.5
LOG2E = 1.4426950408889634
TO_LOG2 = SCALE * LOG2E
BRIEF = pl.CostEstimate(flops=1 << 20, bytes_accessed=1 << 16, transcendentals=0)
F32 = jnp.float32
BF16 = jnp.bfloat16
NT = (((1,), (1,)), ((), ()))
NN = (((1,), (0,)), ((), ()))


def mm(left, right, dims):
    return lax.dot_general(left, right, dims, preferred_element_type=F32)


def same_run_later(keys, rows):
    run = rows // 2
    key = lax.broadcasted_iota(jnp.int32, (keys, rows), 0)
    query = lax.broadcasted_iota(jnp.int32, (keys, rows), 1)
    return (key > query) & ((key // run) == (query // run))


def split_heads(pair_ref, which, low_ref, high_ref):
    both = pair_ref[...]
    turned = pltpu.roll(both.astype(F32), HD, 1).astype(BF16)
    lane = lax.broadcasted_iota(jnp.int32, both.shape, 1)
    zero = jnp.zeros_like(both)
    first, second = (both, turned) if which == 0 else (turned, both)
    low_ref[...] = jnp.where(lane < HD, first, zero)
    high_ref[...] = jnp.where(lane < HD, zero, second)


def biased(scores, bias_ref, block, rows):
    run = rows // 2
    start = pl.multiple_of(block * rows, rows)
    parts = [
        scores[i * run : (i + 1) * run] + bias_ref[pl.ds(block * 2 + i, 1), :]
        for i in range(2)
    ]
    return jnp.concatenate(parts, 0)


def attend_kernel(
    bias_ref, q_ref, kp_ref, vt_ref, o_ref, lse_ref, low, high, vx, turned, *, which, places
):
    rows, width = q_ref.shape
    length = kp_ref.shape[0]
    blocks = length // rows
    split_heads(kp_ref, which, low, high)
    vx[:HD, :] = vt_ref[...]
    top_row = lax.broadcasted_iota(jnp.int32, (16, length), 0) == 0
    vx[HD:, :] = top_row.astype(F32).astype(BF16)

    def scores(key, pair, block):
        start = pl.multiple_of(block * rows, rows)
        column = pl.multiple_of(pair * WIDE, WIDE)
        s = mm(key[pl.ds(start, rows), :], q_ref[:, pl.ds(column, WIDE)], NT) * TO_LOG2
        return biased(s, bias_ref, block, rows)

    def weigh(probs, block):
        start = places[block] * rows
        return mm(vx[:, start : start + rows], probs.astype(BF16), NN)

    def one_pair(pair, _):
        blocked = same_run_later(rows, rows)
        state = []
        for key in (low, high):
            s = jnp.where(blocked, MASKED, scores(key, pair, 0))
            top = jnp.max(s, 0, keepdims=True)
            state.append((top, weigh(jnp.exp2(s - top), 0)))

        def step(block, state):
            raw = [scores(key, pair, block) for key in (low, high)]
            result = []
            for (top, total), s in zip(state, raw):
                new_top = jnp.maximum(top, jnp.max(s, 0, keepdims=True))
                probs = jnp.exp2(s - new_top)
                result.append((new_top, total * jnp.exp2(top - new_top) + weigh(probs, block)))
            return result

        for block in range(1, blocks):
            state = step(block, state)
        for i, (top, total) in enumerate(state):
            weight_sum = total[HD : HD + 1, :]
            turned[i * HD : (i + 1) * HD, :] = total[:HD] / weight_sum
            lse_ref[pl.ds(pair * 2 + i, 1), :] = top + jnp.log2(weight_sum)
        column = pl.multiple_of(pair * WIDE, WIDE)
        o_ref[:, pl.ds(column, WIDE)] = turned[...].T
        return 0

    lax.fori_loop(0, width // WIDE, one_pair, 0)


def attend(group, places, bias, q, keys, vt):
    rows, width = q.shape
    length = keys.shape[0]
    kv_heads = vt.shape[0] // HD
    mine = width // kv_heads
    heads = mine // HD
    return pl.pallas_call(
        functools.partial(attend_kernel, which=group % 2, places=places),
        grid=(1,),
        out_shape=(
            jax.ShapeDtypeStruct((rows, mine), F32),
            jax.ShapeDtypeStruct((heads, rows), F32),
        ),
        in_specs=[
            pl.BlockSpec(bias.shape, lambda i: (0, 0)),
            pl.BlockSpec((rows, mine), lambda i: (0, group)),
            pl.BlockSpec((length, WIDE), lambda i: (0, group // 2)),
            pl.BlockSpec((HD, length), lambda i: (group, 0)),
        ],
        out_specs=(
            pl.BlockSpec((rows, mine), lambda i: (0, 0)),
            pl.BlockSpec((heads, rows), lambda i: (0, 0)),
        ),
        scratch_shapes=[
            pltpu.VMEM((length, WIDE), BF16),
            pltpu.VMEM((length, WIDE), BF16),
            pltpu.VMEM((HD + 16, length), BF16),
            pltpu.VMEM((WIDE, rows), F32),
        ],
        compiler_params=pltpu.CompilerParams(vmem_limit_bytes=40 << 20),
        cost_estimate=BRIEF,
        name="attend",
    )(bias, q, keys, vt)


def attend_back_kernel(
    place_ref, bias_ref, lse_ref, o_ref, q_ref, g_ref, kp_ref, vp_ref, kt_ref,
    dq_ref, dkv_ref, k_low, k_high, v_low, v_high, dqt, delta_ref, *, which, unroll
):
    rows, width = q_ref.shape
    length = kp_ref.shape[0]
    blocks = length // rows
    pairs = width // WIDE
    split_heads(kp_ref, which, k_low, k_high)
    split_heads(vp_ref, which, v_low, v_high)
    row = lax.broadcasted_iota(jnp.int32, (16, WIDE), 0)
    lane = lax.broadcasted_iota(jnp.int32, (16, WIDE), 1)
    chosen = (row == lane // HD).astype(F32).astype(BF16)
    for pair in range(pairs):
        column = pl.ds(pair * WIDE, WIDE)
        product = g_ref[:, column].astype(F32) * o_ref[:, column]
        main = product.astype(BF16)
        rest = (product - main.astype(F32)).astype(BF16)
        both = mm(chosen, main, NT) + mm(chosen, rest, NT)
        delta_ref[2 * pair : 2 * pair + 2, :] = both[:2]

    def block(index, diagonal):
        start = pl.multiple_of(index * rows, rows)
        value_start = pl.multiple_of(place_ref[index] * rows, rows)

        def some_heads(i, sums):
            sums = list(sums)
            work = []
            for t in range(unroll):
                pair = i * unroll + t
                column = pl.multiple_of(pair * WIDE, WIDE)
                query = q_ref[:, pl.ds(column, WIDE)]
                grad = g_ref[:, pl.ds(column, WIDE)]
                for side, (key, value) in enumerate(((k_low, v_low), (k_high, v_high))):
                    head = pair * 2 + side
                    shift = -lse_ref[pl.ds(head, 1), :]
                    run = rows // 2
                    s = mm(key[pl.ds(start, rows), :], query, NT) * TO_LOG2
                    s = jnp.concatenate(
                        [
                            s[r * run : (r + 1) * run]
                            + (bias_ref[pl.ds(index * 2 + r, 1), :] + shift)
                            for r in range(2)
                        ],
                        0,
                    )
                    p = jnp.exp2(s)
                    if diagonal:
                        p = jnp.where(same_run_later(rows, rows), 0.0, p)
                    slope = mm(value[pl.ds(value_start, rows), :], grad, NT)
                    d = (p * (slope - delta_ref[pl.ds(head, 1), :])).astype(BF16)
                    work.append((side, pair, query, grad, p.astype(BF16), d))
            for side, pair, query, grad, p, d in work:
                sums[side] = sums[side] + mm(d, query, NN)
                sums[2 + side] = sums[2 + side] + mm(p, grad, NN)
                term = mm(kt_ref[:, pl.ds(start, rows)], d, NN)
                row = pl.multiple_of(pair * WIDE + side * HD, HD)
                if diagonal:
                    dqt[pl.ds(row, HD), :] = term
                else:
                    dqt[pl.ds(row, HD), :] += term
            return tuple(sums)

        zero = jnp.zeros((rows, WIDE), F32)
        sums = lax.fori_loop(0, pairs // unroll, some_heads, (zero,) * 4)
        lane = lax.broadcasted_iota(jnp.int32, (rows, WIDE), 1)
        key_sum = sums[0] + pltpu.roll(sums[1], HD, 1)
        value_sum = pltpu.roll(sums[2], HD, 1) + sums[3]
        dkv_ref[pl.ds(start, rows), :] = jnp.where(
            lane < HD, key_sum * SCALE, value_sum
        ).astype(BF16)

    block(0, True)

    def rest(j, _):
        block(j, False)
        return 0

    lax.fori_loop(1, blocks, rest, 0)
    for pair in range(pairs):
        dq_ref[:, pair * WIDE : (pair + 1) * WIDE] = (
            dqt[pair * WIDE : (pair + 1) * WIDE, :] * SCALE
        ).T


def attend_back(group, places, bias, lse, out, q, g, keys, values, kt, unroll=2):
    rows, width = q.shape
    length = keys.shape[0]
    kv_heads = kt.shape[0] // HD
    mine = width // kv_heads
    heads = mine // HD
    return pl.pallas_call(
        functools.partial(attend_back_kernel, which=group % 2, unroll=unroll),
        grid=(1,),
        out_shape=(
            jax.ShapeDtypeStruct((rows, mine), F32),
            jax.ShapeDtypeStruct((length, WIDE), BF16),
        ),
        in_specs=[
            pl.BlockSpec(memory_space=pltpu.SMEM),
            pl.BlockSpec(bias.shape, lambda i: (0, 0)),
            pl.BlockSpec((heads, rows), lambda i: (0, 0)),
            pl.BlockSpec((rows, mine), lambda i: (0, 0)),
            pl.BlockSpec((rows, mine), lambda i: (0, group)),
            pl.BlockSpec((rows, mine), lambda i: (0, group)),
            pl.BlockSpec((length, WIDE), lambda i: (0, group // 2)),
            pl.BlockSpec((length, WIDE), lambda i: (0, group // 2)),
            pl.BlockSpec((HD, length), lambda i: (group, 0)),
        ],
        out_specs=(
            pl.BlockSpec((rows, mine), lambda i: (0, 0)),
            pl.BlockSpec((length, WIDE), lambda i: (0, 0)),
        ),
        scratch_shapes=[pltpu.VMEM((length, WIDE), BF16)] * 4
        + [pltpu.VMEM((mine, rows), F32), pltpu.VMEM((heads, rows), F32)],
        compiler_params=pltpu.CompilerParams(vmem_limit_bytes=48 << 20),
        cost_estimate=BRIEF,
        name="attend_back",
    )(jnp.array(places, jnp.int32), bias, lse, out, q, g, keys, values, kt)


def turn_pairs(x, cosine, sine):
    lane = lax.broadcasted_iota(jnp.int32, x.shape, 1)
    swapped = jnp.where(
        lane % HD < HD // 2, pltpu.roll(x, WIDE - HD // 2, 1), pltpu.roll(x, HD // 2, 1)
    )
    return x * cosine + swapped * sine


def rotate_kernel(cos_ref, sin_ref, raw_ref, q_ref, kv_ref, *, kv_width):
    cosine, sine = cos_ref[...], sin_ref[...]
    width = q_ref.shape[1]
    for at in range(0, width, WIDE):
        q_ref[:, at : at + WIDE] = turn_pairs(raw_ref[:, at : at + WIDE], cosine, sine).astype(BF16)
    for at in range(0, kv_width, WIDE):
        column = slice(width + at, width + at + WIDE)
        kv_ref[:, at : at + WIDE] = turn_pairs(raw_ref[:, column], cosine, sine).astype(BF16)
    kv_ref[:, kv_width:] = raw_ref[:, width + kv_width :].astype(BF16)


def rotated(raw, cosine, sine, kv_width):
    rows, total = raw.shape
    return pl.pallas_call(
        functools.partial(rotate_kernel, kv_width=kv_width),
        out_shape=(
            jax.ShapeDtypeStruct((rows, total - 2 * kv_width), BF16),
            jax.ShapeDtypeStruct((rows, 2 * kv_width), BF16),
        ),
        in_specs=[pl.BlockSpec(memory_space=pltpu.VMEM)] * 3,
        out_specs=(pl.BlockSpec(memory_space=pltpu.VMEM),) * 2,
        compiler_params=pltpu.CompilerParams(vmem_limit_bytes=32 << 20),
        cost_estimate=pl.CostEstimate(
            flops=8 * raw.size, bytes_accessed=6 * raw.size, transcendentals=0
        ),
        name="rotated",
    )(cosine, sine, raw)


def unrotate_queries_kernel(cos_ref, sin_ref, *refs):
    cosine, sine = cos_ref[...], -sin_ref[...]
    out_ref = refs[-1]
    mine = refs[0].shape[1]
    for n, ref in enumerate(refs[:-1]):
        for at in range(0, mine, WIDE):
            turned = turn_pairs(ref[:, at : at + WIDE], cosine, sine)
            out_ref[:, n * mine + at : n * mine + at + WIDE] = turned.astype(BF16)


def unrotate_keys_kernel(cos_ref, sin_ref, *refs):
    cosine, sine = cos_ref[...], -sin_ref[...]
    out_ref = refs[-1]
    count = len(refs) - 1
    lane = lax.broadcasted_iota(jnp.int32, cosine.shape, 1)
    for i in range(count // 2):
        first, second = refs[2 * i][...].astype(F32), refs[2 * i + 1][...].astype(F32)
        keys = jnp.where(lane < HD, first, pltpu.roll(second, HD, 1))
        values = jnp.where(lane < HD, pltpu.roll(first, HD, 1), second)
        at = i * WIDE
        out_ref[:, at : at + WIDE] = turn_pairs(keys, cosine, sine).astype(BF16)
        at = count * HD + i * WIDE
        out_ref[:, at : at + WIDE] = values.astype(BF16)


def unrotated(kernel, parts, cosine, sine):
    rows, mine = parts[0].shape
    total = len(parts) * mine
    return pl.pallas_call(
        kernel,
        out_shape=jax.ShapeDtypeStruct((rows, total), BF16),
        in_specs=[pl.BlockSpec(memory_space=pltpu.VMEM)] * (2 + len(parts)),
        out_specs=pl.BlockSpec(memory_space=pltpu.VMEM),
        compiler_params=pltpu.CompilerParams(vmem_limit_bytes=32 << 20),
        cost_estimate=pl.CostEstimate(
            flops=8 * rows * total, bytes_accessed=6 * rows * total, transcendentals=0
        ),
        name="unrotated",
    )(cosine, sine, *parts)


BOTH = ("dp", "ctx")


class Grid:
    def __init__(self, n_dp, n_ctx):
        self.n_dp, self.n_a, self.n_b = n_dp, 2, n_ctx // 4
        self.n_ctx = n_ctx
        self.ring = [0, 1, 3, 2] if n_dp == 4 else list(range(n_dp))
        own = lax.axis_index("ctx").astype(jnp.int32)
        self.a = own // (2 * self.n_b)
        self.b = (own // 2) % self.n_b
        self.c = own % 2
        places = np.argsort(np.array(self.ring)).astype(np.int32)
        self.d = jnp.asarray(places)[lax.axis_index("dp")]

    def size(self, axis):
        return {"a": self.n_a, "b": self.n_b, "c": 2, "d": self.n_dp}[axis]

    def next(self, values, axis):
        if axis == "d":
            around = self.ring[1:] + self.ring[:1]
            return lax.ppermute(values, "dp", list(zip(self.ring, around)))
        pairs = []
        for i in range(self.n_ctx):
            a, b, c = i // (2 * self.n_b), (i // 2) % self.n_b, i % 2
            if axis == "a":
                a = (a + 1) % self.n_a
            elif axis == "b":
                b = (b + 1) % self.n_b
            else:
                c = 1 - c
            pairs.append((i, (a * self.n_b + b) * 2 + c))
        return lax.ppermute(values, "ctx", pairs)

    def natural(self, rows):
        rows = np.array(rows, np.int32)
        a = (self.a - rows[:, 2]) % self.n_a
        b = (self.b - rows[:, 3]) % self.n_b
        c = (self.c - rows[:, 0]) % 2
        return ((rows[:, 1] * self.n_a + a) * self.n_b + b) * 2 + c

    def block_order(self, around):
        half = self.n_dp // 2
        rows, hops = [], []
        for core in range(2):
            for h, (first, second) in enumerate(HALVES):
                for i in range(self.size(first)):
                    for j in range(self.size(second)):
                        for d in range(half):
                            near = {first: i, second: j}
                            at = h * half + d
                            rows.append((core, 0 if around else at, near["a"], near["b"]))
                            hops.append(at)
        return self.natural(rows) + (self.around(hops) * self.n_ctx if around else 0)

    def around(self, hops):
        ring = jnp.asarray(np.array(self.ring, np.int32))
        return ring[(self.d - np.array(hops, np.int32)) % self.n_dp]

    def ring_order(self):
        rows, hops = [], []
        for core in range(2):
            for d in range(self.n_dp):
                for b in range(self.n_b):
                    for a in range(self.n_a):
                        rows.append((core, 0, a, b))
                        hops.append(d)
        return self.natural(rows) + self.around(hops) * self.n_ctx

    def ctx_order(self):
        rows = [
            (c, 0, a, b) for c in range(2) for b in range(self.n_b) for a in range(self.n_a)
        ]
        return self.natural(rows)

    def value_places(self):
        cells = [(c, b, a) for c in range(2) for b in range(self.n_b) for a in range(self.n_a)]
        return tuple((c * self.n_a + a) * self.n_b + b for c, b, a in cells)


HALVES = (("b", "a"), ("a", "b"))


def turn_kernel(order_ref, x_ref, o_ref, held, *, blk):
    tokens, width = x_ref.shape
    for i in range(width // WIDE):
        held[i * WIDE : (i + 1) * WIDE, :] = x_ref[:, i * WIDE : (i + 1) * WIDE].T

    def move(i, _):
        source = pl.multiple_of(order_ref[i] * blk, blk)
        target = pl.multiple_of(i * blk, blk)
        o_ref[pl.ds(target, blk), :] = held[pl.ds(source, blk), :]
        return 0

    lax.fori_loop(0, width // blk, move, 0)


def turned(x, order):
    tokens, width = x.shape
    blk = width // order.shape[0]
    if blk % 16:
        blocks = jnp.take(x.T.reshape(order.shape[0], blk, tokens), order, axis=0)
        return blocks.reshape(width, tokens)
    return pl.pallas_call(
        functools.partial(turn_kernel, blk=blk),
        out_shape=jax.ShapeDtypeStruct((width, tokens), x.dtype),
        in_specs=[
            pl.BlockSpec(memory_space=pltpu.SMEM),
            pl.BlockSpec(memory_space=pltpu.VMEM),
        ],
        out_specs=pl.BlockSpec(memory_space=pltpu.VMEM),
        scratch_shapes=[pltpu.VMEM((width, tokens), x.dtype)],
        compiler_params=pltpu.CompilerParams(vmem_limit_bytes=32 << 20),
        cost_estimate=pl.CostEstimate(flops=0, bytes_accessed=4 * x.size, transcendentals=0),
        name="turned",
    )(order, x)


def reduce_term(grid, left, right, extra=None, around=False):
    rows = left.shape[0]
    mine = rows // 2

    def term(start, size):
        part = mm(left[start : start + size], right, NN)
        if extra is not None:
            part = jnp.concatenate([part, extra[start : start + size].astype(F32)], 1)
        return part

    (arrived,) = yield [grid.next(term(mine, mine).astype(BF16), "c")]
    held = []
    for h, axes in enumerate(HALVES):
        start = h * (mine // 2)
        count = grid.size(axes[0])
        size = mine // 2 // count
        held.append(
            [
                (term(at, size) + arrived[at : at + size].astype(F32)).astype(BF16)
                for at in range(start, start + count * size, size)
            ]
        )
    for step in range(2):
        totals = [None, None]
        counts = [grid.size(axes[step]) for axes in HALVES]
        for k in range(1, max(counts)):
            live = [h for h in range(2) if k < counts[h]]
            sent = [
                grid.next(held[h][1] if k == 1 else totals[h], HALVES[h][step]) for h in live
            ]
            came = yield sent
            for h, part in zip(live, came):
                own = held[h][(k + 1) % counts[h]]
                totals[h] = (part.astype(F32) + own.astype(F32)).astype(BF16)
        if step == 0:
            held = []
            for h, total in enumerate(totals):
                count = grid.size(HALVES[h][1])
                size = total.shape[0] // count
                held.append([total[j * size : (j + 1) * size] for j in range(count)])
    if not around:
        joined = jnp.concatenate(totals, 0)
        (share,) = yield [lax.psum_scatter(joined, "dp", scatter_dimension=0, tiled=True)]
        return share.astype(F32)
    half = grid.n_dp // 2
    size = totals[0].shape[0] // half
    held = [t[at : at + size] for t in totals for at in range(0, half * size, size)]
    total = held[1]
    for k in range(1, grid.n_dp):
        (came,) = yield [grid.next(total, "d")]
        total = came.astype(F32) + held[(k + 1) % grid.n_dp].astype(F32)
        total = total if k == grid.n_dp - 1 else total.astype(BF16)
    return total


def place_kernel(order_ref, *refs, sources, slots):
    pieces = refs[: -(3 + 1)]
    out_ref, held, in_sem, out_sem = refs[-4:]
    count = len(sources)

    def fetch(i):
        piece, place = sources[i]
        return pltpu.make_async_copy(
            pieces[piece].at[place], held.at[i % slots], in_sem.at[i % slots]
        )

    def store(i):
        return pltpu.make_async_copy(
            held.at[i % slots], out_ref.at[order_ref[i]], out_sem.at[i % slots]
        )

    ahead = slots // 2
    for i in range(min(ahead, count)):
        fetch(i).start()
    for i in range(count):
        fetch(i).wait()
        store(i).start()
        later = i + ahead
        if later < count:
            if later >= slots:
                store(later - slots).wait()
            fetch(later).start()
    for i in range(max(0, count - slots), count):
        store(i).wait()


def placed(order, pieces):
    blk, width = pieces[0].shape[-2:]
    flat = [p.reshape((-1, blk, width)) for p in pieces]
    sources = [(n, j) for n, p in enumerate(flat) for j in range(p.shape[0])]
    slots = 8
    whole = pl.pallas_call(
        functools.partial(place_kernel, sources=sources, slots=slots),
        out_shape=jax.ShapeDtypeStruct((len(sources), blk, width), flat[0].dtype),
        in_specs=[pl.BlockSpec(memory_space=pltpu.SMEM)]
        + [pl.BlockSpec(memory_space=pl.ANY)] * len(flat),
        out_specs=pl.BlockSpec(memory_space=pl.ANY),
        scratch_shapes=[
            pltpu.VMEM((slots, blk, width), flat[0].dtype),
            pltpu.SemaphoreType.DMA((slots,)),
            pltpu.SemaphoreType.DMA((slots,)),
        ],
        compiler_params=pltpu.CompilerParams(vmem_limit_bytes=16 << 20),
        cost_estimate=pl.CostEstimate(
            flops=0, bytes_accessed=4 * len(sources) * blk * width, transcendentals=0
        ),
        name="placed",
    )(order, *flat)
    return whole.reshape(len(sources) * blk, width)


def gather_weight(grid, weight, around=False):
    half = grid.n_dp // 2
    if around:
        column = [weight]
        for _ in range(grid.n_dp - 1):
            (came,) = yield [grid.next(column[-1], "d")]
            column.append(came)
        parts = [jnp.stack(column[:half]), jnp.stack(column[half:])]
    else:
        (column,) = yield [lax.all_gather(weight, "dp", axis=0)]
        parts = [column[:half], column[half:]]
    steps = [[parts[0]], [parts[1]]]
    for stage in (1, 0):
        counts = [grid.size(axes[stage]) for axes in HALVES]
        for k in range(1, max(counts)):
            live = [h for h in range(2) if k < counts[h]]
            came = yield [grid.next(steps[h][-1], HALVES[h][stage]) for h in live]
            for h, part in zip(live, came):
                steps[h].append(part)
        if stage == 1:
            steps = [[jnp.stack(s)] for s in steps]
    near = jnp.concatenate([p.reshape((-1,) + p.shape[-2:]) for p in steps[0] + steps[1]], 0)
    (far,) = yield [grid.next(near, "c")]
    return placed(grid.block_order(around), [near, far])


def gather_ring(grid, weight):
    part = weight
    for axis in ("a", "b"):
        steps = [part]
        for _ in range(grid.size(axis) - 1):
            (came,) = yield [grid.next(steps[-1], axis)]
            steps.append(came)
        part = jnp.stack(steps)
    near, far = [part], []
    waiting = [part]
    for k in range(grid.n_dp - 1):
        sent = [grid.next(near[-1], "d")]
        early = k == grid.n_dp - 2
        if early:
            sent.append(grid.next(jnp.stack(waiting[:-1]), "c"))
            waiting = waiting[-1:]
        came = yield sent
        if early:
            far.append(came[1])
        near.append(came[0])
        waiting.append(came[0])
    (other,) = yield [grid.next(jnp.stack(waiting), "c")]
    return placed(grid.ring_order(), near + far + [other])


def reduce_ring(grid, left, right):
    mine = left.shape[0] // 2
    (arrived,) = yield [grid.next(mm(left[mine:], right, NN).astype(BF16), "c")]
    size = mine // grid.n_dp
    held = [
        (mm(left[at : at + size], right, NN) + arrived[at : at + size].astype(F32)).astype(BF16)
        for at in range(0, mine, size)
    ]
    for axis in ("d", "b", "a"):
        count = grid.size(axis)
        total = held[1]
        for k in range(1, count):
            (came,) = yield [grid.next(total, axis)]
            total = (came.astype(F32) + held[(k + 1) % count].astype(F32)).astype(BF16)
        following = {"d": grid.n_b, "b": grid.n_a, "a": 1}[axis]
        size = total.shape[0] // following
        held = [total[at : at + size] for at in range(0, total.shape[0], size)]
    return held[0].astype(F32)


def gather_keys(grid, own):
    width = own.shape[1] // 2
    steps = [[own[:, :width]], [own[:, width:]]]
    for stage in (1, 0):
        counts = [grid.size(axes[stage]) for axes in HALVES]
        for k in range(1, max(counts)):
            live = [h for h in range(2) if k < counts[h]]
            came = yield [grid.next(steps[h][-1], HALVES[h][stage]) for h in live]
            for h, part in zip(live, came):
                steps[h].append(part)
        steps = [[jnp.stack(s)] for s in steps]
    near = [s[0] for s in steps]
    far = yield [grid.next(part, "c") for part in near]
    return tuple(
        jnp.stack([one, two]).reshape(-1, width) for one, two in zip(near, far)
    )


def reduce_keys(grid, terms):
    mine = terms.shape[0] // 2
    (came,) = yield [grid.next(terms[mine:], "c")]
    total = (terms[:mine].astype(F32) + came.astype(F32)).astype(BF16)
    for axis in ("b", "a"):
        count = grid.size(axis)
        size = total.shape[0] // count
        held = [total[at : at + size] for at in range(0, count * size, size)]
        total = held[1]
        for k in range(1, count):
            (came,) = yield [grid.next(total, axis)]
            total = (came.astype(F32) + held[(k + 1) % count].astype(F32)).astype(BF16)
    return total


class Chain:
    def __init__(self, generator):
        self.generator, self.done, self.result = generator, False, None
        self.flight = next(generator)

    def advance(self, arrived):
        try:
            self.flight = self.generator.send(arrived)
        except StopIteration as stop:
            self.done, self.result, self.flight = True, stop.value, []


def meet(main, *chains):
    chains = [c for c in chains if not c.done]
    main, flights = lax.optimization_barrier((main, [list(c.flight) for c in chains]))
    for chain, flight in zip(chains, flights):
        chain.advance(flight)
    return main


def settle(main, *chains):
    main, flights = lax.optimization_barrier((main, [list(c.flight) for c in chains]))
    for chain, flight in zip(chains, flights):
        chain.flight = flight
    return main


def finish(chain):
    while not chain.done:
        chain.advance(chain.flight)
    return chain.result


def angles(positions):
    lane = jnp.arange(WIDE)
    freq = 10000.0 ** (-((lane % (HD // 2)).astype(F32) * 2.0 / HD))
    turn = positions.astype(F32)[:, None] * freq[None, :]
    sign = jnp.where(lane % HD < HD // 2, -1.0, 1.0)
    return jnp.cos(turn), jnp.sin(turn) * sign[None, :]


def normalize(rows):
    factor = lax.rsqrt(jnp.mean(rows * rows, -1, keepdims=True) + EPS)
    return (rows * factor, factor)


def norm_back(upstream, normed, factor, gain):
    scaled = upstream * gain
    inner = jnp.mean(scaled * normed, -1, keepdims=True)
    return (factor * (scaled - normed * inner), jnp.sum(upstream * normed, 0))


def body(
    n_dp,
    n_ctx,
    layer_in,
    positions,
    attn_gain,
    query_proj,
    key_proj,
    value_proj,
    merge_proj,
    ffn_gain,
    gate_proj,
    up_proj,
    down_proj,
    out_grad,
):
    _, rows, model = layer_in.shape
    kv_width = key_proj.shape[1]
    kv_heads = kv_width // HD
    width = query_proj.shape[1]
    run = rows // 2
    positions = positions[0]
    grid = Grid(n_dp, n_ctx)
    order = grid.block_order(False)
    ring_order, ctx_order = grid.ring_order(), grid.ctx_order()
    places = grid.value_places()

    gains = jnp.stack([attn_gain, ffn_gain], -1)
    gains = jnp.concatenate([gains, jnp.zeros((gains.shape[0], WIDE - 2), BF16)], 1)
    packed = jnp.concatenate([query_proj, key_proj, value_proj, gains], 1)
    packed, down_proj, gate_proj, merge_proj = lax.optimization_barrier(
        (packed, down_proj, gate_proj, merge_proj)
    )
    first_chain = Chain(gather_weight(grid, packed))
    down_chain = Chain(gather_weight(grid, down_proj))
    gate_chain = Chain(gather_weight(grid, gate_proj))
    merge_chain = Chain(gather_weight(grid, merge_proj))
    up_chain = Chain(gather_ring(grid, up_proj))
    all_pos = lax.all_gather(positions[::run], "ctx", axis=0, tiled=True)
    cosine, sine = angles(positions)
    rows_in = layer_in.reshape(rows, model).astype(F32)
    normed_one, factor_one = normalize(rows_in)
    all_pos, factor_one, cosine = meet((all_pos, factor_one, cosine), first_chain, up_chain)
    factor_one = meet(factor_one, first_chain, up_chain)
    first_weights = finish(first_chain)
    attn_all = first_weights[:, : width + 2 * kv_width]
    gain_one = first_weights[:, width + 2 * kv_width].astype(F32)
    gain_two = first_weights[:, width + 2 * kv_width + 1].astype(F32)

    first_in = (normed_one * gain_one).astype(BF16)
    first_in = meet(first_in, down_chain)
    raw = mm(first_in, attn_all, NN)
    queries, own_kv = rotated(raw, cosine, sine, kv_width)
    kv_chain = Chain(gather_keys(grid, own_kv))
    later = all_pos.reshape(n_ctx, 2)[ctx_order].reshape(2 * n_ctx, 1)
    later = later > jnp.repeat(positions[::run], run)[None, :]
    bias = jnp.where(later, MASKED, 0.0).astype(F32)
    bias = meet(bias, kv_chain, down_chain, up_chain)
    bias = meet(bias, kv_chain)
    bias = meet(bias, kv_chain, gate_chain)
    all_keys, all_values = finish(kv_chain)
    kt, vt = all_keys.T, all_values.T

    grad_rows = out_grad.reshape(rows, model)
    plan = (
        (),
        (down_chain, merge_chain, up_chain),
        (down_chain, merge_chain, gate_chain),
        (gate_chain, merge_chain, up_chain),
    )
    outs, log_sums = [], []
    for group in range(kv_heads):
        out, log_sum = attend(group, places, bias, queries, all_keys, vt)
        if group < 2:
            out = settle(out, (merge_chain, gate_chain)[group])
        queries, out, grad_rows = meet((queries, out, grad_rows), *plan[group % 4])
        if group == 2:
            down_all = finish(down_chain)
            grad_hidden = mm(grad_rows, down_all, NT)
            queries, grad_hidden = lax.optimization_barrier((queries, grad_hidden))
        outs.append(out)
        log_sums.append(log_sum)
    mixed = jnp.concatenate([out.astype(BF16) for out in outs], 1)
    mixed = meet(mixed, merge_chain)
    merge_all = finish(merge_chain)
    middle = rows_in + mm(mixed, merge_all, NN)
    normed_two, factor_two = normalize(middle)
    second_in = (normed_two * gain_two).astype(BF16)
    second_in = meet(second_in, gate_chain, up_chain)
    gate_all = finish(gate_chain)
    gate = mm(second_in, gate_all, NN)
    up_all = finish(up_chain)
    lift = mm(second_in, up_all, NN)
    sigma = jax.nn.sigmoid(gate)
    activated = gate * sigma
    hidden = (activated * lift).astype(BF16)
    grad_gate = (grad_hidden * lift * sigma * (1.0 + gate * (1.0 - sigma))).astype(BF16)
    grad_lift = (grad_hidden * activated).astype(BF16)
    hidden, grad_gate, grad_lift = lax.optimization_barrier((hidden, grad_gate, grad_lift))
    second_turned = turned(second_in, order)
    gate_sum = Chain(reduce_term(grid, second_turned, grad_gate))
    up_sum = Chain(reduce_term(grid, second_turned, grad_lift))
    down_sum = Chain(reduce_ring(grid, turned(hidden, ring_order), grad_rows))
    grad_second = mm(grad_gate, gate_all, NT)
    grad_second, grad_lift = meet((grad_second, grad_lift), gate_sum)
    grad_second = grad_second + mm(grad_lift, up_all, NT)
    grad_norm_two, gain_two_term = norm_back(grad_second, normed_two, factor_two, gain_two)
    grad_middle = grad_rows.astype(F32) + grad_norm_two
    grad_branch = grad_middle.astype(BF16)
    grad_mixed = mm(grad_branch, merge_all, NT).astype(BF16)
    grad_mixed, grad_branch = meet((grad_mixed, grad_branch), down_sum, up_sum)
    first_turned = turned(first_in, order)
    mixed_turned = turned(mixed, order)

    dqs, dkvs = [], []
    for group in range(kv_heads):
        dq, dkv = attend_back(
            group, places, bias, log_sums[group], outs[group], queries, grad_mixed,
            all_keys, all_values, kt,
        )
        dqs.append(dq)
        dkvs.append(dkv)
        if group == kv_heads - 4:
            grad_mixed, dkv = meet((grad_mixed, dkv), gate_sum, down_sum)
        elif group == kv_heads - 3:
            grad_mixed, dkv, grad_branch = meet(
                (grad_mixed, dkv, grad_branch), gate_sum, up_sum, down_sum
            )
            merge_sum = Chain(reduce_term(grid, mixed_turned, grad_branch))
        elif group == kv_heads - 2:
            grad_mixed, dkvs = meet((grad_mixed, dkvs), up_sum, merge_sum, down_sum)
            keys_sum = Chain(reduce_keys(grid, jnp.concatenate(dkvs, 1)))
    dqs, dkv, hidden = meet((dqs, dkv, hidden), merge_sum, keys_sum, gate_sum, down_sum)
    last_keys = Chain(reduce_keys(grid, dkv))
    query_grads = unrotated(unrotate_queries_kernel, dqs, cosine, sine)
    grad_first = mm(query_grads, attn_all[:, :width], NT)
    grad_first, query_grads, hidden = meet(
        (grad_first, query_grads, hidden), last_keys, keys_sum, merge_sum, down_sum
    )
    query_sum = Chain(reduce_term(grid, first_turned, query_grads))
    result = middle + mm(hidden, down_all, NN)
    layer_out = result.astype(BF16).reshape(layer_in.shape)
    grad_first, layer_out = meet((grad_first, layer_out), last_keys, keys_sum, query_sum)
    grad_first = meet(grad_first, last_keys)
    wide = finish(keys_sum)
    dkv_parts = [wide[:, at : at + WIDE] for at in range(0, wide.shape[1], WIDE)]
    dkv_parts.append(finish(last_keys))
    kv_grads = unrotated(unrotate_keys_kernel, dkv_parts, cosine, sine)
    grad_first = grad_first + mm(kv_grads, attn_all[:, width:], NT)
    grad_norm_one, gain_one_term = norm_back(grad_first, normed_one, factor_one, gain_one)
    gain_terms = jnp.stack([gain_one_term, gain_two_term], 0)
    gain_terms = jnp.concatenate([gain_terms, jnp.zeros((WIDE - 2, model), F32)], 0)
    gain_columns = turned(gain_terms.astype(BF16), order)
    last = Chain(reduce_term(grid, first_turned, kv_grads, gain_columns))
    input_grad = (grad_middle + grad_norm_one).astype(BF16).reshape(layer_in.shape)
    input_grad = meet(input_grad, last, query_sum, up_sum)
    input_grad = meet(input_grad, last, query_sum, merge_sum)
    input_grad = meet(input_grad, last)
    query_share, last_share = finish(query_sum), finish(last)
    merge_share, gate_share = finish(merge_sum), finish(gate_sum)
    up_share, down_share = finish(up_sum), finish(down_sum)
    return (
        layer_out,
        input_grad,
        last_share[:, 2 * kv_width],
        query_share,
        last_share[:, :kv_width],
        last_share[:, kv_width : 2 * kv_width],
        merge_share,
        last_share[:, 2 * kv_width + 1],
        gate_share,
        up_share,
        down_share,
    )


def solution(mesh):
    acts = P("dp", "ctx", None)
    rows = P(BOTH, None)
    flat = P(BOTH)
    return jax.shard_map(
        functools.partial(body, mesh.shape["dp"], mesh.shape["ctx"]),
        mesh=mesh,
        in_specs=(acts, P("dp", "ctx"), flat, rows, rows, rows, rows, flat, rows, rows, rows, acts),
        out_specs=(acts, acts, flat, rows, rows, rows, rows, flat, rows, rows, rows),
        check_vma=False,
    )
```

```python
import functools

import jax
import jax.numpy as jnp
import numpy as np
from jax import lax
from jax.experimental import pallas as pl
from jax.experimental.pallas import tpu as pltpu
from jax.sharding import PartitionSpec as P

HD = 64
EPS = 1e-05
WIDE = 128
MASKED = -1e30
SCALE = HD**-0.5
LOG2E = 1.4426950408889634
TO_LOG2 = SCALE * LOG2E
BRIEF = pl.CostEstimate(flops=1 << 20, bytes_accessed=1 << 16, transcendentals=0)
F32 = jnp.float32
BF16 = jnp.bfloat16
NT = (((1,), (1,)), ((), ()))
NN = (((1,), (0,)), ((), ()))


def mm(left, right, dims):
    return lax.dot_general(left, right, dims, preferred_element_type=F32)


def same_run_later(keys, rows):
    run = rows // 2
    key = lax.broadcasted_iota(jnp.int32, (keys, rows), 0)
    query = lax.broadcasted_iota(jnp.int32, (keys, rows), 1)
    return (key > query) & ((key // run) == (query // run))


def split_heads(pair_ref, which, low_ref, high_ref):
    both = pair_ref[...]
    turned = pltpu.roll(both.astype(F32), HD, 1).astype(BF16)
    lane = lax.broadcasted_iota(jnp.int32, both.shape, 1)
    zero = jnp.zeros_like(both)
    first, second = (both, turned) if which == 0 else (turned, both)
    low_ref[...] = jnp.where(lane < HD, first, zero)
    high_ref[...] = jnp.where(lane < HD, zero, second)


def biased(scores, bias_ref, block, rows):
    run = rows // 2
    start = pl.multiple_of(block * rows, rows)
    parts = [
        scores[i * run : (i + 1) * run] + bias_ref[pl.ds(block * 2 + i, 1), :]
        for i in range(2)
    ]
    return jnp.concatenate(parts, 0)


def attend_kernel(
    bias_ref, q_ref, kp_ref, vt_ref, o_ref, lse_ref, low, high, vx, turned, *, which, places
):
    rows, width = q_ref.shape
    length = kp_ref.shape[0]
    blocks = length // rows
    split_heads(kp_ref, which, low, high)
    vx[:HD, :] = vt_ref[...]
    top_row = lax.broadcasted_iota(jnp.int32, (16, length), 0) == 0
    vx[HD:, :] = top_row.astype(F32).astype(BF16)

    def scores(key, pair, block):
        start = pl.multiple_of(block * rows, rows)
        column = pl.multiple_of(pair * WIDE, WIDE)
        s = mm(key[pl.ds(start, rows), :], q_ref[:, pl.ds(column, WIDE)], NT) * TO_LOG2
        return biased(s, bias_ref, block, rows)

    def weigh(probs, block):
        start = places[block] * rows
        return mm(vx[:, start : start + rows], probs.astype(BF16), NN)

    def one_pair(pair, _):
        blocked = same_run_later(rows, rows)
        state = []
        for key in (low, high):
            s = jnp.where(blocked, MASKED, scores(key, pair, 0))
            top = jnp.max(s, 0, keepdims=True)
            state.append((top, weigh(jnp.exp2(s - top), 0)))

        def step(block, state):
            raw = [scores(key, pair, block) for key in (low, high)]
            result = []
            for (top, total), s in zip(state, raw):
                new_top = jnp.maximum(top, jnp.max(s, 0, keepdims=True))
                probs = jnp.exp2(s - new_top)
                result.append((new_top, total * jnp.exp2(top - new_top) + weigh(probs, block)))
            return result

        for block in range(1, blocks):
            state = step(block, state)
        for i, (top, total) in enumerate(state):
            weight_sum = total[HD : HD + 1, :]
            turned[i * HD : (i + 1) * HD, :] = total[:HD] / weight_sum
            lse_ref[pl.ds(pair * 2 + i, 1), :] = top + jnp.log2(weight_sum)
        column = pl.multiple_of(pair * WIDE, WIDE)
        o_ref[:, pl.ds(column, WIDE)] = turned[...].T
        return 0

    lax.fori_loop(0, width // WIDE, one_pair, 0)


def attend(group, places, bias, q, keys, vt):
    rows, width = q.shape
    length = keys.shape[0]
    kv_heads = vt.shape[0] // HD
    mine = width // kv_heads
    heads = mine // HD
    return pl.pallas_call(
        functools.partial(attend_kernel, which=group % 2, places=places),
        grid=(1,),
        out_shape=(
            jax.ShapeDtypeStruct((rows, mine), F32),
            jax.ShapeDtypeStruct((heads, rows), F32),
        ),
        in_specs=[
            pl.BlockSpec(bias.shape, lambda i: (0, 0)),
            pl.BlockSpec((rows, mine), lambda i: (0, group)),
            pl.BlockSpec((length, WIDE), lambda i: (0, group // 2)),
            pl.BlockSpec((HD, length), lambda i: (group, 0)),
        ],
        out_specs=(
            pl.BlockSpec((rows, mine), lambda i: (0, 0)),
            pl.BlockSpec((heads, rows), lambda i: (0, 0)),
        ),
        scratch_shapes=[
            pltpu.VMEM((length, WIDE), BF16),
            pltpu.VMEM((length, WIDE), BF16),
            pltpu.VMEM((HD + 16, length), BF16),
            pltpu.VMEM((WIDE, rows), F32),
        ],
        compiler_params=pltpu.CompilerParams(vmem_limit_bytes=40 << 20),
        cost_estimate=BRIEF,
        name="attend",
    )(bias, q, keys, vt)


def attend_back_kernel(
    place_ref, bias_ref, lse_ref, o_ref, q_ref, g_ref, kp_ref, vp_ref, kt_ref,
    dq_ref, dkv_ref, k_low, k_high, v_low, v_high, dqt, delta_ref, *, which, unroll
):
    rows, width = q_ref.shape
    length = kp_ref.shape[0]
    blocks = length // rows
    pairs = width // WIDE
    split_heads(kp_ref, which, k_low, k_high)
    split_heads(vp_ref, which, v_low, v_high)
    row = lax.broadcasted_iota(jnp.int32, (16, WIDE), 0)
    lane = lax.broadcasted_iota(jnp.int32, (16, WIDE), 1)
    chosen = (row == lane // HD).astype(F32).astype(BF16)
    for pair in range(pairs):
        column = pl.ds(pair * WIDE, WIDE)
        product = g_ref[:, column].astype(F32) * o_ref[:, column]
        main = product.astype(BF16)
        rest = (product - main.astype(F32)).astype(BF16)
        both = mm(chosen, main, NT) + mm(chosen, rest, NT)
        delta_ref[2 * pair : 2 * pair + 2, :] = both[:2]

    def block(index, diagonal):
        start = pl.multiple_of(index * rows, rows)
        value_start = pl.multiple_of(place_ref[index] * rows, rows)

        def some_heads(i, sums):
            sums = list(sums)
            work = []
            for t in range(unroll):
                pair = i * unroll + t
                column = pl.multiple_of(pair * WIDE, WIDE)
                query = q_ref[:, pl.ds(column, WIDE)]
                grad = g_ref[:, pl.ds(column, WIDE)]
                for side, (key, value) in enumerate(((k_low, v_low), (k_high, v_high))):
                    head = pair * 2 + side
                    shift = -lse_ref[pl.ds(head, 1), :]
                    run = rows // 2
                    s = mm(key[pl.ds(start, rows), :], query, NT) * TO_LOG2
                    s = jnp.concatenate(
                        [
                            s[r * run : (r + 1) * run]
                            + (bias_ref[pl.ds(index * 2 + r, 1), :] + shift)
                            for r in range(2)
                        ],
                        0,
                    )
                    p = jnp.exp2(s)
                    if diagonal:
                        p = jnp.where(same_run_later(rows, rows), 0.0, p)
                    slope = mm(value[pl.ds(value_start, rows), :], grad, NT)
                    d = (p * (slope - delta_ref[pl.ds(head, 1), :])).astype(BF16)
                    work.append((side, pair, query, grad, p.astype(BF16), d))
            for side, pair, query, grad, p, d in work:
                sums[side] = sums[side] + mm(d, query, NN)
                sums[2 + side] = sums[2 + side] + mm(p, grad, NN)
                term = mm(kt_ref[:, pl.ds(start, rows)], d, NN)
                row = pl.multiple_of(pair * WIDE + side * HD, HD)
                if diagonal:
                    dqt[pl.ds(row, HD), :] = term
                else:
                    dqt[pl.ds(row, HD), :] += term
            return tuple(sums)

        zero = jnp.zeros((rows, WIDE), F32)
        sums = lax.fori_loop(0, pairs // unroll, some_heads, (zero,) * 4)
        lane = lax.broadcasted_iota(jnp.int32, (rows, WIDE), 1)
        key_sum = sums[0] + pltpu.roll(sums[1], HD, 1)
        value_sum = pltpu.roll(sums[2], HD, 1) + sums[3]
        dkv_ref[pl.ds(start, rows), :] = jnp.where(
            lane < HD, key_sum * SCALE, value_sum
        ).astype(BF16)

    block(0, True)

    def rest(j, _):
        block(j, False)
        return 0

    lax.fori_loop(1, blocks, rest, 0)
    for pair in range(pairs):
        dq_ref[:, pair * WIDE : (pair + 1) * WIDE] = (
            dqt[pair * WIDE : (pair + 1) * WIDE, :] * SCALE
        ).T


def attend_back(group, places, bias, lse, out, q, g, keys, values, kt, unroll=2):
    rows, width = q.shape
    length = keys.shape[0]
    kv_heads = kt.shape[0] // HD
    mine = width // kv_heads
    heads = mine // HD
    return pl.pallas_call(
        functools.partial(attend_back_kernel, which=group % 2, unroll=unroll),
        grid=(1,),
        out_shape=(
            jax.ShapeDtypeStruct((rows, mine), F32),
            jax.ShapeDtypeStruct((length, WIDE), BF16),
        ),
        in_specs=[
            pl.BlockSpec(memory_space=pltpu.SMEM),
            pl.BlockSpec(bias.shape, lambda i: (0, 0)),
            pl.BlockSpec((heads, rows), lambda i: (0, 0)),
            pl.BlockSpec((rows, mine), lambda i: (0, 0)),
            pl.BlockSpec((rows, mine), lambda i: (0, group)),
            pl.BlockSpec((rows, mine), lambda i: (0, group)),
            pl.BlockSpec((length, WIDE), lambda i: (0, group // 2)),
            pl.BlockSpec((length, WIDE), lambda i: (0, group // 2)),
            pl.BlockSpec((HD, length), lambda i: (group, 0)),
        ],
        out_specs=(
            pl.BlockSpec((rows, mine), lambda i: (0, 0)),
            pl.BlockSpec((length, WIDE), lambda i: (0, 0)),
        ),
        scratch_shapes=[pltpu.VMEM((length, WIDE), BF16)] * 4
        + [pltpu.VMEM((mine, rows), F32), pltpu.VMEM((heads, rows), F32)],
        compiler_params=pltpu.CompilerParams(vmem_limit_bytes=48 << 20),
        cost_estimate=BRIEF,
        name="attend_back",
    )(jnp.array(places, jnp.int32), bias, lse, out, q, g, keys, values, kt)


def turn_pairs(x, cosine, sine):
    lane = lax.broadcasted_iota(jnp.int32, x.shape, 1)
    swapped = jnp.where(
        lane % HD < HD // 2, pltpu.roll(x, WIDE - HD // 2, 1), pltpu.roll(x, HD // 2, 1)
    )
    return x * cosine + swapped * sine


def rotate_kernel(cos_ref, sin_ref, raw_ref, q_ref, kv_ref, *, kv_width):
    cosine, sine = cos_ref[...], sin_ref[...]
    width = q_ref.shape[1]
    for at in range(0, width, WIDE):
        q_ref[:, at : at + WIDE] = turn_pairs(raw_ref[:, at : at + WIDE], cosine, sine).astype(BF16)
    for at in range(0, kv_width, WIDE):
        column = slice(width + at, width + at + WIDE)
        kv_ref[:, at : at + WIDE] = turn_pairs(raw_ref[:, column], cosine, sine).astype(BF16)
    kv_ref[:, kv_width:] = raw_ref[:, width + kv_width :].astype(BF16)


def rotated(raw, cosine, sine, kv_width):
    rows, total = raw.shape
    return pl.pallas_call(
        functools.partial(rotate_kernel, kv_width=kv_width),
        out_shape=(
            jax.ShapeDtypeStruct((rows, total - 2 * kv_width), BF16),
            jax.ShapeDtypeStruct((rows, 2 * kv_width), BF16),
        ),
        in_specs=[pl.BlockSpec(memory_space=pltpu.VMEM)] * 3,
        out_specs=(pl.BlockSpec(memory_space=pltpu.VMEM),) * 2,
        compiler_params=pltpu.CompilerParams(vmem_limit_bytes=32 << 20),
        cost_estimate=pl.CostEstimate(
            flops=8 * raw.size, bytes_accessed=6 * raw.size, transcendentals=0
        ),
        name="rotated",
    )(cosine, sine, raw)


def unrotate_queries_kernel(cos_ref, sin_ref, *refs):
    cosine, sine = cos_ref[...], -sin_ref[...]
    out_ref = refs[-1]
    mine = refs[0].shape[1]
    for n, ref in enumerate(refs[:-1]):
        for at in range(0, mine, WIDE):
            turned = turn_pairs(ref[:, at : at + WIDE], cosine, sine)
            out_ref[:, n * mine + at : n * mine + at + WIDE] = turned.astype(BF16)


def unrotate_keys_kernel(cos_ref, sin_ref, *refs):
    cosine, sine = cos_ref[...], -sin_ref[...]
    out_ref = refs[-1]
    count = len(refs) - 1
    lane = lax.broadcasted_iota(jnp.int32, cosine.shape, 1)
    for i in range(count // 2):
        first, second = refs[2 * i][...].astype(F32), refs[2 * i + 1][...].astype(F32)
        keys = jnp.where(lane < HD, first, pltpu.roll(second, HD, 1))
        values = jnp.where(lane < HD, pltpu.roll(first, HD, 1), second)
        at = i * WIDE
        out_ref[:, at : at + WIDE] = turn_pairs(keys, cosine, sine).astype(BF16)
        at = count * HD + i * WIDE
        out_ref[:, at : at + WIDE] = values.astype(BF16)


def unrotated(kernel, parts, cosine, sine):
    rows, mine = parts[0].shape
    total = len(parts) * mine
    return pl.pallas_call(
        kernel,
        out_shape=jax.ShapeDtypeStruct((rows, total), BF16),
        in_specs=[pl.BlockSpec(memory_space=pltpu.VMEM)] * (2 + len(parts)),
        out_specs=pl.BlockSpec(memory_space=pltpu.VMEM),
        compiler_params=pltpu.CompilerParams(vmem_limit_bytes=32 << 20),
        cost_estimate=pl.CostEstimate(
            flops=8 * rows * total, bytes_accessed=6 * rows * total, transcendentals=0
        ),
        name="unrotated",
    )(cosine, sine, *parts)


BOTH = ("dp", "ctx")


class Grid:
    def __init__(self, n_dp, n_ctx):
        self.n_dp, self.n_a, self.n_b = n_dp, 2, n_ctx // 4
        self.n_ctx = n_ctx
        self.ring = [0, 1, 3, 2] if n_dp == 4 else list(range(n_dp))
        own = lax.axis_index("ctx").astype(jnp.int32)
        self.a = own // (2 * self.n_b)
        self.b = (own // 2) % self.n_b
        self.c = own % 2
        places = np.argsort(np.array(self.ring)).astype(np.int32)
        self.d = jnp.asarray(places)[lax.axis_index("dp")]

    def size(self, axis):
        return {"a": self.n_a, "b": self.n_b, "c": 2, "d": self.n_dp}[axis]

    def next(self, values, axis):
        if axis == "d":
            around = self.ring[1:] + self.ring[:1]
            return lax.ppermute(values, "dp", list(zip(self.ring, around)))
        pairs = []
        for i in range(self.n_ctx):
            a, b, c = i // (2 * self.n_b), (i // 2) % self.n_b, i % 2
            if axis == "a":
                a = (a + 1) % self.n_a
            elif axis == "b":
                b = (b + 1) % self.n_b
            else:
                c = 1 - c
            pairs.append((i, (a * self.n_b + b) * 2 + c))
        return lax.ppermute(values, "ctx", pairs)

    def natural(self, rows):
        rows = np.array(rows, np.int32)
        a = (self.a - rows[:, 2]) % self.n_a
        b = (self.b - rows[:, 3]) % self.n_b
        c = (self.c - rows[:, 0]) % 2
        return ((rows[:, 1] * self.n_a + a) * self.n_b + b) * 2 + c

    def block_order(self, around):
        half = self.n_dp // 2
        rows, hops = [], []
        for core in range(2):
            for h, (first, second) in enumerate(HALVES):
                for i in range(self.size(first)):
                    for j in range(self.size(second)):
                        for d in range(half):
                            near = {first: i, second: j}
                            at = h * half + d
                            rows.append((core, 0 if around else at, near["a"], near["b"]))
                            hops.append(at)
        return self.natural(rows) + (self.around(hops) * self.n_ctx if around else 0)

    def around(self, hops):
        ring = jnp.asarray(np.array(self.ring, np.int32))
        return ring[(self.d - np.array(hops, np.int32)) % self.n_dp]

    def ring_order(self):
        rows, hops = [], []
        for core in range(2):
            for d in range(self.n_dp):
                for b in range(self.n_b):
                    for a in range(self.n_a):
                        rows.append((core, 0, a, b))
                        hops.append(d)
        return self.natural(rows) + self.around(hops) * self.n_ctx

    def ctx_order(self):
        rows = [
            (c, 0, a, b) for c in range(2) for b in range(self.n_b) for a in range(self.n_a)
        ]
        return self.natural(rows)

    def value_places(self):
        cells = [(c, b, a) for c in range(2) for b in range(self.n_b) for a in range(self.n_a)]
        return tuple((c * self.n_a + a) * self.n_b + b for c, b, a in cells)


HALVES = (("b", "a"), ("a", "b"))


def turn_kernel(order_ref, x_ref, o_ref, held, *, blk):
    tokens, width = x_ref.shape
    for i in range(width // WIDE):
        held[i * WIDE : (i + 1) * WIDE, :] = x_ref[:, i * WIDE : (i + 1) * WIDE].T

    def move(i, _):
        source = pl.multiple_of(order_ref[i] * blk, blk)
        target = pl.multiple_of(i * blk, blk)
        o_ref[pl.ds(target, blk), :] = held[pl.ds(source, blk), :]
        return 0

    lax.fori_loop(0, width // blk, move, 0)


def turned(x, order):
    tokens, width = x.shape
    blk = width // order.shape[0]
    if blk % 16:
        blocks = jnp.take(x.T.reshape(order.shape[0], blk, tokens), order, axis=0)
        return blocks.reshape(width, tokens)
    return pl.pallas_call(
        functools.partial(turn_kernel, blk=blk),
        out_shape=jax.ShapeDtypeStruct((width, tokens), x.dtype),
        in_specs=[
            pl.BlockSpec(memory_space=pltpu.SMEM),
            pl.BlockSpec(memory_space=pltpu.VMEM),
        ],
        out_specs=pl.BlockSpec(memory_space=pltpu.VMEM),
        scratch_shapes=[pltpu.VMEM((width, tokens), x.dtype)],
        compiler_params=pltpu.CompilerParams(vmem_limit_bytes=32 << 20),
        cost_estimate=pl.CostEstimate(flops=0, bytes_accessed=4 * x.size, transcendentals=0),
        name="turned",
    )(order, x)


def reduce_term(grid, left, right, extra=None, around=False):
    rows = left.shape[0]
    mine = rows // 2

    def term(start, size):
        part = mm(left[start : start + size], right, NN)
        if extra is not None:
            part = jnp.concatenate([part, extra[start : start + size].astype(F32)], 1)
        return part

    (arrived,) = yield [grid.next(term(mine, mine).astype(BF16), "c")]
    held = []
    for h, axes in enumerate(HALVES):
        start = h * (mine // 2)
        count = grid.size(axes[0])
        size = mine // 2 // count
        held.append(
            [
                (term(at, size) + arrived[at : at + size].astype(F32)).astype(BF16)
                for at in range(start, start + count * size, size)
            ]
        )
    for step in range(2):
        totals = [None, None]
        counts = [grid.size(axes[step]) for axes in HALVES]
        for k in range(1, max(counts)):
            live = [h for h in range(2) if k < counts[h]]
            sent = [
                grid.next(held[h][1] if k == 1 else totals[h], HALVES[h][step]) for h in live
            ]
            came = yield sent
            for h, part in zip(live, came):
                own = held[h][(k + 1) % counts[h]]
                totals[h] = (part.astype(F32) + own.astype(F32)).astype(BF16)
        if step == 0:
            held = []
            for h, total in enumerate(totals):
                count = grid.size(HALVES[h][1])
                size = total.shape[0] // count
                held.append([total[j * size : (j + 1) * size] for j in range(count)])
    if not around:
        joined = jnp.concatenate(totals, 0)
        (share,) = yield [lax.psum_scatter(joined, "dp", scatter_dimension=0, tiled=True)]
        return share.astype(F32)
    half = grid.n_dp // 2
    size = totals[0].shape[0] // half
    held = [t[at : at + size] for t in totals for at in range(0, half * size, size)]
    total = held[1]
    for k in range(1, grid.n_dp):
        (came,) = yield [grid.next(total, "d")]
        total = came.astype(F32) + held[(k + 1) % grid.n_dp].astype(F32)
        total = total if k == grid.n_dp - 1 else total.astype(BF16)
    return total


def place_kernel(order_ref, *refs, sources, slots):
    pieces = refs[: -(3 + 1)]
    out_ref, held, in_sem, out_sem = refs[-4:]
    count = len(sources)

    def fetch(i):
        piece, place = sources[i]
        return pltpu.make_async_copy(
            pieces[piece].at[place], held.at[i % slots], in_sem.at[i % slots]
        )

    def store(i):
        return pltpu.make_async_copy(
            held.at[i % slots], out_ref.at[order_ref[i]], out_sem.at[i % slots]
        )

    ahead = slots // 2
    for i in range(min(ahead, count)):
        fetch(i).start()
    for i in range(count):
        fetch(i).wait()
        store(i).start()
        later = i + ahead
        if later < count:
            if later >= slots:
                store(later - slots).wait()
            fetch(later).start()
    for i in range(max(0, count - slots), count):
        store(i).wait()


def placed(order, pieces):
    blk, width = pieces[0].shape[-2:]
    flat = [p.reshape((-1, blk, width)) for p in pieces]
    sources = [(n, j) for n, p in enumerate(flat) for j in range(p.shape[0])]
    slots = 8
    whole = pl.pallas_call(
        functools.partial(place_kernel, sources=sources, slots=slots),
        out_shape=jax.ShapeDtypeStruct((len(sources), blk, width), flat[0].dtype),
        in_specs=[pl.BlockSpec(memory_space=pltpu.SMEM)]
        + [pl.BlockSpec(memory_space=pl.ANY)] * len(flat),
        out_specs=pl.BlockSpec(memory_space=pl.ANY),
        scratch_shapes=[
            pltpu.VMEM((slots, blk, width), flat[0].dtype),
            pltpu.SemaphoreType.DMA((slots,)),
            pltpu.SemaphoreType.DMA((slots,)),
        ],
        compiler_params=pltpu.CompilerParams(vmem_limit_bytes=16 << 20),
        cost_estimate=pl.CostEstimate(
            flops=0, bytes_accessed=4 * len(sources) * blk * width, transcendentals=0
        ),
        name="placed",
    )(order, *flat)
    return whole.reshape(len(sources) * blk, width)


def gather_weight(grid, weight, around=False):
    half = grid.n_dp // 2
    if around:
        column = [weight]
        for _ in range(grid.n_dp - 1):
            (came,) = yield [grid.next(column[-1], "d")]
            column.append(came)
        parts = [jnp.stack(column[:half]), jnp.stack(column[half:])]
    else:
        (column,) = yield [lax.all_gather(weight, "dp", axis=0)]
        parts = [column[:half], column[half:]]
    steps = [[parts[0]], [parts[1]]]
    for stage in (1, 0):
        counts = [grid.size(axes[stage]) for axes in HALVES]
        for k in range(1, max(counts)):
            live = [h for h in range(2) if k < counts[h]]
            came = yield [grid.next(steps[h][-1], HALVES[h][stage]) for h in live]
            for h, part in zip(live, came):
                steps[h].append(part)
        if stage == 1:
            steps = [[jnp.stack(s)] for s in steps]
    near = jnp.concatenate([p.reshape((-1,) + p.shape[-2:]) for p in steps[0] + steps[1]], 0)
    (far,) = yield [grid.next(near, "c")]
    return placed(grid.block_order(around), [near, far])


def gather_ring(grid, weight):
    part = weight
    for axis in ("a", "b"):
        steps = [part]
        for _ in range(grid.size(axis) - 1):
            (came,) = yield [grid.next(steps[-1], axis)]
            steps.append(came)
        part = jnp.stack(steps)
    near, far = [part], []
    waiting = [part]
    for k in range(grid.n_dp - 1):
        sent = [grid.next(near[-1], "d")]
        early = k == grid.n_dp // 2 - 1
        if early:
            sent.append(grid.next(jnp.stack(waiting), "c"))
            waiting = []
        came = yield sent
        if early:
            far.append(came[1])
        near.append(came[0])
        waiting.append(came[0])
    (other,) = yield [grid.next(jnp.stack(waiting), "c")]
    return placed(grid.ring_order(), near + far + [other])


def reduce_ring(grid, left, right):
    mine = left.shape[0] // 2
    (arrived,) = yield [grid.next(mm(left[mine:], right, NN).astype(BF16), "c")]
    size = mine // grid.n_dp
    held = [
        (mm(left[at : at + size], right, NN) + arrived[at : at + size].astype(F32)).astype(BF16)
        for at in range(0, mine, size)
    ]
    for axis in ("d", "b", "a"):
        count = grid.size(axis)
        total = held[1]
        for k in range(1, count):
            (came,) = yield [grid.next(total, axis)]
            total = (came.astype(F32) + held[(k + 1) % count].astype(F32)).astype(BF16)
        following = {"d": grid.n_b, "b": grid.n_a, "a": 1}[axis]
        size = total.shape[0] // following
        held = [total[at : at + size] for at in range(0, total.shape[0], size)]
    return held[0].astype(F32)


def gather_keys(grid, own):
    width = own.shape[1] // 2
    steps = [[own[:, :width]], [own[:, width:]]]
    for stage in (1, 0):
        counts = [grid.size(axes[stage]) for axes in HALVES]
        for k in range(1, max(counts)):
            live = [h for h in range(2) if k < counts[h]]
            came = yield [grid.next(steps[h][-1], HALVES[h][stage]) for h in live]
            for h, part in zip(live, came):
                steps[h].append(part)
        steps = [[jnp.stack(s)] for s in steps]
    near = [s[0] for s in steps]
    far = yield [grid.next(part, "c") for part in near]
    return tuple(
        jnp.stack([one, two]).reshape(-1, width) for one, two in zip(near, far)
    )


def reduce_keys(grid, terms):
    mine = terms.shape[0] // 2
    (came,) = yield [grid.next(terms[mine:], "c")]
    total = (terms[:mine].astype(F32) + came.astype(F32)).astype(BF16)
    for axis in ("b", "a"):
        count = grid.size(axis)
        size = total.shape[0] // count
        held = [total[at : at + size] for at in range(0, count * size, size)]
        total = held[1]
        for k in range(1, count):
            (came,) = yield [grid.next(total, axis)]
            total = (came.astype(F32) + held[(k + 1) % count].astype(F32)).astype(BF16)
    return total


class Chain:
    def __init__(self, generator):
        self.generator, self.done, self.result = generator, False, None
        self.flight = next(generator)

    def advance(self, arrived):
        try:
            self.flight = self.generator.send(arrived)
        except StopIteration as stop:
            self.done, self.result, self.flight = True, stop.value, []


def meet(main, *chains, hold=()):
    chains = [c for c in chains if not c.done]
    both = chains + [c for c in hold if not c.done]
    main, flights = lax.optimization_barrier((main, [list(c.flight) for c in both]))
    for i, (chain, flight) in enumerate(zip(both, flights)):
        chain.flight = flight
        if i < len(chains):
            chain.advance(flight)
    return main


def finish(chain):
    while not chain.done:
        chain.advance(chain.flight)
    return chain.result


def angles(positions):
    lane = jnp.arange(WIDE)
    freq = 10000.0 ** (-((lane % (HD // 2)).astype(F32) * 2.0 / HD))
    turn = positions.astype(F32)[:, None] * freq[None, :]
    sign = jnp.where(lane % HD < HD // 2, -1.0, 1.0)
    return jnp.cos(turn), jnp.sin(turn) * sign[None, :]


def normalize(rows):
    factor = lax.rsqrt(jnp.mean(rows * rows, -1, keepdims=True) + EPS)
    return (rows * factor, factor)


def norm_back(upstream, normed, factor, gain):
    scaled = upstream * gain
    inner = jnp.mean(scaled * normed, -1, keepdims=True)
    return (factor * (scaled - normed * inner), jnp.sum(upstream * normed, 0))


def body(
    n_dp,
    n_ctx,
    layer_in,
    positions,
    attn_gain,
    query_proj,
    key_proj,
    value_proj,
    merge_proj,
    ffn_gain,
    gate_proj,
    up_proj,
    down_proj,
    out_grad,
):
    _, rows, model = layer_in.shape
    kv_width = key_proj.shape[1]
    kv_heads = kv_width // HD
    width = query_proj.shape[1]
    run = rows // 2
    positions = positions[0]
    grid = Grid(n_dp, n_ctx)
    order, sum_order = grid.block_order(False), grid.block_order(True)
    ring_order, ctx_order = grid.ring_order(), grid.ctx_order()
    places = grid.value_places()

    gains = jnp.stack([attn_gain, ffn_gain], -1)
    gains = jnp.concatenate([gains, jnp.zeros((gains.shape[0], WIDE - 2), BF16)], 1)
    packed = jnp.concatenate([query_proj, key_proj, value_proj, gains], 1)
    packed, down_proj, gate_proj, merge_proj = lax.optimization_barrier(
        (packed, down_proj, gate_proj, merge_proj)
    )
    first_chain = Chain(gather_weight(grid, packed))
    down_chain = Chain(gather_weight(grid, down_proj))
    gate_chain = Chain(gather_weight(grid, gate_proj))
    merge_chain = Chain(gather_weight(grid, merge_proj))
    up_chain = Chain(gather_ring(grid, up_proj))
    all_pos = lax.all_gather(positions[::run], "ctx", axis=0, tiled=True)
    cosine, sine = angles(positions)
    rows_in = layer_in.reshape(rows, model).astype(F32)
    normed_one, factor_one = normalize(rows_in)
    all_pos, factor_one, cosine = meet((all_pos, factor_one, cosine), first_chain, up_chain)
    first_weights = finish(first_chain)
    attn_all = first_weights[:, : width + 2 * kv_width]
    gain_one = first_weights[:, width + 2 * kv_width].astype(F32)
    gain_two = first_weights[:, width + 2 * kv_width + 1].astype(F32)

    first_in = (normed_one * gain_one).astype(BF16)
    first_in = meet(first_in, down_chain)
    raw = mm(first_in, attn_all, NN)
    queries, own_kv = rotated(raw, cosine, sine, kv_width)
    kv_chain = Chain(gather_keys(grid, own_kv))
    later = all_pos.reshape(n_ctx, 2)[ctx_order].reshape(2 * n_ctx, 1)
    later = later > jnp.repeat(positions[::run], run)[None, :]
    bias = jnp.where(later, MASKED, 0.0).astype(F32)
    bias = meet(bias, kv_chain)
    bias = meet(bias, kv_chain)
    bias = meet(bias, kv_chain, down_chain, up_chain, gate_chain)
    all_keys, all_values = finish(kv_chain)
    kt, vt = all_keys.T, all_values.T

    grad_rows = out_grad.reshape(rows, model)
    plan = (
        ((), ()),
        ((up_chain,), ()),
        ((down_chain, merge_chain), (gate_chain,)),
        ((down_chain, merge_chain, gate_chain, up_chain), ()),
    )
    outs, log_sums = [], []
    for group in range(kv_heads):
        out, log_sum = attend(group, places, bias, queries, all_keys, vt)
        on, hold = plan[group % 4]
        queries, out, grad_rows = meet((queries, out, grad_rows), *on, hold=hold)
        outs.append(out)
        log_sums.append(log_sum)
    down_all = finish(down_chain)
    grad_hidden = mm(grad_rows, down_all, NT)
    outs, grad_hidden = meet((outs, grad_hidden), merge_chain)
    mixed = jnp.concatenate([out.astype(BF16) for out in outs], 1)
    mixed = meet(mixed, merge_chain)
    merge_all = finish(merge_chain)
    middle = rows_in + mm(mixed, merge_all, NN)
    normed_two, factor_two = normalize(middle)
    second_in = (normed_two * gain_two).astype(BF16)
    second_in = meet(second_in, up_chain)
    second_in = meet(second_in, gate_chain)
    up_all = finish(up_chain)
    lift = mm(second_in, up_all, NN)
    lift = meet(lift, gate_chain)
    gate_all = finish(gate_chain)
    gate = mm(second_in, gate_all, NN)
    sigma = jax.nn.sigmoid(gate)
    activated = gate * sigma
    hidden = (activated * lift).astype(BF16)
    grad_gate = (grad_hidden * lift * sigma * (1.0 + gate * (1.0 - sigma))).astype(BF16)
    grad_lift = (grad_hidden * activated).astype(BF16)
    hidden, grad_gate, grad_lift = lax.optimization_barrier((hidden, grad_gate, grad_lift))
    second_turned = turned(second_in, order)
    gate_sum = Chain(reduce_term(grid, second_turned, grad_gate))
    up_sum = Chain(reduce_term(grid, second_turned, grad_lift))
    down_sum = Chain(reduce_ring(grid, turned(hidden, ring_order), grad_rows))
    grad_second = mm(grad_gate, gate_all, NT)
    grad_second, grad_lift = meet((grad_second, grad_lift), gate_sum)
    grad_second = grad_second + mm(grad_lift, up_all, NT)
    grad_norm_two, gain_two_term = norm_back(grad_second, normed_two, factor_two, gain_two)
    grad_middle = grad_rows.astype(F32) + grad_norm_two
    grad_branch = grad_middle.astype(BF16)
    grad_mixed = mm(grad_branch, merge_all, NT).astype(BF16)
    grad_mixed, grad_branch = meet((grad_mixed, grad_branch), down_sum, up_sum)
    first_turned = turned(first_in, order)
    mixed_turned = turned(mixed, order)

    dqs, dkvs = [], []
    for group in range(kv_heads):
        dq, dkv = attend_back(
            group, places, bias, log_sums[group], outs[group], queries, grad_mixed,
            all_keys, all_values, kt,
        )
        dqs.append(dq)
        dkvs.append(dkv)
        if group == kv_heads - 4:
            grad_mixed, dkv = meet((grad_mixed, dkv), gate_sum, down_sum)
        elif group == kv_heads - 3:
            grad_mixed, dkv, grad_branch = meet(
                (grad_mixed, dkv, grad_branch), up_sum, down_sum, hold=(gate_sum,)
            )
            merge_sum = Chain(reduce_term(grid, mixed_turned, grad_branch))
        elif group == kv_heads - 2:
            grad_mixed, dkvs = meet((grad_mixed, dkvs), gate_sum, up_sum, merge_sum, down_sum)
            keys_sum = Chain(reduce_keys(grid, jnp.concatenate(dkvs, 1)))
    dqs, dkv = meet((dqs, dkv), keys_sum, gate_sum, down_sum, hold=(merge_sum,))
    last_keys = Chain(reduce_keys(grid, dkv))
    query_grads = unrotated(unrotate_queries_kernel, dqs, cosine, sine)
    query_sum = Chain(reduce_term(grid, first_turned, query_grads))
    grad_first = mm(query_grads, attn_all[:, :width], NT)
    grad_first = meet(grad_first, last_keys, keys_sum, query_sum, down_sum)
    grad_first = meet(grad_first, last_keys, keys_sum, merge_sum)
    grad_first = meet(grad_first, last_keys)
    wide = finish(keys_sum)
    dkv_parts = [wide[:, at : at + WIDE] for at in range(0, wide.shape[1], WIDE)]
    dkv_parts.append(finish(last_keys))
    kv_grads = unrotated(unrotate_keys_kernel, dkv_parts, cosine, sine)
    grad_first = grad_first + mm(kv_grads, attn_all[:, width:], NT)
    grad_norm_one, gain_one_term = norm_back(grad_first, normed_one, factor_one, gain_one)
    gain_terms = jnp.stack([gain_one_term, gain_two_term], 0)
    gain_terms = jnp.concatenate([gain_terms, jnp.zeros((WIDE - 2, model), F32)], 0)
    gain_columns = turned(gain_terms.astype(BF16), sum_order)
    last_turned = turned(first_in, sum_order)
    last = Chain(reduce_term(grid, last_turned, kv_grads, gain_columns, around=True))
    grad_norm_one, hidden = meet((grad_norm_one, hidden), last, query_sum, merge_sum, up_sum)
    result = middle + mm(hidden, down_all, NN)
    layer_out = result.astype(BF16).reshape(layer_in.shape)
    input_grad = (grad_middle + grad_norm_one).astype(BF16).reshape(layer_in.shape)
    layer_out, input_grad = meet((layer_out, input_grad), last, query_sum)
    while not last.done:
        input_grad = meet(input_grad, last)
    query_share, last_share = finish(query_sum), finish(last)
    merge_share, gate_share = finish(merge_sum), finish(gate_sum)
    up_share, down_share = finish(up_sum), finish(down_sum)
    return (
        layer_out,
        input_grad,
        last_share[:, 2 * kv_width],
        query_share,
        last_share[:, :kv_width],
        last_share[:, kv_width : 2 * kv_width],
        merge_share,
        last_share[:, 2 * kv_width + 1],
        gate_share,
        up_share,
        down_share,
    )


def solution(mesh):
    acts = P("dp", "ctx", None)
    rows = P(BOTH, None)
    flat = P(BOTH)
    return jax.shard_map(
        functools.partial(body, mesh.shape["dp"], mesh.shape["ctx"]),
        mesh=mesh,
        in_specs=(acts, P("dp", "ctx"), flat, rows, rows, rows, rows, flat, rows, rows, rows, acts),
        out_specs=(acts, acts, flat, rows, rows, rows, rows, flat, rows, rows, rows),
        check_vma=False,
    )
```

```python
import functools

import jax
import jax.numpy as jnp
import numpy as np
from jax import lax
from jax.experimental import pallas as pl
from jax.experimental.pallas import tpu as pltpu
from jax.sharding import PartitionSpec as P

HD = 64
EPS = 1e-05
WIDE = 128
MASKED = -1e30
SCALE = HD**-0.5
LOG2E = 1.4426950408889634
TO_LOG2 = SCALE * LOG2E
BRIEF = pl.CostEstimate(flops=1 << 20, bytes_accessed=1 << 16, transcendentals=0)
F32 = jnp.float32
BF16 = jnp.bfloat16
NT = (((1,), (1,)), ((), ()))
NN = (((1,), (0,)), ((), ()))


def mm(left, right, dims):
    return lax.dot_general(left, right, dims, preferred_element_type=F32)


def same_run_later(keys, rows):
    run = rows // 2
    key = lax.broadcasted_iota(jnp.int32, (keys, rows), 0)
    query = lax.broadcasted_iota(jnp.int32, (keys, rows), 1)
    return (key > query) & ((key // run) == (query // run))


def split_heads(pair_ref, which, low_ref, high_ref):
    both = pair_ref[...]
    turned = pltpu.roll(both.astype(F32), HD, 1).astype(BF16)
    lane = lax.broadcasted_iota(jnp.int32, both.shape, 1)
    zero = jnp.zeros_like(both)
    first, second = (both, turned) if which == 0 else (turned, both)
    low_ref[...] = jnp.where(lane < HD, first, zero)
    high_ref[...] = jnp.where(lane < HD, zero, second)


def biased(scores, bias_ref, block, rows):
    run = rows // 2
    start = pl.multiple_of(block * rows, rows)
    parts = [
        scores[i * run : (i + 1) * run] + bias_ref[pl.ds(block * 2 + i, 1), :]
        for i in range(2)
    ]
    return jnp.concatenate(parts, 0)


def attend_kernel(
    bias_ref, q_ref, kp_ref, vt_ref, o_ref, lse_ref, low, high, vx, turned, *, which, places
):
    rows, width = q_ref.shape
    length = kp_ref.shape[0]
    blocks = length // rows
    split_heads(kp_ref, which, low, high)
    vx[:HD, :] = vt_ref[...]
    top_row = lax.broadcasted_iota(jnp.int32, (16, length), 0) == 0
    vx[HD:, :] = top_row.astype(F32).astype(BF16)

    def scores(key, pair, block):
        start = pl.multiple_of(block * rows, rows)
        column = pl.multiple_of(pair * WIDE, WIDE)
        s = mm(key[pl.ds(start, rows), :], q_ref[:, pl.ds(column, WIDE)], NT) * TO_LOG2
        return biased(s, bias_ref, block, rows)

    def weigh(probs, block):
        start = places[block] * rows
        return mm(vx[:, start : start + rows], probs.astype(BF16), NN)

    def one_pair(pair, _):
        blocked = same_run_later(rows, rows)
        state = []
        for key in (low, high):
            s = jnp.where(blocked, MASKED, scores(key, pair, 0))
            top = jnp.max(s, 0, keepdims=True)
            state.append((top, weigh(jnp.exp2(s - top), 0)))

        def step(block, state):
            raw = [scores(key, pair, block) for key in (low, high)]
            result = []
            for (top, total), s in zip(state, raw):
                new_top = jnp.maximum(top, jnp.max(s, 0, keepdims=True))
                probs = jnp.exp2(s - new_top)
                result.append((new_top, total * jnp.exp2(top - new_top) + weigh(probs, block)))
            return result

        for block in range(1, blocks):
            state = step(block, state)
        for i, (top, total) in enumerate(state):
            weight_sum = total[HD : HD + 1, :]
            turned[i * HD : (i + 1) * HD, :] = total[:HD] / weight_sum
            lse_ref[pl.ds(pair * 2 + i, 1), :] = top + jnp.log2(weight_sum)
        column = pl.multiple_of(pair * WIDE, WIDE)
        o_ref[:, pl.ds(column, WIDE)] = turned[...].T
        return 0

    lax.fori_loop(0, width // WIDE, one_pair, 0)


def attend(group, places, bias, q, keys, vt):
    rows, width = q.shape
    length = keys.shape[0]
    kv_heads = vt.shape[0] // HD
    mine = width // kv_heads
    heads = mine // HD
    return pl.pallas_call(
        functools.partial(attend_kernel, which=group % 2, places=places),
        grid=(1,),
        out_shape=(
            jax.ShapeDtypeStruct((rows, mine), F32),
            jax.ShapeDtypeStruct((heads, rows), F32),
        ),
        in_specs=[
            pl.BlockSpec(bias.shape, lambda i: (0, 0)),
            pl.BlockSpec((rows, mine), lambda i: (0, group)),
            pl.BlockSpec((length, WIDE), lambda i: (0, group // 2)),
            pl.BlockSpec((HD, length), lambda i: (group, 0)),
        ],
        out_specs=(
            pl.BlockSpec((rows, mine), lambda i: (0, 0)),
            pl.BlockSpec((heads, rows), lambda i: (0, 0)),
        ),
        scratch_shapes=[
            pltpu.VMEM((length, WIDE), BF16),
            pltpu.VMEM((length, WIDE), BF16),
            pltpu.VMEM((HD + 16, length), BF16),
            pltpu.VMEM((WIDE, rows), F32),
        ],
        compiler_params=pltpu.CompilerParams(vmem_limit_bytes=40 << 20),
        cost_estimate=BRIEF,
        name="attend",
    )(bias, q, keys, vt)


def attend_back_kernel(
    place_ref, bias_ref, lse_ref, o_ref, q_ref, g_ref, kp_ref, vp_ref, kt_ref,
    dq_ref, dkv_ref, k_low, k_high, v_low, v_high, dqt, delta_ref, *, which, unroll
):
    rows, width = q_ref.shape
    length = kp_ref.shape[0]
    blocks = length // rows
    pairs = width // WIDE
    split_heads(kp_ref, which, k_low, k_high)
    split_heads(vp_ref, which, v_low, v_high)
    row = lax.broadcasted_iota(jnp.int32, (16, WIDE), 0)
    lane = lax.broadcasted_iota(jnp.int32, (16, WIDE), 1)
    chosen = (row == lane // HD).astype(F32).astype(BF16)
    for pair in range(pairs):
        column = pl.ds(pair * WIDE, WIDE)
        product = g_ref[:, column].astype(F32) * o_ref[:, column]
        main = product.astype(BF16)
        rest = (product - main.astype(F32)).astype(BF16)
        both = mm(chosen, main, NT) + mm(chosen, rest, NT)
        delta_ref[2 * pair : 2 * pair + 2, :] = both[:2]

    def block(index, diagonal):
        start = pl.multiple_of(index * rows, rows)
        value_start = pl.multiple_of(place_ref[index] * rows, rows)

        def some_heads(i, sums):
            sums = list(sums)
            work = []
            for t in range(unroll):
                pair = i * unroll + t
                column = pl.multiple_of(pair * WIDE, WIDE)
                query = q_ref[:, pl.ds(column, WIDE)]
                grad = g_ref[:, pl.ds(column, WIDE)]
                for side, (key, value) in enumerate(((k_low, v_low), (k_high, v_high))):
                    head = pair * 2 + side
                    shift = -lse_ref[pl.ds(head, 1), :]
                    run = rows // 2
                    s = mm(key[pl.ds(start, rows), :], query, NT) * TO_LOG2
                    s = jnp.concatenate(
                        [
                            s[r * run : (r + 1) * run]
                            + (bias_ref[pl.ds(index * 2 + r, 1), :] + shift)
                            for r in range(2)
                        ],
                        0,
                    )
                    p = jnp.exp2(s)
                    if diagonal:
                        p = jnp.where(same_run_later(rows, rows), 0.0, p)
                    slope = mm(value[pl.ds(value_start, rows), :], grad, NT)
                    d = (p * (slope - delta_ref[pl.ds(head, 1), :])).astype(BF16)
                    work.append((side, pair, query, grad, p.astype(BF16), d))
            for side, pair, query, grad, p, d in work:
                sums[side] = sums[side] + mm(d, query, NN)
                sums[2 + side] = sums[2 + side] + mm(p, grad, NN)
                term = mm(kt_ref[:, pl.ds(start, rows)], d, NN)
                row = pl.multiple_of(pair * WIDE + side * HD, HD)
                if diagonal:
                    dqt[pl.ds(row, HD), :] = term
                else:
                    dqt[pl.ds(row, HD), :] += term
            return tuple(sums)

        zero = jnp.zeros((rows, WIDE), F32)
        sums = lax.fori_loop(0, pairs // unroll, some_heads, (zero,) * 4)
        lane = lax.broadcasted_iota(jnp.int32, (rows, WIDE), 1)
        key_sum = sums[0] + pltpu.roll(sums[1], HD, 1)
        value_sum = pltpu.roll(sums[2], HD, 1) + sums[3]
        dkv_ref[pl.ds(start, rows), :] = jnp.where(
            lane < HD, key_sum * SCALE, value_sum
        ).astype(BF16)

    block(0, True)

    def rest(j, _):
        block(j, False)
        return 0

    lax.fori_loop(1, blocks, rest, 0)
    for pair in range(pairs):
        dq_ref[:, pair * WIDE : (pair + 1) * WIDE] = (
            dqt[pair * WIDE : (pair + 1) * WIDE, :] * SCALE
        ).T


def attend_back(group, places, bias, lse, out, q, g, keys, values, kt, unroll=2):
    rows, width = q.shape
    length = keys.shape[0]
    kv_heads = kt.shape[0] // HD
    mine = width // kv_heads
    heads = mine // HD
    return pl.pallas_call(
        functools.partial(attend_back_kernel, which=group % 2, unroll=unroll),
        grid=(1,),
        out_shape=(
            jax.ShapeDtypeStruct((rows, mine), F32),
            jax.ShapeDtypeStruct((length, WIDE), BF16),
        ),
        in_specs=[
            pl.BlockSpec(memory_space=pltpu.SMEM),
            pl.BlockSpec(bias.shape, lambda i: (0, 0)),
            pl.BlockSpec((heads, rows), lambda i: (0, 0)),
            pl.BlockSpec((rows, mine), lambda i: (0, 0)),
            pl.BlockSpec((rows, mine), lambda i: (0, group)),
            pl.BlockSpec((rows, mine), lambda i: (0, group)),
            pl.BlockSpec((length, WIDE), lambda i: (0, group // 2)),
            pl.BlockSpec((length, WIDE), lambda i: (0, group // 2)),
            pl.BlockSpec((HD, length), lambda i: (group, 0)),
        ],
        out_specs=(
            pl.BlockSpec((rows, mine), lambda i: (0, 0)),
            pl.BlockSpec((length, WIDE), lambda i: (0, 0)),
        ),
        scratch_shapes=[pltpu.VMEM((length, WIDE), BF16)] * 4
        + [pltpu.VMEM((mine, rows), F32), pltpu.VMEM((heads, rows), F32)],
        compiler_params=pltpu.CompilerParams(vmem_limit_bytes=48 << 20),
        cost_estimate=BRIEF,
        name="attend_back",
    )(jnp.array(places, jnp.int32), bias, lse, out, q, g, keys, values, kt)


def turn_pairs(x, cosine, sine):
    lane = lax.broadcasted_iota(jnp.int32, x.shape, 1)
    swapped = jnp.where(
        lane % HD < HD // 2, pltpu.roll(x, WIDE - HD // 2, 1), pltpu.roll(x, HD // 2, 1)
    )
    return x * cosine + swapped * sine


def rotate_kernel(cos_ref, sin_ref, raw_ref, q_ref, kv_ref, *, kv_width):
    cosine, sine = cos_ref[...], sin_ref[...]
    width = q_ref.shape[1]
    for at in range(0, width, WIDE):
        q_ref[:, at : at + WIDE] = turn_pairs(raw_ref[:, at : at + WIDE], cosine, sine).astype(BF16)
    for at in range(0, kv_width, WIDE):
        column = slice(width + at, width + at + WIDE)
        kv_ref[:, at : at + WIDE] = turn_pairs(raw_ref[:, column], cosine, sine).astype(BF16)
    kv_ref[:, kv_width:] = raw_ref[:, width + kv_width :].astype(BF16)


def rotated(raw, cosine, sine, kv_width):
    rows, total = raw.shape
    return pl.pallas_call(
        functools.partial(rotate_kernel, kv_width=kv_width),
        out_shape=(
            jax.ShapeDtypeStruct((rows, total - 2 * kv_width), BF16),
            jax.ShapeDtypeStruct((rows, 2 * kv_width), BF16),
        ),
        in_specs=[pl.BlockSpec(memory_space=pltpu.VMEM)] * 3,
        out_specs=(pl.BlockSpec(memory_space=pltpu.VMEM),) * 2,
        compiler_params=pltpu.CompilerParams(vmem_limit_bytes=32 << 20),
        cost_estimate=pl.CostEstimate(
            flops=8 * raw.size, bytes_accessed=6 * raw.size, transcendentals=0
        ),
        name="rotated",
    )(cosine, sine, raw)


def unrotate_queries_kernel(cos_ref, sin_ref, *refs):
    cosine, sine = cos_ref[...], -sin_ref[...]
    out_ref = refs[-1]
    mine = refs[0].shape[1]
    for n, ref in enumerate(refs[:-1]):
        for at in range(0, mine, WIDE):
            turned = turn_pairs(ref[:, at : at + WIDE], cosine, sine)
            out_ref[:, n * mine + at : n * mine + at + WIDE] = turned.astype(BF16)


def unrotate_keys_kernel(cos_ref, sin_ref, *refs):
    cosine, sine = cos_ref[...], -sin_ref[...]
    out_ref = refs[-1]
    count = len(refs) - 1
    lane = lax.broadcasted_iota(jnp.int32, cosine.shape, 1)
    for i in range(count // 2):
        first, second = refs[2 * i][...].astype(F32), refs[2 * i + 1][...].astype(F32)
        keys = jnp.where(lane < HD, first, pltpu.roll(second, HD, 1))
        values = jnp.where(lane < HD, pltpu.roll(first, HD, 1), second)
        at = i * WIDE
        out_ref[:, at : at + WIDE] = turn_pairs(keys, cosine, sine).astype(BF16)
        at = count * HD + i * WIDE
        out_ref[:, at : at + WIDE] = values.astype(BF16)


def unrotated(kernel, parts, cosine, sine):
    rows, mine = parts[0].shape
    total = len(parts) * mine
    return pl.pallas_call(
        kernel,
        out_shape=jax.ShapeDtypeStruct((rows, total), BF16),
        in_specs=[pl.BlockSpec(memory_space=pltpu.VMEM)] * (2 + len(parts)),
        out_specs=pl.BlockSpec(memory_space=pltpu.VMEM),
        compiler_params=pltpu.CompilerParams(vmem_limit_bytes=32 << 20),
        cost_estimate=pl.CostEstimate(
            flops=8 * rows * total, bytes_accessed=6 * rows * total, transcendentals=0
        ),
        name="unrotated",
    )(cosine, sine, *parts)


BOTH = ("dp", "ctx")


class Grid:
    def __init__(self, n_dp, n_ctx):
        self.n_dp, self.n_a, self.n_b = n_dp, 2, n_ctx // 4
        self.n_ctx = n_ctx
        self.ring = [0, 1, 3, 2] if n_dp == 4 else list(range(n_dp))
        own = lax.axis_index("ctx").astype(jnp.int32)
        self.a = own // (2 * self.n_b)
        self.b = (own // 2) % self.n_b
        self.c = own % 2
        places = np.argsort(np.array(self.ring)).astype(np.int32)
        self.d = jnp.asarray(places)[lax.axis_index("dp")]

    def size(self, axis):
        return {"a": self.n_a, "b": self.n_b, "c": 2, "d": self.n_dp}[axis]

    def next(self, values, axis):
        if axis == "d":
            around = self.ring[1:] + self.ring[:1]
            return lax.ppermute(values, "dp", list(zip(self.ring, around)))
        pairs = []
        for i in range(self.n_ctx):
            a, b, c = i // (2 * self.n_b), (i // 2) % self.n_b, i % 2
            if axis == "a":
                a = (a + 1) % self.n_a
            elif axis == "b":
                b = (b + 1) % self.n_b
            else:
                c = 1 - c
            pairs.append((i, (a * self.n_b + b) * 2 + c))
        return lax.ppermute(values, "ctx", pairs)

    def natural(self, rows):
        rows = np.array(rows, np.int32)
        a = (self.a - rows[:, 2]) % self.n_a
        b = (self.b - rows[:, 3]) % self.n_b
        c = (self.c - rows[:, 0]) % 2
        return ((rows[:, 1] * self.n_a + a) * self.n_b + b) * 2 + c

    def block_order(self, around):
        half = self.n_dp // 2
        rows, hops = [], []
        for core in range(2):
            for h, (first, second) in enumerate(HALVES):
                for i in range(self.size(first)):
                    for j in range(self.size(second)):
                        for d in range(half):
                            near = {first: i, second: j}
                            at = h * half + d
                            rows.append((core, 0 if around else at, near["a"], near["b"]))
                            hops.append(at)
        return self.natural(rows) + (self.around(hops) * self.n_ctx if around else 0)

    def around(self, hops):
        ring = jnp.asarray(np.array(self.ring, np.int32))
        return ring[(self.d - np.array(hops, np.int32)) % self.n_dp]

    def ring_order(self):
        rows, hops = [], []
        for core in range(2):
            for d in range(self.n_dp):
                for b in range(self.n_b):
                    for a in range(self.n_a):
                        rows.append((core, 0, a, b))
                        hops.append(d)
        return self.natural(rows) + self.around(hops) * self.n_ctx

    def ctx_order(self):
        rows = [
            (c, 0, a, b) for c in range(2) for b in range(self.n_b) for a in range(self.n_a)
        ]
        return self.natural(rows)

    def value_places(self):
        cells = [(c, b, a) for c in range(2) for b in range(self.n_b) for a in range(self.n_a)]
        return tuple((c * self.n_a + a) * self.n_b + b for c, b, a in cells)


HALVES = (("b", "a"), ("a", "b"))


def turn_kernel(order_ref, x_ref, o_ref, held, *, blk):
    tokens, width = x_ref.shape
    for i in range(width // WIDE):
        held[i * WIDE : (i + 1) * WIDE, :] = x_ref[:, i * WIDE : (i + 1) * WIDE].T

    def move(i, _):
        source = pl.multiple_of(order_ref[i] * blk, blk)
        target = pl.multiple_of(i * blk, blk)
        o_ref[pl.ds(target, blk), :] = held[pl.ds(source, blk), :]
        return 0

    lax.fori_loop(0, width // blk, move, 0)


def turned(x, order):
    tokens, width = x.shape
    blk = width // order.shape[0]
    if blk % 16:
        blocks = jnp.take(x.T.reshape(order.shape[0], blk, tokens), order, axis=0)
        return blocks.reshape(width, tokens)
    return pl.pallas_call(
        functools.partial(turn_kernel, blk=blk),
        out_shape=jax.ShapeDtypeStruct((width, tokens), x.dtype),
        in_specs=[
            pl.BlockSpec(memory_space=pltpu.SMEM),
            pl.BlockSpec(memory_space=pltpu.VMEM),
        ],
        out_specs=pl.BlockSpec(memory_space=pltpu.VMEM),
        scratch_shapes=[pltpu.VMEM((width, tokens), x.dtype)],
        compiler_params=pltpu.CompilerParams(vmem_limit_bytes=32 << 20),
        cost_estimate=pl.CostEstimate(flops=0, bytes_accessed=4 * x.size, transcendentals=0),
        name="turned",
    )(order, x)


def reduce_term(grid, left, right, extra=None, around=False):
    rows = left.shape[0]
    mine = rows // 2

    def term(start, size):
        part = mm(left[start : start + size], right, NN)
        if extra is not None:
            part = jnp.concatenate([part, extra[start : start + size].astype(F32)], 1)
        return part

    (arrived,) = yield [grid.next(term(mine, mine).astype(BF16), "c")]
    held = []
    for h, axes in enumerate(HALVES):
        start = h * (mine // 2)
        count = grid.size(axes[0])
        size = mine // 2 // count
        held.append(
            [
                (term(at, size) + arrived[at : at + size].astype(F32)).astype(BF16)
                for at in range(start, start + count * size, size)
            ]
        )
    for step in range(2):
        totals = [None, None]
        counts = [grid.size(axes[step]) for axes in HALVES]
        for k in range(1, max(counts)):
            live = [h for h in range(2) if k < counts[h]]
            sent = [
                grid.next(held[h][1] if k == 1 else totals[h], HALVES[h][step]) for h in live
            ]
            came = yield sent
            for h, part in zip(live, came):
                own = held[h][(k + 1) % counts[h]]
                totals[h] = (part.astype(F32) + own.astype(F32)).astype(BF16)
        if step == 0:
            held = []
            for h, total in enumerate(totals):
                count = grid.size(HALVES[h][1])
                size = total.shape[0] // count
                held.append([total[j * size : (j + 1) * size] for j in range(count)])
    if not around:
        joined = jnp.concatenate(totals, 0)
        (share,) = yield [lax.psum_scatter(joined, "dp", scatter_dimension=0, tiled=True)]
        return share.astype(F32)
    half = grid.n_dp // 2
    size = totals[0].shape[0] // half
    held = [t[at : at + size] for t in totals for at in range(0, half * size, size)]
    total = held[1]
    for k in range(1, grid.n_dp):
        (came,) = yield [grid.next(total, "d")]
        total = came.astype(F32) + held[(k + 1) % grid.n_dp].astype(F32)
        total = total if k == grid.n_dp - 1 else total.astype(BF16)
    return total


def place_kernel(order_ref, *refs, sources, slots):
    pieces = refs[: -(3 + 1)]
    out_ref, held, in_sem, out_sem = refs[-4:]
    count = len(sources)

    def fetch(i):
        piece, place = sources[i]
        return pltpu.make_async_copy(
            pieces[piece].at[place], held.at[i % slots], in_sem.at[i % slots]
        )

    def store(i):
        return pltpu.make_async_copy(
            held.at[i % slots], out_ref.at[order_ref[i]], out_sem.at[i % slots]
        )

    ahead = slots // 2
    for i in range(min(ahead, count)):
        fetch(i).start()
    for i in range(count):
        fetch(i).wait()
        store(i).start()
        later = i + ahead
        if later < count:
            if later >= slots:
                store(later - slots).wait()
            fetch(later).start()
    for i in range(max(0, count - slots), count):
        store(i).wait()


def placed(order, pieces):
    blk, width = pieces[0].shape[-2:]
    flat = [p.reshape((-1, blk, width)) for p in pieces]
    sources = [(n, j) for n, p in enumerate(flat) for j in range(p.shape[0])]
    slots = 8
    whole = pl.pallas_call(
        functools.partial(place_kernel, sources=sources, slots=slots),
        out_shape=jax.ShapeDtypeStruct((len(sources), blk, width), flat[0].dtype),
        in_specs=[pl.BlockSpec(memory_space=pltpu.SMEM)]
        + [pl.BlockSpec(memory_space=pl.ANY)] * len(flat),
        out_specs=pl.BlockSpec(memory_space=pl.ANY),
        scratch_shapes=[
            pltpu.VMEM((slots, blk, width), flat[0].dtype),
            pltpu.SemaphoreType.DMA((slots,)),
            pltpu.SemaphoreType.DMA((slots,)),
        ],
        compiler_params=pltpu.CompilerParams(vmem_limit_bytes=16 << 20),
        cost_estimate=pl.CostEstimate(
            flops=0, bytes_accessed=4 * len(sources) * blk * width, transcendentals=0
        ),
        name="placed",
    )(order, *flat)
    return whole.reshape(len(sources) * blk, width)


def gather_weight(grid, weight, around=False):
    half = grid.n_dp // 2
    if around:
        column = [weight]
        for _ in range(grid.n_dp - 1):
            (came,) = yield [grid.next(column[-1], "d")]
            column.append(came)
        parts = [jnp.stack(column[:half]), jnp.stack(column[half:])]
    else:
        (column,) = yield [lax.all_gather(weight, "dp", axis=0)]
        parts = [column[:half], column[half:]]
    steps = [[parts[0]], [parts[1]]]
    for stage in (1, 0):
        counts = [grid.size(axes[stage]) for axes in HALVES]
        for k in range(1, max(counts)):
            live = [h for h in range(2) if k < counts[h]]
            came = yield [grid.next(steps[h][-1], HALVES[h][stage]) for h in live]
            for h, part in zip(live, came):
                steps[h].append(part)
        if stage == 1:
            steps = [[jnp.stack(s)] for s in steps]
    near = jnp.concatenate([p.reshape((-1,) + p.shape[-2:]) for p in steps[0] + steps[1]], 0)
    (far,) = yield [grid.next(near, "c")]
    return placed(grid.block_order(around), [near, far])


def gather_ring(grid, weight):
    part = weight
    for axis in ("a", "b"):
        steps = [part]
        for _ in range(grid.size(axis) - 1):
            (came,) = yield [grid.next(steps[-1], axis)]
            steps.append(came)
        part = jnp.stack(steps)
    near, far = [part], []
    waiting = [part]
    for k in range(grid.n_dp - 1):
        sent = [grid.next(near[-1], "d")]
        early = k == grid.n_dp - 2
        if early:
            sent.append(grid.next(jnp.stack(waiting[:-1]), "c"))
            waiting = waiting[-1:]
        came = yield sent
        if early:
            far.append(came[1])
        near.append(came[0])
        waiting.append(came[0])
    (other,) = yield [grid.next(jnp.stack(waiting), "c")]
    return placed(grid.ring_order(), near + far + [other])


def reduce_ring(grid, left, right):
    mine = left.shape[0] // 2
    (arrived,) = yield [grid.next(mm(left[mine:], right, NN).astype(BF16), "c")]
    size = mine // grid.n_dp
    held = [
        (mm(left[at : at + size], right, NN) + arrived[at : at + size].astype(F32)).astype(BF16)
        for at in range(0, mine, size)
    ]
    for axis in ("d", "b", "a"):
        count = grid.size(axis)
        total = held[1]
        for k in range(1, count):
            (came,) = yield [grid.next(total, axis)]
            total = (came.astype(F32) + held[(k + 1) % count].astype(F32)).astype(BF16)
        following = {"d": grid.n_b, "b": grid.n_a, "a": 1}[axis]
        size = total.shape[0] // following
        held = [total[at : at + size] for at in range(0, total.shape[0], size)]
    return held[0].astype(F32)


def gather_keys(grid, own):
    width = own.shape[1] // 2
    steps = [[own[:, :width]], [own[:, width:]]]
    for stage in (1, 0):
        counts = [grid.size(axes[stage]) for axes in HALVES]
        for k in range(1, max(counts)):
            live = [h for h in range(2) if k < counts[h]]
            came = yield [grid.next(steps[h][-1], HALVES[h][stage]) for h in live]
            for h, part in zip(live, came):
                steps[h].append(part)
        steps = [[jnp.stack(s)] for s in steps]
    near = [s[0] for s in steps]
    far = yield [grid.next(part, "c") for part in near]
    return tuple(
        jnp.stack([one, two]).reshape(-1, width) for one, two in zip(near, far)
    )


def reduce_keys(grid, terms):
    mine = terms.shape[0] // 2
    (came,) = yield [grid.next(terms[mine:], "c")]
    total = (terms[:mine].astype(F32) + came.astype(F32)).astype(BF16)
    for axis in ("b", "a"):
        count = grid.size(axis)
        size = total.shape[0] // count
        held = [total[at : at + size] for at in range(0, count * size, size)]
        total = held[1]
        for k in range(1, count):
            (came,) = yield [grid.next(total, axis)]
            total = (came.astype(F32) + held[(k + 1) % count].astype(F32)).astype(BF16)
    return total


class Chain:
    def __init__(self, generator):
        self.generator, self.done, self.result = generator, False, None
        self.flight = next(generator)

    def advance(self, arrived):
        try:
            self.flight = self.generator.send(arrived)
        except StopIteration as stop:
            self.done, self.result, self.flight = True, stop.value, []


def meet(main, *chains, hold=()):
    chains = [c for c in chains if not c.done]
    both = chains + [c for c in hold if not c.done]
    main, flights = lax.optimization_barrier((main, [list(c.flight) for c in both]))
    for i, (chain, flight) in enumerate(zip(both, flights)):
        chain.flight = flight
        if i < len(chains):
            chain.advance(flight)
    return main


def finish(chain):
    while not chain.done:
        chain.advance(chain.flight)
    return chain.result


def angles(positions):
    lane = jnp.arange(WIDE)
    freq = 10000.0 ** (-((lane % (HD // 2)).astype(F32) * 2.0 / HD))
    turn = positions.astype(F32)[:, None] * freq[None, :]
    sign = jnp.where(lane % HD < HD // 2, -1.0, 1.0)
    return jnp.cos(turn), jnp.sin(turn) * sign[None, :]


def normalize(rows):
    factor = lax.rsqrt(jnp.mean(rows * rows, -1, keepdims=True) + EPS)
    return (rows * factor, factor)


def norm_back(upstream, normed, factor, gain):
    scaled = upstream * gain
    inner = jnp.mean(scaled * normed, -1, keepdims=True)
    return (factor * (scaled - normed * inner), jnp.sum(upstream * normed, 0))


def body(
    n_dp,
    n_ctx,
    layer_in,
    positions,
    attn_gain,
    query_proj,
    key_proj,
    value_proj,
    merge_proj,
    ffn_gain,
    gate_proj,
    up_proj,
    down_proj,
    out_grad,
):
    _, rows, model = layer_in.shape
    kv_width = key_proj.shape[1]
    kv_heads = kv_width // HD
    width = query_proj.shape[1]
    run = rows // 2
    positions = positions[0]
    grid = Grid(n_dp, n_ctx)
    order, sum_order = grid.block_order(False), grid.block_order(True)
    ring_order, ctx_order = grid.ring_order(), grid.ctx_order()
    places = grid.value_places()

    gains = jnp.stack([attn_gain, ffn_gain], -1)
    gains = jnp.concatenate([gains, jnp.zeros((gains.shape[0], WIDE - 2), BF16)], 1)
    packed = jnp.concatenate([query_proj, key_proj, value_proj, gains], 1)
    down_chain = Chain(gather_weight(grid, down_proj))
    gate_chain = Chain(gather_weight(grid, gate_proj))
    merge_chain = Chain(gather_weight(grid, merge_proj))
    first_chain = Chain(gather_weight(grid, packed, True))
    up_chain = Chain(gather_ring(grid, up_proj))
    all_pos = lax.all_gather(positions[::run], "ctx", axis=0, tiled=True)
    cosine, sine = angles(positions)
    rows_in = layer_in.reshape(rows, model).astype(F32)
    normed_one, factor_one = normalize(rows_in)
    all_pos, factor_one = meet((all_pos, factor_one), first_chain, up_chain)
    factor_one = meet(factor_one, first_chain)
    cosine, sine = meet((cosine, sine), first_chain, up_chain)
    cosine = meet(cosine, first_chain, down_chain)
    first_weights = finish(first_chain)
    attn_all = first_weights[:, : width + 2 * kv_width]
    gain_one = first_weights[:, width + 2 * kv_width].astype(F32)
    gain_two = first_weights[:, width + 2 * kv_width + 1].astype(F32)

    first_in = (normed_one * gain_one).astype(BF16)
    first_in = meet(first_in, down_chain)
    raw = mm(first_in, attn_all, NN)
    queries, own_kv = rotated(raw, cosine, sine, kv_width)
    kv_chain = Chain(gather_keys(grid, own_kv))
    later = all_pos.reshape(n_ctx, 2)[ctx_order].reshape(2 * n_ctx, 1)
    later = later > jnp.repeat(positions[::run], run)[None, :]
    bias = jnp.where(later, MASKED, 0.0).astype(F32)
    bias = meet(bias, kv_chain)
    bias = meet(bias, kv_chain)
    bias = meet(bias, kv_chain, gate_chain, up_chain)
    all_keys, all_values = finish(kv_chain)
    kt, vt = all_keys.T, all_values.T

    grad_rows = out_grad.reshape(rows, model)
    plan = (
        ((), ()),
        ((down_chain, merge_chain, up_chain), (gate_chain,)),
        ((down_chain, merge_chain, gate_chain), ()),
        ((merge_chain, gate_chain, up_chain), ()),
    )
    outs, log_sums = [], []
    for group in range(kv_heads):
        out, log_sum = attend(group, places, bias, queries, all_keys, vt)
        on, hold = plan[group % 4]
        queries, out, grad_rows = meet((queries, out, grad_rows), *on, hold=hold)
        if group == 2:
            down_all = finish(down_chain)
            grad_hidden = mm(grad_rows, down_all, NT)
            queries, grad_hidden = lax.optimization_barrier((queries, grad_hidden))
        outs.append(out)
        log_sums.append(log_sum)
    mixed = jnp.concatenate([out.astype(BF16) for out in outs], 1)
    mixed = meet(mixed, merge_chain)
    merge_all = finish(merge_chain)
    middle = rows_in + mm(mixed, merge_all, NN)
    normed_two, factor_two = normalize(middle)
    second_in = (normed_two * gain_two).astype(BF16)
    second_in = meet(second_in, up_chain)
    up_all = finish(up_chain)
    lift = mm(second_in, up_all, NN)
    lift = meet(lift, gate_chain)
    gate_all = finish(gate_chain)
    gate = mm(second_in, gate_all, NN)
    sigma = jax.nn.sigmoid(gate)
    activated = gate * sigma
    hidden = (activated * lift).astype(BF16)
    grad_gate = (grad_hidden * lift * sigma * (1.0 + gate * (1.0 - sigma))).astype(BF16)
    grad_lift = (grad_hidden * activated).astype(BF16)
    hidden, grad_gate, grad_lift = lax.optimization_barrier((hidden, grad_gate, grad_lift))
    second_turned = turned(second_in, order)
    gate_sum = Chain(reduce_term(grid, second_turned, grad_gate))
    up_sum = Chain(reduce_term(grid, second_turned, grad_lift))
    down_sum = Chain(reduce_ring(grid, turned(hidden, ring_order), grad_rows))
    grad_second = mm(grad_gate, gate_all, NT)
    grad_second, grad_lift = meet((grad_second, grad_lift), gate_sum)
    grad_second = grad_second + mm(grad_lift, up_all, NT)
    grad_norm_two, gain_two_term = norm_back(grad_second, normed_two, factor_two, gain_two)
    grad_middle = grad_rows.astype(F32) + grad_norm_two
    grad_branch = grad_middle.astype(BF16)
    grad_mixed = mm(grad_branch, merge_all, NT).astype(BF16)
    grad_mixed, grad_branch = meet((grad_mixed, grad_branch), down_sum, up_sum)
    first_turned = turned(first_in, order)
    mixed_turned = turned(mixed, order)

    dqs, dkvs = [], []
    for group in range(kv_heads):
        dq, dkv = attend_back(
            group, places, bias, log_sums[group], outs[group], queries, grad_mixed,
            all_keys, all_values, kt,
        )
        dqs.append(dq)
        dkvs.append(dkv)
        if group == kv_heads - 4:
            grad_mixed, dkv = meet((grad_mixed, dkv), gate_sum, down_sum)
        elif group == kv_heads - 3:
            grad_mixed, dkv, grad_branch = meet(
                (grad_mixed, dkv, grad_branch), up_sum, down_sum, hold=(gate_sum,)
            )
            merge_sum = Chain(reduce_term(grid, mixed_turned, grad_branch))
        elif group == kv_heads - 2:
            grad_mixed, dkvs = meet((grad_mixed, dkvs), gate_sum, up_sum, merge_sum, down_sum)
            keys_sum = Chain(reduce_keys(grid, jnp.concatenate(dkvs, 1)))
    dqs, dkv = meet((dqs, dkv), keys_sum, gate_sum, merge_sum, hold=(down_sum,))
    last_keys = Chain(reduce_keys(grid, dkv))
    query_grads = unrotated(unrotate_queries_kernel, dqs, cosine, sine)
    query_sum = Chain(reduce_term(grid, first_turned, query_grads))
    grad_first = mm(query_grads, attn_all[:, :width], NT)
    grad_first = meet(grad_first, last_keys, keys_sum, query_sum, merge_sum)
    grad_first = meet(grad_first, last_keys, keys_sum, down_sum)
    grad_first = meet(grad_first, last_keys)
    wide = finish(keys_sum)
    dkv_parts = [wide[:, at : at + WIDE] for at in range(0, wide.shape[1], WIDE)]
    dkv_parts.append(finish(last_keys))
    kv_grads = unrotated(unrotate_keys_kernel, dkv_parts, cosine, sine)
    grad_first = grad_first + mm(kv_grads, attn_all[:, width:], NT)
    grad_norm_one, gain_one_term = norm_back(grad_first, normed_one, factor_one, gain_one)
    gain_terms = jnp.stack([gain_one_term, gain_two_term], 0)
    gain_terms = jnp.concatenate([gain_terms, jnp.zeros((WIDE - 2, model), F32)], 0)
    gain_columns = turned(gain_terms.astype(BF16), sum_order)
    last_turned = turned(first_in, sum_order)
    last = Chain(reduce_term(grid, last_turned, kv_grads, gain_columns, around=True))
    input_grad = (grad_middle + grad_norm_one).astype(BF16).reshape(layer_in.shape)
    last.flight, input_grad = lax.optimization_barrier((last.flight, input_grad))
    input_grad = meet(input_grad, last, query_sum, up_sum, down_sum)
    input_grad, hidden = meet((input_grad, hidden), last, query_sum)
    result = middle + mm(hidden, down_all, NN)
    layer_out = result.astype(BF16).reshape(layer_in.shape)
    input_grad = meet(input_grad, last)
    input_grad, layer_out = meet((input_grad, layer_out), last, merge_sum)
    while not last.done:
        input_grad = meet(input_grad, last)
    query_share, last_share = finish(query_sum), finish(last)
    merge_share, gate_share = finish(merge_sum), finish(gate_sum)
    up_share, down_share = finish(up_sum), finish(down_sum)
    return (
        layer_out,
        input_grad,
        last_share[:, 2 * kv_width],
        query_share,
        last_share[:, :kv_width],
        last_share[:, kv_width : 2 * kv_width],
        merge_share,
        last_share[:, 2 * kv_width + 1],
        gate_share,
        up_share,
        down_share,
    )


def solution(mesh):
    acts = P("dp", "ctx", None)
    rows = P(BOTH, None)
    flat = P(BOTH)
    return jax.shard_map(
        functools.partial(body, mesh.shape["dp"], mesh.shape["ctx"]),
        mesh=mesh,
        in_specs=(acts, P("dp", "ctx"), flat, rows, rows, rows, rows, flat, rows, rows, rows, acts),
        out_specs=(acts, acts, flat, rows, rows, rows, rows, flat, rows, rows, rows),
        check_vma=False,
    )
```

```python
import functools

import jax
import jax.numpy as jnp
import numpy as np
from jax import lax
from jax.experimental import pallas as pl
from jax.experimental.pallas import tpu as pltpu
from jax.sharding import PartitionSpec as P

HD = 64
EPS = 1e-05
WIDE = 128
MASKED = -1e30
SCALE = HD**-0.5
LOG2E = 1.4426950408889634
TO_LOG2 = SCALE * LOG2E
BRIEF = pl.CostEstimate(flops=1 << 20, bytes_accessed=1 << 16, transcendentals=0)
F32 = jnp.float32
BF16 = jnp.bfloat16
NT = (((1,), (1,)), ((), ()))
NN = (((1,), (0,)), ((), ()))


def mm(left, right, dims):
    return lax.dot_general(left, right, dims, preferred_element_type=F32)


def same_run_later(keys, rows):
    run = rows // 2
    key = lax.broadcasted_iota(jnp.int32, (keys, rows), 0)
    query = lax.broadcasted_iota(jnp.int32, (keys, rows), 1)
    return (key > query) & ((key // run) == (query // run))


def split_heads(pair_ref, which, low_ref, high_ref):
    both = pair_ref[...]
    turned = pltpu.roll(both.astype(F32), HD, 1).astype(BF16)
    lane = lax.broadcasted_iota(jnp.int32, both.shape, 1)
    zero = jnp.zeros_like(both)
    first, second = (both, turned) if which == 0 else (turned, both)
    low_ref[...] = jnp.where(lane < HD, first, zero)
    high_ref[...] = jnp.where(lane < HD, zero, second)


def biased(scores, bias_ref, block, rows):
    run = rows // 2
    start = pl.multiple_of(block * rows, rows)
    parts = [
        scores[i * run : (i + 1) * run] + bias_ref[pl.ds(block * 2 + i, 1), :]
        for i in range(2)
    ]
    return jnp.concatenate(parts, 0)


def attend_kernel(
    bias_ref, q_ref, kp_ref, vt_ref, o_ref, lse_ref, low, high, vx, turned, *, which, places
):
    rows, width = q_ref.shape
    length = kp_ref.shape[0]
    blocks = length // rows
    split_heads(kp_ref, which, low, high)
    vx[:HD, :] = vt_ref[...]
    top_row = lax.broadcasted_iota(jnp.int32, (16, length), 0) == 0
    vx[HD:, :] = top_row.astype(F32).astype(BF16)

    def scores(key, pair, block):
        start = pl.multiple_of(block * rows, rows)
        column = pl.multiple_of(pair * WIDE, WIDE)
        s = mm(key[pl.ds(start, rows), :], q_ref[:, pl.ds(column, WIDE)], NT) * TO_LOG2
        return biased(s, bias_ref, block, rows)

    def weigh(probs, block):
        start = places[block] * rows
        return mm(vx[:, start : start + rows], probs.astype(BF16), NN)

    def one_pair(pair, _):
        blocked = same_run_later(rows, rows)
        state = []
        for key in (low, high):
            s = jnp.where(blocked, MASKED, scores(key, pair, 0))
            top = jnp.max(s, 0, keepdims=True)
            state.append((top, weigh(jnp.exp2(s - top), 0)))

        def step(block, state):
            raw = [scores(key, pair, block) for key in (low, high)]
            result = []
            for (top, total), s in zip(state, raw):
                new_top = jnp.maximum(top, jnp.max(s, 0, keepdims=True))
                probs = jnp.exp2(s - new_top)
                result.append((new_top, total * jnp.exp2(top - new_top) + weigh(probs, block)))
            return result

        for block in range(1, blocks):
            state = step(block, state)
        for i, (top, total) in enumerate(state):
            weight_sum = total[HD : HD + 1, :]
            turned[i * HD : (i + 1) * HD, :] = total[:HD] / weight_sum
            lse_ref[pl.ds(pair * 2 + i, 1), :] = top + jnp.log2(weight_sum)
        column = pl.multiple_of(pair * WIDE, WIDE)
        o_ref[:, pl.ds(column, WIDE)] = turned[...].T
        return 0

    lax.fori_loop(0, width // WIDE, one_pair, 0)


def attend(group, places, bias, q, keys, vt):
    rows, width = q.shape
    length = keys.shape[0]
    kv_heads = vt.shape[0] // HD
    mine = width // kv_heads
    heads = mine // HD
    return pl.pallas_call(
        functools.partial(attend_kernel, which=group % 2, places=places),
        grid=(1,),
        out_shape=(
            jax.ShapeDtypeStruct((rows, mine), F32),
            jax.ShapeDtypeStruct((heads, rows), F32),
        ),
        in_specs=[
            pl.BlockSpec(bias.shape, lambda i: (0, 0)),
            pl.BlockSpec((rows, mine), lambda i: (0, group)),
            pl.BlockSpec((length, WIDE), lambda i: (0, group // 2)),
            pl.BlockSpec((HD, length), lambda i: (group, 0)),
        ],
        out_specs=(
            pl.BlockSpec((rows, mine), lambda i: (0, 0)),
            pl.BlockSpec((heads, rows), lambda i: (0, 0)),
        ),
        scratch_shapes=[
            pltpu.VMEM((length, WIDE), BF16),
            pltpu.VMEM((length, WIDE), BF16),
            pltpu.VMEM((HD + 16, length), BF16),
            pltpu.VMEM((WIDE, rows), F32),
        ],
        compiler_params=pltpu.CompilerParams(vmem_limit_bytes=40 << 20),
        cost_estimate=BRIEF,
        name="attend",
    )(bias, q, keys, vt)


def attend_back_kernel(
    place_ref, bias_ref, lse_ref, o_ref, q_ref, g_ref, kp_ref, vp_ref, kt_ref,
    dq_ref, dkv_ref, k_low, k_high, v_low, v_high, dqt, delta_ref, *, which, unroll
):
    rows, width = q_ref.shape
    length = kp_ref.shape[0]
    blocks = length // rows
    pairs = width // WIDE
    split_heads(kp_ref, which, k_low, k_high)
    split_heads(vp_ref, which, v_low, v_high)
    row = lax.broadcasted_iota(jnp.int32, (16, WIDE), 0)
    lane = lax.broadcasted_iota(jnp.int32, (16, WIDE), 1)
    chosen = (row == lane // HD).astype(F32).astype(BF16)
    for pair in range(pairs):
        column = pl.ds(pair * WIDE, WIDE)
        product = g_ref[:, column].astype(F32) * o_ref[:, column]
        main = product.astype(BF16)
        rest = (product - main.astype(F32)).astype(BF16)
        both = mm(chosen, main, NT) + mm(chosen, rest, NT)
        delta_ref[2 * pair : 2 * pair + 2, :] = both[:2]

    def block(index, diagonal):
        start = pl.multiple_of(index * rows, rows)
        value_start = pl.multiple_of(place_ref[index] * rows, rows)

        def some_heads(i, sums):
            sums = list(sums)
            work = []
            for t in range(unroll):
                pair = i * unroll + t
                column = pl.multiple_of(pair * WIDE, WIDE)
                query = q_ref[:, pl.ds(column, WIDE)]
                grad = g_ref[:, pl.ds(column, WIDE)]
                for side, (key, value) in enumerate(((k_low, v_low), (k_high, v_high))):
                    head = pair * 2 + side
                    shift = -lse_ref[pl.ds(head, 1), :]
                    run = rows // 2
                    s = mm(key[pl.ds(start, rows), :], query, NT) * TO_LOG2
                    s = jnp.concatenate(
                        [
                            s[r * run : (r + 1) * run]
                            + (bias_ref[pl.ds(index * 2 + r, 1), :] + shift)
                            for r in range(2)
                        ],
                        0,
                    )
                    p = jnp.exp2(s)
                    if diagonal:
                        p = jnp.where(same_run_later(rows, rows), 0.0, p)
                    slope = mm(value[pl.ds(value_start, rows), :], grad, NT)
                    d = (p * (slope - delta_ref[pl.ds(head, 1), :])).astype(BF16)
                    work.append((side, pair, query, grad, p.astype(BF16), d))
            for side, pair, query, grad, p, d in work:
                sums[side] = sums[side] + mm(d, query, NN)
                sums[2 + side] = sums[2 + side] + mm(p, grad, NN)
                term = mm(kt_ref[:, pl.ds(start, rows)], d, NN)
                row = pl.multiple_of(pair * WIDE + side * HD, HD)
                if diagonal:
                    dqt[pl.ds(row, HD), :] = term
                else:
                    dqt[pl.ds(row, HD), :] += term
            return tuple(sums)

        zero = jnp.zeros((rows, WIDE), F32)
        sums = lax.fori_loop(0, pairs // unroll, some_heads, (zero,) * 4)
        lane = lax.broadcasted_iota(jnp.int32, (rows, WIDE), 1)
        key_sum = sums[0] + pltpu.roll(sums[1], HD, 1)
        value_sum = pltpu.roll(sums[2], HD, 1) + sums[3]
        dkv_ref[pl.ds(start, rows), :] = jnp.where(
            lane < HD, key_sum * SCALE, value_sum
        ).astype(BF16)

    block(0, True)

    def rest(j, _):
        block(j, False)
        return 0

    lax.fori_loop(1, blocks, rest, 0)
    for pair in range(pairs):
        dq_ref[:, pair * WIDE : (pair + 1) * WIDE] = (
            dqt[pair * WIDE : (pair + 1) * WIDE, :] * SCALE
        ).T


def attend_back(group, places, bias, lse, out, q, g, keys, values, kt, unroll=2):
    rows, width = q.shape
    length = keys.shape[0]
    kv_heads = kt.shape[0] // HD
    mine = width // kv_heads
    heads = mine // HD
    return pl.pallas_call(
        functools.partial(attend_back_kernel, which=group % 2, unroll=unroll),
        grid=(1,),
        out_shape=(
            jax.ShapeDtypeStruct((rows, mine), F32),
            jax.ShapeDtypeStruct((length, WIDE), BF16),
        ),
        in_specs=[
            pl.BlockSpec(memory_space=pltpu.SMEM),
            pl.BlockSpec(bias.shape, lambda i: (0, 0)),
            pl.BlockSpec((heads, rows), lambda i: (0, 0)),
            pl.BlockSpec((rows, mine), lambda i: (0, 0)),
            pl.BlockSpec((rows, mine), lambda i: (0, group)),
            pl.BlockSpec((rows, mine), lambda i: (0, group)),
            pl.BlockSpec((length, WIDE), lambda i: (0, group // 2)),
            pl.BlockSpec((length, WIDE), lambda i: (0, group // 2)),
            pl.BlockSpec((HD, length), lambda i: (group, 0)),
        ],
        out_specs=(
            pl.BlockSpec((rows, mine), lambda i: (0, 0)),
            pl.BlockSpec((length, WIDE), lambda i: (0, 0)),
        ),
        scratch_shapes=[pltpu.VMEM((length, WIDE), BF16)] * 4
        + [pltpu.VMEM((mine, rows), F32), pltpu.VMEM((heads, rows), F32)],
        compiler_params=pltpu.CompilerParams(vmem_limit_bytes=48 << 20),
        cost_estimate=BRIEF,
        name="attend_back",
    )(jnp.array(places, jnp.int32), bias, lse, out, q, g, keys, values, kt)


def turn_pairs(x, cosine, sine):
    lane = lax.broadcasted_iota(jnp.int32, x.shape, 1)
    swapped = jnp.where(
        lane % HD < HD // 2, pltpu.roll(x, WIDE - HD // 2, 1), pltpu.roll(x, HD // 2, 1)
    )
    return x * cosine + swapped * sine


def rotate_kernel(cos_ref, sin_ref, raw_ref, q_ref, kv_ref, *, kv_width):
    cosine, sine = cos_ref[...], sin_ref[...]
    width = q_ref.shape[1]
    for at in range(0, width, WIDE):
        q_ref[:, at : at + WIDE] = turn_pairs(raw_ref[:, at : at + WIDE], cosine, sine).astype(BF16)
    for at in range(0, kv_width, WIDE):
        column = slice(width + at, width + at + WIDE)
        kv_ref[:, at : at + WIDE] = turn_pairs(raw_ref[:, column], cosine, sine).astype(BF16)
    kv_ref[:, kv_width:] = raw_ref[:, width + kv_width :].astype(BF16)


def rotated(raw, cosine, sine, kv_width):
    rows, total = raw.shape
    return pl.pallas_call(
        functools.partial(rotate_kernel, kv_width=kv_width),
        out_shape=(
            jax.ShapeDtypeStruct((rows, total - 2 * kv_width), BF16),
            jax.ShapeDtypeStruct((rows, 2 * kv_width), BF16),
        ),
        in_specs=[pl.BlockSpec(memory_space=pltpu.VMEM)] * 3,
        out_specs=(pl.BlockSpec(memory_space=pltpu.VMEM),) * 2,
        compiler_params=pltpu.CompilerParams(vmem_limit_bytes=32 << 20),
        cost_estimate=pl.CostEstimate(
            flops=8 * raw.size, bytes_accessed=6 * raw.size, transcendentals=0
        ),
        name="rotated",
    )(cosine, sine, raw)


def unrotate_queries_kernel(cos_ref, sin_ref, *refs):
    cosine, sine = cos_ref[...], -sin_ref[...]
    out_ref = refs[-1]
    mine = refs[0].shape[1]
    for n, ref in enumerate(refs[:-1]):
        for at in range(0, mine, WIDE):
            turned = turn_pairs(ref[:, at : at + WIDE], cosine, sine)
            out_ref[:, n * mine + at : n * mine + at + WIDE] = turned.astype(BF16)


def unrotate_keys_kernel(cos_ref, sin_ref, *refs):
    cosine, sine = cos_ref[...], -sin_ref[...]
    out_ref = refs[-1]
    count = len(refs) - 1
    lane = lax.broadcasted_iota(jnp.int32, cosine.shape, 1)
    for i in range(count // 2):
        first, second = refs[2 * i][...].astype(F32), refs[2 * i + 1][...].astype(F32)
        keys = jnp.where(lane < HD, first, pltpu.roll(second, HD, 1))
        values = jnp.where(lane < HD, pltpu.roll(first, HD, 1), second)
        at = i * WIDE
        out_ref[:, at : at + WIDE] = turn_pairs(keys, cosine, sine).astype(BF16)
        at = count * HD + i * WIDE
        out_ref[:, at : at + WIDE] = values.astype(BF16)


def unrotated(kernel, parts, cosine, sine):
    rows, mine = parts[0].shape
    total = len(parts) * mine
    return pl.pallas_call(
        kernel,
        out_shape=jax.ShapeDtypeStruct((rows, total), BF16),
        in_specs=[pl.BlockSpec(memory_space=pltpu.VMEM)] * (2 + len(parts)),
        out_specs=pl.BlockSpec(memory_space=pltpu.VMEM),
        compiler_params=pltpu.CompilerParams(vmem_limit_bytes=32 << 20),
        cost_estimate=pl.CostEstimate(
            flops=8 * rows * total, bytes_accessed=6 * rows * total, transcendentals=0
        ),
        name="unrotated",
    )(cosine, sine, *parts)


BOTH = ("dp", "ctx")


class Grid:
    def __init__(self, n_dp, n_ctx):
        self.n_dp, self.n_a, self.n_b = n_dp, 2, n_ctx // 4
        self.n_ctx = n_ctx
        self.ring = [0, 1, 3, 2] if n_dp == 4 else list(range(n_dp))
        own = lax.axis_index("ctx").astype(jnp.int32)
        self.a = own // (2 * self.n_b)
        self.b = (own // 2) % self.n_b
        self.c = own % 2
        places = np.argsort(np.array(self.ring)).astype(np.int32)
        self.d = jnp.asarray(places)[lax.axis_index("dp")]

    def size(self, axis):
        return {"a": self.n_a, "b": self.n_b, "c": 2, "d": self.n_dp}[axis]

    def next(self, values, axis):
        if axis == "d":
            around = self.ring[1:] + self.ring[:1]
            return lax.ppermute(values, "dp", list(zip(self.ring, around)))
        pairs = []
        for i in range(self.n_ctx):
            a, b, c = i // (2 * self.n_b), (i // 2) % self.n_b, i % 2
            if axis == "a":
                a = (a + 1) % self.n_a
            elif axis == "b":
                b = (b + 1) % self.n_b
            else:
                c = 1 - c
            pairs.append((i, (a * self.n_b + b) * 2 + c))
        return lax.ppermute(values, "ctx", pairs)

    def natural(self, rows):
        rows = np.array(rows, np.int32)
        a = (self.a - rows[:, 2]) % self.n_a
        b = (self.b - rows[:, 3]) % self.n_b
        c = (self.c - rows[:, 0]) % 2
        return ((rows[:, 1] * self.n_a + a) * self.n_b + b) * 2 + c

    def block_order(self, around):
        half = self.n_dp // 2
        rows, hops = [], []
        for core in range(2):
            for h, (first, second) in enumerate(HALVES):
                for i in range(self.size(first)):
                    for j in range(self.size(second)):
                        for d in range(half):
                            near = {first: i, second: j}
                            at = h * half + d
                            rows.append((core, 0 if around else at, near["a"], near["b"]))
                            hops.append(at)
        return self.natural(rows) + (self.around(hops) * self.n_ctx if around else 0)

    def around(self, hops):
        ring = jnp.asarray(np.array(self.ring, np.int32))
        return ring[(self.d - np.array(hops, np.int32)) % self.n_dp]

    def ring_order(self):
        rows, hops = [], []
        for core in range(2):
            for d in range(self.n_dp):
                for b in range(self.n_b):
                    for a in range(self.n_a):
                        rows.append((core, 0, a, b))
                        hops.append(d)
        return self.natural(rows) + self.around(hops) * self.n_ctx

    def ctx_order(self):
        rows = [
            (c, 0, a, b) for c in range(2) for b in range(self.n_b) for a in range(self.n_a)
        ]
        return self.natural(rows)

    def value_places(self):
        cells = [(c, b, a) for c in range(2) for b in range(self.n_b) for a in range(self.n_a)]
        return tuple((c * self.n_a + a) * self.n_b + b for c, b, a in cells)


HALVES = (("b", "a"), ("a", "b"))


def turn_kernel(order_ref, x_ref, o_ref, held, *, blk):
    tokens, width = x_ref.shape
    for i in range(width // WIDE):
        held[i * WIDE : (i + 1) * WIDE, :] = x_ref[:, i * WIDE : (i + 1) * WIDE].T

    def move(i, _):
        source = pl.multiple_of(order_ref[i] * blk, blk)
        target = pl.multiple_of(i * blk, blk)
        o_ref[pl.ds(target, blk), :] = held[pl.ds(source, blk), :]
        return 0

    lax.fori_loop(0, width // blk, move, 0)


def turned(x, order):
    tokens, width = x.shape
    blk = width // order.shape[0]
    if blk % 16:
        blocks = jnp.take(x.T.reshape(order.shape[0], blk, tokens), order, axis=0)
        return blocks.reshape(width, tokens)
    return pl.pallas_call(
        functools.partial(turn_kernel, blk=blk),
        out_shape=jax.ShapeDtypeStruct((width, tokens), x.dtype),
        in_specs=[
            pl.BlockSpec(memory_space=pltpu.SMEM),
            pl.BlockSpec(memory_space=pltpu.VMEM),
        ],
        out_specs=pl.BlockSpec(memory_space=pltpu.VMEM),
        scratch_shapes=[pltpu.VMEM((width, tokens), x.dtype)],
        compiler_params=pltpu.CompilerParams(vmem_limit_bytes=32 << 20),
        cost_estimate=pl.CostEstimate(flops=0, bytes_accessed=4 * x.size, transcendentals=0),
        name="turned",
    )(order, x)


def reduce_term(grid, left, right, extra=None, around=False):
    rows = left.shape[0]
    mine = rows // 2

    def term(start, size):
        part = mm(left[start : start + size], right, NN)
        if extra is not None:
            part = jnp.concatenate([part, extra[start : start + size].astype(F32)], 1)
        return part

    (arrived,) = yield [grid.next(term(mine, mine).astype(BF16), "c")]
    held = []
    for h, axes in enumerate(HALVES):
        start = h * (mine // 2)
        count = grid.size(axes[0])
        size = mine // 2 // count
        held.append(
            [
                (term(at, size) + arrived[at : at + size].astype(F32)).astype(BF16)
                for at in range(start, start + count * size, size)
            ]
        )
    for step in range(2):
        totals = [None, None]
        counts = [grid.size(axes[step]) for axes in HALVES]
        for k in range(1, max(counts)):
            live = [h for h in range(2) if k < counts[h]]
            sent = [
                grid.next(held[h][1] if k == 1 else totals[h], HALVES[h][step]) for h in live
            ]
            came = yield sent
            for h, part in zip(live, came):
                own = held[h][(k + 1) % counts[h]]
                totals[h] = (part.astype(F32) + own.astype(F32)).astype(BF16)
        if step == 0:
            held = []
            for h, total in enumerate(totals):
                count = grid.size(HALVES[h][1])
                size = total.shape[0] // count
                held.append([total[j * size : (j + 1) * size] for j in range(count)])
    if not around:
        joined = jnp.concatenate(totals, 0)
        (share,) = yield [lax.psum_scatter(joined, "dp", scatter_dimension=0, tiled=True)]
        return share.astype(F32)
    half = grid.n_dp // 2
    size = totals[0].shape[0] // half
    held = [t[at : at + size] for t in totals for at in range(0, half * size, size)]
    total = held[1]
    for k in range(1, grid.n_dp):
        (came,) = yield [grid.next(total, "d")]
        total = came.astype(F32) + held[(k + 1) % grid.n_dp].astype(F32)
        total = total if k == grid.n_dp - 1 else total.astype(BF16)
    return total


def place_kernel(order_ref, *refs, sources, slots):
    pieces = refs[: -(3 + 1)]
    out_ref, held, in_sem, out_sem = refs[-4:]
    count = len(sources)

    def fetch(i):
        piece, place = sources[i]
        return pltpu.make_async_copy(
            pieces[piece].at[place], held.at[i % slots], in_sem.at[i % slots]
        )

    def store(i):
        return pltpu.make_async_copy(
            held.at[i % slots], out_ref.at[order_ref[i]], out_sem.at[i % slots]
        )

    ahead = slots // 2
    for i in range(min(ahead, count)):
        fetch(i).start()
    for i in range(count):
        fetch(i).wait()
        store(i).start()
        later = i + ahead
        if later < count:
            if later >= slots:
                store(later - slots).wait()
            fetch(later).start()
    for i in range(max(0, count - slots), count):
        store(i).wait()


def placed(order, pieces):
    blk, width = pieces[0].shape[-2:]
    flat = [p.reshape((-1, blk, width)) for p in pieces]
    sources = [(n, j) for n, p in enumerate(flat) for j in range(p.shape[0])]
    slots = 8
    whole = pl.pallas_call(
        functools.partial(place_kernel, sources=sources, slots=slots),
        out_shape=jax.ShapeDtypeStruct((len(sources), blk, width), flat[0].dtype),
        in_specs=[pl.BlockSpec(memory_space=pltpu.SMEM)]
        + [pl.BlockSpec(memory_space=pl.ANY)] * len(flat),
        out_specs=pl.BlockSpec(memory_space=pl.ANY),
        scratch_shapes=[
            pltpu.VMEM((slots, blk, width), flat[0].dtype),
            pltpu.SemaphoreType.DMA((slots,)),
            pltpu.SemaphoreType.DMA((slots,)),
        ],
        compiler_params=pltpu.CompilerParams(vmem_limit_bytes=16 << 20),
        cost_estimate=pl.CostEstimate(
            flops=0, bytes_accessed=4 * len(sources) * blk * width, transcendentals=0
        ),
        name="placed",
    )(order, *flat)
    return whole.reshape(len(sources) * blk, width)


def gather_weight(grid, weight, around=False):
    half = grid.n_dp // 2
    if around:
        column = [weight]
        for _ in range(grid.n_dp - 1):
            (came,) = yield [grid.next(column[-1], "d")]
            column.append(came)
        parts = [jnp.stack(column[:half]), jnp.stack(column[half:])]
    else:
        (column,) = yield [lax.all_gather(weight, "dp", axis=0)]
        parts = [column[:half], column[half:]]
    steps = [[parts[0]], [parts[1]]]
    for stage in (1, 0):
        counts = [grid.size(axes[stage]) for axes in HALVES]
        for k in range(1, max(counts)):
            live = [h for h in range(2) if k < counts[h]]
            came = yield [grid.next(steps[h][-1], HALVES[h][stage]) for h in live]
            for h, part in zip(live, came):
                steps[h].append(part)
        if stage == 1:
            steps = [[jnp.stack(s)] for s in steps]
    near = jnp.concatenate([p.reshape((-1,) + p.shape[-2:]) for p in steps[0] + steps[1]], 0)
    (far,) = yield [grid.next(near, "c")]
    return placed(grid.block_order(around), [near, far])


def gather_ring(grid, weight):
    part = weight
    for axis in ("a", "b"):
        steps = [part]
        for _ in range(grid.size(axis) - 1):
            (came,) = yield [grid.next(steps[-1], axis)]
            steps.append(came)
        part = jnp.stack(steps)
    near, far = [part], []
    waiting = [part]
    for k in range(grid.n_dp - 1):
        sent = [grid.next(near[-1], "d")]
        early = k == grid.n_dp // 2 - 1
        if early:
            sent.append(grid.next(jnp.stack(waiting), "c"))
            waiting = []
        came = yield sent
        if early:
            far.append(came[1])
        near.append(came[0])
        waiting.append(came[0])
    (other,) = yield [grid.next(jnp.stack(waiting), "c")]
    return placed(grid.ring_order(), near + far + [other])


def reduce_ring(grid, left, right):
    mine = left.shape[0] // 2
    (arrived,) = yield [grid.next(mm(left[mine:], right, NN).astype(BF16), "c")]
    size = mine // grid.n_dp
    held = [
        (mm(left[at : at + size], right, NN) + arrived[at : at + size].astype(F32)).astype(BF16)
        for at in range(0, mine, size)
    ]
    for axis in ("d", "b", "a"):
        count = grid.size(axis)
        total = held[1]
        for k in range(1, count):
            (came,) = yield [grid.next(total, axis)]
            total = (came.astype(F32) + held[(k + 1) % count].astype(F32)).astype(BF16)
        following = {"d": grid.n_b, "b": grid.n_a, "a": 1}[axis]
        size = total.shape[0] // following
        held = [total[at : at + size] for at in range(0, total.shape[0], size)]
    return held[0].astype(F32)


def gather_keys(grid, own):
    width = own.shape[1] // 2
    steps = [[own[:, :width]], [own[:, width:]]]
    for stage in (1, 0):
        counts = [grid.size(axes[stage]) for axes in HALVES]
        for k in range(1, max(counts)):
            live = [h for h in range(2) if k < counts[h]]
            came = yield [grid.next(steps[h][-1], HALVES[h][stage]) for h in live]
            for h, part in zip(live, came):
                steps[h].append(part)
        steps = [[jnp.stack(s)] for s in steps]
    near = [s[0] for s in steps]
    far = yield [grid.next(part, "c") for part in near]
    return tuple(
        jnp.stack([one, two]).reshape(-1, width) for one, two in zip(near, far)
    )


def reduce_keys(grid, terms):
    mine = terms.shape[0] // 2
    (came,) = yield [grid.next(terms[mine:], "c")]
    total = (terms[:mine].astype(F32) + came.astype(F32)).astype(BF16)
    for axis in ("b", "a"):
        count = grid.size(axis)
        size = total.shape[0] // count
        held = [total[at : at + size] for at in range(0, count * size, size)]
        total = held[1]
        for k in range(1, count):
            (came,) = yield [grid.next(total, axis)]
            total = (came.astype(F32) + held[(k + 1) % count].astype(F32)).astype(BF16)
    return total


class Chain:
    def __init__(self, generator):
        self.generator, self.done, self.result = generator, False, None
        self.flight = next(generator)

    def advance(self, arrived):
        try:
            self.flight = self.generator.send(arrived)
        except StopIteration as stop:
            self.done, self.result, self.flight = True, stop.value, []


def meet(main, *chains, hold=()):
    chains = [c for c in chains if not c.done]
    both = chains + [c for c in hold if not c.done]
    main, flights = lax.optimization_barrier((main, [list(c.flight) for c in both]))
    for i, (chain, flight) in enumerate(zip(both, flights)):
        chain.flight = flight
        if i < len(chains):
            chain.advance(flight)
    return main


def finish(chain):
    while not chain.done:
        chain.advance(chain.flight)
    return chain.result


def angles(positions):
    lane = jnp.arange(WIDE)
    freq = 10000.0 ** (-((lane % (HD // 2)).astype(F32) * 2.0 / HD))
    turn = positions.astype(F32)[:, None] * freq[None, :]
    sign = jnp.where(lane % HD < HD // 2, -1.0, 1.0)
    return jnp.cos(turn), jnp.sin(turn) * sign[None, :]


def normalize(rows):
    factor = lax.rsqrt(jnp.mean(rows * rows, -1, keepdims=True) + EPS)
    return (rows * factor, factor)


def norm_back(upstream, normed, factor, gain):
    scaled = upstream * gain
    inner = jnp.mean(scaled * normed, -1, keepdims=True)
    return (factor * (scaled - normed * inner), jnp.sum(upstream * normed, 0))


def body(
    n_dp,
    n_ctx,
    layer_in,
    positions,
    attn_gain,
    query_proj,
    key_proj,
    value_proj,
    merge_proj,
    ffn_gain,
    gate_proj,
    up_proj,
    down_proj,
    out_grad,
):
    _, rows, model = layer_in.shape
    kv_width = key_proj.shape[1]
    kv_heads = kv_width // HD
    width = query_proj.shape[1]
    run = rows // 2
    positions = positions[0]
    grid = Grid(n_dp, n_ctx)
    order, sum_order = grid.block_order(False), grid.block_order(True)
    ring_order, ctx_order = grid.ring_order(), grid.ctx_order()
    places = grid.value_places()

    gains = jnp.stack([attn_gain, ffn_gain], -1)
    gains = jnp.concatenate([gains, jnp.zeros((gains.shape[0], WIDE - 2), BF16)], 1)
    packed = jnp.concatenate([query_proj, key_proj, value_proj, gains], 1)
    down_chain = Chain(gather_weight(grid, down_proj))
    gate_chain = Chain(gather_weight(grid, gate_proj))
    merge_chain = Chain(gather_weight(grid, merge_proj))
    first_chain = Chain(gather_weight(grid, packed, True))
    up_chain = Chain(gather_ring(grid, up_proj))
    all_pos = lax.all_gather(positions[::run], "ctx", axis=0, tiled=True)
    cosine, sine = angles(positions)
    rows_in = layer_in.reshape(rows, model).astype(F32)
    normed_one, factor_one = normalize(rows_in)
    all_pos, factor_one = meet((all_pos, factor_one), first_chain, up_chain)
    factor_one = meet(factor_one, first_chain)
    cosine, sine = meet((cosine, sine), first_chain, up_chain)
    cosine = meet(cosine, first_chain, down_chain)
    first_weights = finish(first_chain)
    attn_all = first_weights[:, : width + 2 * kv_width]
    gain_one = first_weights[:, width + 2 * kv_width].astype(F32)
    gain_two = first_weights[:, width + 2 * kv_width + 1].astype(F32)

    first_in = (normed_one * gain_one).astype(BF16)
    first_in = meet(first_in, down_chain)
    raw = mm(first_in, attn_all, NN)
    queries, own_kv = rotated(raw, cosine, sine, kv_width)
    kv_chain = Chain(gather_keys(grid, own_kv))
    later = all_pos.reshape(n_ctx, 2)[ctx_order].reshape(2 * n_ctx, 1)
    later = later > jnp.repeat(positions[::run], run)[None, :]
    bias = jnp.where(later, MASKED, 0.0).astype(F32)
    bias = meet(bias, kv_chain)
    bias = meet(bias, kv_chain)
    bias = meet(bias, kv_chain)
    all_keys, all_values = finish(kv_chain)
    kt, vt = all_keys.T, all_values.T

    grad_rows = out_grad.reshape(rows, model)
    plan = (
        ((gate_chain, up_chain), ()),
        ((down_chain,), ()),
        ((down_chain, merge_chain, up_chain), (gate_chain,)),
        ((merge_chain, gate_chain), ()),
    )
    outs, log_sums = [], []
    for group in range(kv_heads):
        out, log_sum = attend(group, places, bias, queries, all_keys, vt)
        on, hold = plan[group % 4]
        queries, out, grad_rows = meet((queries, out, grad_rows), *on, hold=hold)
        outs.append(out)
        log_sums.append(log_sum)
    down_all = finish(down_chain)
    grad_hidden = mm(grad_rows, down_all, NT)
    outs, grad_hidden = meet((outs, grad_hidden), merge_chain, up_chain, hold=(gate_chain,))
    mixed = jnp.concatenate([out.astype(BF16) for out in outs], 1)
    mixed = meet(mixed, merge_chain, gate_chain)
    merge_all = finish(merge_chain)
    middle = rows_in + mm(mixed, merge_all, NN)
    normed_two, factor_two = normalize(middle)
    second_in = (normed_two * gain_two).astype(BF16)
    up_all = finish(up_chain)
    lift = mm(second_in, up_all, NN)
    lift = meet(lift, gate_chain)
    gate_all = finish(gate_chain)
    gate = mm(second_in, gate_all, NN)
    sigma = jax.nn.sigmoid(gate)
    activated = gate * sigma
    hidden = (activated * lift).astype(BF16)
    grad_gate = (grad_hidden * lift * sigma * (1.0 + gate * (1.0 - sigma))).astype(BF16)
    grad_lift = (grad_hidden * activated).astype(BF16)
    hidden, grad_gate, grad_lift = lax.optimization_barrier((hidden, grad_gate, grad_lift))
    second_turned = turned(second_in, order)
    gate_sum = Chain(reduce_term(grid, second_turned, grad_gate))
    up_sum = Chain(reduce_term(grid, second_turned, grad_lift))
    down_sum = Chain(reduce_ring(grid, turned(hidden, ring_order), grad_rows))
    grad_second = mm(grad_gate, gate_all, NT)
    grad_second, grad_lift = meet((grad_second, grad_lift), gate_sum)
    grad_second = grad_second + mm(grad_lift, up_all, NT)
    grad_norm_two, gain_two_term = norm_back(grad_second, normed_two, factor_two, gain_two)
    grad_middle = grad_rows.astype(F32) + grad_norm_two
    grad_branch = grad_middle.astype(BF16)
    grad_mixed = mm(grad_branch, merge_all, NT).astype(BF16)
    grad_mixed, grad_branch = meet((grad_mixed, grad_branch), down_sum, up_sum)
    first_turned = turned(first_in, order)
    mixed_turned = turned(mixed, order)

    dqs, dkvs = [], []
    for group in range(kv_heads):
        dq, dkv = attend_back(
            group, places, bias, log_sums[group], outs[group], queries, grad_mixed,
            all_keys, all_values, kt,
        )
        dqs.append(dq)
        dkvs.append(dkv)
        if group == kv_heads - 4:
            grad_mixed, dkv = meet((grad_mixed, dkv), gate_sum, down_sum)
        elif group == kv_heads - 3:
            grad_mixed, dkv, grad_branch = meet(
                (grad_mixed, dkv, grad_branch), up_sum, down_sum, hold=(gate_sum,)
            )
            merge_sum = Chain(reduce_term(grid, mixed_turned, grad_branch))
        elif group == kv_heads - 2:
            grad_mixed, dkvs = meet((grad_mixed, dkvs), gate_sum, up_sum, merge_sum, down_sum)
            keys_sum = Chain(reduce_keys(grid, jnp.concatenate(dkvs, 1)))
    dqs, dkv = meet((dqs, dkv), keys_sum, gate_sum, merge_sum, hold=(down_sum,))
    last_keys = Chain(reduce_keys(grid, dkv))
    query_grads = unrotated(unrotate_queries_kernel, dqs, cosine, sine)
    query_sum = Chain(reduce_term(grid, first_turned, query_grads))
    grad_first = mm(query_grads, attn_all[:, :width], NT)
    grad_first = meet(grad_first, last_keys, keys_sum)
    grad_first = meet(grad_first, last_keys, keys_sum, merge_sum)
    grad_first = meet(grad_first, last_keys, query_sum, down_sum)
    wide = finish(keys_sum)
    dkv_parts = [wide[:, at : at + WIDE] for at in range(0, wide.shape[1], WIDE)]
    dkv_parts.append(finish(last_keys))
    kv_grads = unrotated(unrotate_keys_kernel, dkv_parts, cosine, sine)
    grad_first = grad_first + mm(kv_grads, attn_all[:, width:], NT)
    grad_norm_one, gain_one_term = norm_back(grad_first, normed_one, factor_one, gain_one)
    gain_terms = jnp.stack([gain_one_term, gain_two_term], 0)
    gain_terms = jnp.concatenate([gain_terms, jnp.zeros((WIDE - 2, model), F32)], 0)
    gain_columns = turned(gain_terms.astype(BF16), sum_order)
    last_turned = turned(first_in, sum_order)
    last = Chain(reduce_term(grid, last_turned, kv_grads, gain_columns, around=True))
    input_grad = (grad_middle + grad_norm_one).astype(BF16).reshape(layer_in.shape)
    last.flight, input_grad = lax.optimization_barrier((last.flight, input_grad))
    input_grad = meet(input_grad, last, query_sum, up_sum, down_sum)
    input_grad, hidden = meet((input_grad, hidden), last, query_sum)
    result = middle + mm(hidden, down_all, NN)
    layer_out = result.astype(BF16).reshape(layer_in.shape)
    input_grad = meet(input_grad, last)
    input_grad, layer_out = meet((input_grad, layer_out), last, merge_sum)
    while not last.done:
        input_grad = meet(input_grad, last)
    query_share, last_share = finish(query_sum), finish(last)
    merge_share, gate_share = finish(merge_sum), finish(gate_sum)
    up_share, down_share = finish(up_sum), finish(down_sum)
    return (
        layer_out,
        input_grad,
        last_share[:, 2 * kv_width],
        query_share,
        last_share[:, :kv_width],
        last_share[:, kv_width : 2 * kv_width],
        merge_share,
        last_share[:, 2 * kv_width + 1],
        gate_share,
        up_share,
        down_share,
    )


def solution(mesh):
    acts = P("dp", "ctx", None)
    rows = P(BOTH, None)
    flat = P(BOTH)
    return jax.shard_map(
        functools.partial(body, mesh.shape["dp"], mesh.shape["ctx"]),
        mesh=mesh,
        in_specs=(acts, P("dp", "ctx"), flat, rows, rows, rows, rows, flat, rows, rows, rows, acts),
        out_specs=(acts, acts, flat, rows, rows, rows, rows, flat, rows, rows, rows),
        check_vma=False,
    )
```

```python
import functools

import jax
import jax.numpy as jnp
import numpy as np
from jax import lax
from jax.experimental import pallas as pl
from jax.experimental.pallas import tpu as pltpu
from jax.sharding import PartitionSpec as P

HD = 64
EPS = 1e-05
WIDE = 128
MASKED = -1e30
SCALE = HD**-0.5
LOG2E = 1.4426950408889634
TO_LOG2 = SCALE * LOG2E
BRIEF = pl.CostEstimate(flops=1 << 20, bytes_accessed=1 << 16, transcendentals=0)
F32 = jnp.float32
BF16 = jnp.bfloat16
NT = (((1,), (1,)), ((), ()))
NN = (((1,), (0,)), ((), ()))


def mm(left, right, dims):
    return lax.dot_general(left, right, dims, preferred_element_type=F32)


def same_run_later(keys, rows):
    run = rows // 2
    key = lax.broadcasted_iota(jnp.int32, (keys, rows), 0)
    query = lax.broadcasted_iota(jnp.int32, (keys, rows), 1)
    return (key > query) & ((key // run) == (query // run))


def split_heads(pair_ref, which, low_ref, high_ref):
    both = pair_ref[...]
    turned = pltpu.roll(both.astype(F32), HD, 1).astype(BF16)
    lane = lax.broadcasted_iota(jnp.int32, both.shape, 1)
    zero = jnp.zeros_like(both)
    first, second = (both, turned) if which == 0 else (turned, both)
    low_ref[...] = jnp.where(lane < HD, first, zero)
    high_ref[...] = jnp.where(lane < HD, zero, second)


def biased(scores, bias_ref, block, rows):
    run = rows // 2
    start = pl.multiple_of(block * rows, rows)
    parts = [
        scores[i * run : (i + 1) * run] + bias_ref[pl.ds(block * 2 + i, 1), :]
        for i in range(2)
    ]
    return jnp.concatenate(parts, 0)


def attend_kernel(
    bias_ref, q_ref, kp_ref, vt_ref, o_ref, lse_ref, low, high, vx, turned, *, which, places
):
    rows, width = q_ref.shape
    length = kp_ref.shape[0]
    blocks = length // rows
    split_heads(kp_ref, which, low, high)
    vx[:HD, :] = vt_ref[...]
    top_row = lax.broadcasted_iota(jnp.int32, (16, length), 0) == 0
    vx[HD:, :] = top_row.astype(F32).astype(BF16)

    def scores(key, pair, block):
        start = pl.multiple_of(block * rows, rows)
        column = pl.multiple_of(pair * WIDE, WIDE)
        s = mm(key[pl.ds(start, rows), :], q_ref[:, pl.ds(column, WIDE)], NT) * TO_LOG2
        return biased(s, bias_ref, block, rows)

    def weigh(probs, block):
        start = places[block] * rows
        return mm(vx[:, start : start + rows], probs.astype(BF16), NN)

    def one_pair(pair, _):
        blocked = same_run_later(rows, rows)
        state = []
        for key in (low, high):
            s = jnp.where(blocked, MASKED, scores(key, pair, 0))
            top = jnp.max(s, 0, keepdims=True)
            state.append((top, weigh(jnp.exp2(s - top), 0)))

        def step(block, state):
            raw = [scores(key, pair, block) for key in (low, high)]
            result = []
            for (top, total), s in zip(state, raw):
                new_top = jnp.maximum(top, jnp.max(s, 0, keepdims=True))
                probs = jnp.exp2(s - new_top)
                result.append((new_top, total * jnp.exp2(top - new_top) + weigh(probs, block)))
            return result

        for block in range(1, blocks):
            state = step(block, state)
        for i, (top, total) in enumerate(state):
            weight_sum = total[HD : HD + 1, :]
            turned[i * HD : (i + 1) * HD, :] = total[:HD] / weight_sum
            lse_ref[pl.ds(pair * 2 + i, 1), :] = top + jnp.log2(weight_sum)
        column = pl.multiple_of(pair * WIDE, WIDE)
        o_ref[:, pl.ds(column, WIDE)] = turned[...].T
        return 0

    lax.fori_loop(0, width // WIDE, one_pair, 0)


def attend(group, places, bias, q, keys, vt):
    rows, width = q.shape
    length = keys.shape[0]
    kv_heads = vt.shape[0] // HD
    mine = width // kv_heads
    heads = mine // HD
    return pl.pallas_call(
        functools.partial(attend_kernel, which=group % 2, places=places),
        grid=(1,),
        out_shape=(
            jax.ShapeDtypeStruct((rows, mine), F32),
            jax.ShapeDtypeStruct((heads, rows), F32),
        ),
        in_specs=[
            pl.BlockSpec(bias.shape, lambda i: (0, 0)),
            pl.BlockSpec((rows, mine), lambda i: (0, group)),
            pl.BlockSpec((length, WIDE), lambda i: (0, group // 2)),
            pl.BlockSpec((HD, length), lambda i: (group, 0)),
        ],
        out_specs=(
            pl.BlockSpec((rows, mine), lambda i: (0, 0)),
            pl.BlockSpec((heads, rows), lambda i: (0, 0)),
        ),
        scratch_shapes=[
            pltpu.VMEM((length, WIDE), BF16),
            pltpu.VMEM((length, WIDE), BF16),
            pltpu.VMEM((HD + 16, length), BF16),
            pltpu.VMEM((WIDE, rows), F32),
        ],
        compiler_params=pltpu.CompilerParams(vmem_limit_bytes=40 << 20),
        cost_estimate=BRIEF,
        name="attend",
    )(bias, q, keys, vt)


def attend_back_kernel(
    place_ref, bias_ref, lse_ref, o_ref, q_ref, g_ref, kp_ref, vp_ref, kt_ref,
    dq_ref, dkv_ref, k_low, k_high, v_low, v_high, dqt, delta_ref, *, which, unroll
):
    rows, width = q_ref.shape
    length = kp_ref.shape[0]
    blocks = length // rows
    pairs = width // WIDE
    split_heads(kp_ref, which, k_low, k_high)
    split_heads(vp_ref, which, v_low, v_high)
    row = lax.broadcasted_iota(jnp.int32, (16, WIDE), 0)
    lane = lax.broadcasted_iota(jnp.int32, (16, WIDE), 1)
    chosen = (row == lane // HD).astype(F32).astype(BF16)
    for pair in range(pairs):
        column = pl.ds(pair * WIDE, WIDE)
        product = g_ref[:, column].astype(F32) * o_ref[:, column]
        main = product.astype(BF16)
        rest = (product - main.astype(F32)).astype(BF16)
        both = mm(chosen, main, NT) + mm(chosen, rest, NT)
        delta_ref[2 * pair : 2 * pair + 2, :] = both[:2]

    def block(index, diagonal):
        start = pl.multiple_of(index * rows, rows)
        value_start = pl.multiple_of(place_ref[index] * rows, rows)

        def some_heads(i, sums):
            sums = list(sums)
            work = []
            for t in range(unroll):
                pair = i * unroll + t
                column = pl.multiple_of(pair * WIDE, WIDE)
                query = q_ref[:, pl.ds(column, WIDE)]
                grad = g_ref[:, pl.ds(column, WIDE)]
                for side, (key, value) in enumerate(((k_low, v_low), (k_high, v_high))):
                    head = pair * 2 + side
                    shift = -lse_ref[pl.ds(head, 1), :]
                    run = rows // 2
                    s = mm(key[pl.ds(start, rows), :], query, NT) * TO_LOG2
                    s = jnp.concatenate(
                        [
                            s[r * run : (r + 1) * run]
                            + (bias_ref[pl.ds(index * 2 + r, 1), :] + shift)
                            for r in range(2)
                        ],
                        0,
                    )
                    p = jnp.exp2(s)
                    if diagonal:
                        p = jnp.where(same_run_later(rows, rows), 0.0, p)
                    slope = mm(value[pl.ds(value_start, rows), :], grad, NT)
                    d = (p * (slope - delta_ref[pl.ds(head, 1), :])).astype(BF16)
                    work.append((side, pair, query, grad, p.astype(BF16), d))
            for side, pair, query, grad, p, d in work:
                sums[side] = sums[side] + mm(d, query, NN)
                sums[2 + side] = sums[2 + side] + mm(p, grad, NN)
                term = mm(kt_ref[:, pl.ds(start, rows)], d, NN)
                row = pl.multiple_of(pair * WIDE + side * HD, HD)
                if diagonal:
                    dqt[pl.ds(row, HD), :] = term
                else:
                    dqt[pl.ds(row, HD), :] += term
            return tuple(sums)

        zero = jnp.zeros((rows, WIDE), F32)
        sums = lax.fori_loop(0, pairs // unroll, some_heads, (zero,) * 4)
        lane = lax.broadcasted_iota(jnp.int32, (rows, WIDE), 1)
        key_sum = sums[0] + pltpu.roll(sums[1], HD, 1)
        value_sum = pltpu.roll(sums[2], HD, 1) + sums[3]
        dkv_ref[pl.ds(start, rows), :] = jnp.where(
            lane < HD, key_sum * SCALE, value_sum
        ).astype(BF16)

    block(0, True)

    def rest(j, _):
        block(j, False)
        return 0

    lax.fori_loop(1, blocks, rest, 0)
    for pair in range(pairs):
        dq_ref[:, pair * WIDE : (pair + 1) * WIDE] = (
            dqt[pair * WIDE : (pair + 1) * WIDE, :] * SCALE
        ).T


def attend_back(group, places, bias, lse, out, q, g, keys, values, kt, unroll=2):
    rows, width = q.shape
    length = keys.shape[0]
    kv_heads = kt.shape[0] // HD
    mine = width // kv_heads
    heads = mine // HD
    return pl.pallas_call(
        functools.partial(attend_back_kernel, which=group % 2, unroll=unroll),
        grid=(1,),
        out_shape=(
            jax.ShapeDtypeStruct((rows, mine), F32),
            jax.ShapeDtypeStruct((length, WIDE), BF16),
        ),
        in_specs=[
            pl.BlockSpec(memory_space=pltpu.SMEM),
            pl.BlockSpec(bias.shape, lambda i: (0, 0)),
            pl.BlockSpec((heads, rows), lambda i: (0, 0)),
            pl.BlockSpec((rows, mine), lambda i: (0, 0)),
            pl.BlockSpec((rows, mine), lambda i: (0, group)),
            pl.BlockSpec((rows, mine), lambda i: (0, group)),
            pl.BlockSpec((length, WIDE), lambda i: (0, group // 2)),
            pl.BlockSpec((length, WIDE), lambda i: (0, group // 2)),
            pl.BlockSpec((HD, length), lambda i: (group, 0)),
        ],
        out_specs=(
            pl.BlockSpec((rows, mine), lambda i: (0, 0)),
            pl.BlockSpec((length, WIDE), lambda i: (0, 0)),
        ),
        scratch_shapes=[pltpu.VMEM((length, WIDE), BF16)] * 4
        + [pltpu.VMEM((mine, rows), F32), pltpu.VMEM((heads, rows), F32)],
        compiler_params=pltpu.CompilerParams(vmem_limit_bytes=48 << 20),
        cost_estimate=BRIEF,
        name="attend_back",
    )(jnp.array(places, jnp.int32), bias, lse, out, q, g, keys, values, kt)


def turn_pairs(x, cosine, sine):
    lane = lax.broadcasted_iota(jnp.int32, x.shape, 1)
    swapped = jnp.where(
        lane % HD < HD // 2, pltpu.roll(x, WIDE - HD // 2, 1), pltpu.roll(x, HD // 2, 1)
    )
    return x * cosine + swapped * sine


def rotate_kernel(cos_ref, sin_ref, raw_ref, q_ref, kv_ref, *, kv_width):
    cosine, sine = cos_ref[...], sin_ref[...]
    width = q_ref.shape[1]
    for at in range(0, width, WIDE):
        q_ref[:, at : at + WIDE] = turn_pairs(raw_ref[:, at : at + WIDE], cosine, sine).astype(BF16)
    for at in range(0, kv_width, WIDE):
        column = slice(width + at, width + at + WIDE)
        kv_ref[:, at : at + WIDE] = turn_pairs(raw_ref[:, column], cosine, sine).astype(BF16)
    kv_ref[:, kv_width:] = raw_ref[:, width + kv_width :].astype(BF16)


def rotated(raw, cosine, sine, kv_width):
    rows, total = raw.shape
    return pl.pallas_call(
        functools.partial(rotate_kernel, kv_width=kv_width),
        out_shape=(
            jax.ShapeDtypeStruct((rows, total - 2 * kv_width), BF16),
            jax.ShapeDtypeStruct((rows, 2 * kv_width), BF16),
        ),
        in_specs=[pl.BlockSpec(memory_space=pltpu.VMEM)] * 3,
        out_specs=(pl.BlockSpec(memory_space=pltpu.VMEM),) * 2,
        compiler_params=pltpu.CompilerParams(vmem_limit_bytes=32 << 20),
        cost_estimate=pl.CostEstimate(
            flops=8 * raw.size, bytes_accessed=6 * raw.size, transcendentals=0
        ),
        name="rotated",
    )(cosine, sine, raw)


def unrotate_queries_kernel(cos_ref, sin_ref, *refs):
    cosine, sine = cos_ref[...], -sin_ref[...]
    out_ref = refs[-1]
    mine = refs[0].shape[1]
    for n, ref in enumerate(refs[:-1]):
        for at in range(0, mine, WIDE):
            turned = turn_pairs(ref[:, at : at + WIDE], cosine, sine)
            out_ref[:, n * mine + at : n * mine + at + WIDE] = turned.astype(BF16)


def unrotate_keys_kernel(cos_ref, sin_ref, *refs):
    cosine, sine = cos_ref[...], -sin_ref[...]
    out_ref = refs[-1]
    count = len(refs) - 1
    lane = lax.broadcasted_iota(jnp.int32, cosine.shape, 1)
    for i in range(count // 2):
        first, second = refs[2 * i][...].astype(F32), refs[2 * i + 1][...].astype(F32)
        keys = jnp.where(lane < HD, first, pltpu.roll(second, HD, 1))
        values = jnp.where(lane < HD, pltpu.roll(first, HD, 1), second)
        at = i * WIDE
        out_ref[:, at : at + WIDE] = turn_pairs(keys, cosine, sine).astype(BF16)
        at = count * HD + i * WIDE
        out_ref[:, at : at + WIDE] = values.astype(BF16)


def unrotated(kernel, parts, cosine, sine):
    rows, mine = parts[0].shape
    total = len(parts) * mine
    return pl.pallas_call(
        kernel,
        out_shape=jax.ShapeDtypeStruct((rows, total), BF16),
        in_specs=[pl.BlockSpec(memory_space=pltpu.VMEM)] * (2 + len(parts)),
        out_specs=pl.BlockSpec(memory_space=pltpu.VMEM),
        compiler_params=pltpu.CompilerParams(vmem_limit_bytes=32 << 20),
        cost_estimate=pl.CostEstimate(
            flops=8 * rows * total, bytes_accessed=6 * rows * total, transcendentals=0
        ),
        name="unrotated",
    )(cosine, sine, *parts)


BOTH = ("dp", "ctx")


class Grid:
    def __init__(self, n_dp, n_ctx):
        self.n_dp, self.n_a, self.n_b = n_dp, 2, n_ctx // 4
        self.n_ctx = n_ctx
        self.ring = [0, 1, 3, 2] if n_dp == 4 else list(range(n_dp))
        own = lax.axis_index("ctx").astype(jnp.int32)
        self.a = own // (2 * self.n_b)
        self.b = (own // 2) % self.n_b
        self.c = own % 2
        places = np.argsort(np.array(self.ring)).astype(np.int32)
        self.d = jnp.asarray(places)[lax.axis_index("dp")]

    def size(self, axis):
        return {"a": self.n_a, "b": self.n_b, "c": 2, "d": self.n_dp}[axis]

    def next(self, values, axis):
        if axis == "d":
            around = self.ring[1:] + self.ring[:1]
            return lax.ppermute(values, "dp", list(zip(self.ring, around)))
        pairs = []
        for i in range(self.n_ctx):
            a, b, c = i // (2 * self.n_b), (i // 2) % self.n_b, i % 2
            if axis == "a":
                a = (a + 1) % self.n_a
            elif axis == "b":
                b = (b + 1) % self.n_b
            else:
                c = 1 - c
            pairs.append((i, (a * self.n_b + b) * 2 + c))
        return lax.ppermute(values, "ctx", pairs)

    def natural(self, rows):
        rows = np.array(rows, np.int32)
        a = (self.a - rows[:, 2]) % self.n_a
        b = (self.b - rows[:, 3]) % self.n_b
        c = (self.c - rows[:, 0]) % 2
        return ((rows[:, 1] * self.n_a + a) * self.n_b + b) * 2 + c

    def block_order(self, around):
        half = self.n_dp // 2
        rows, hops = [], []
        for core in range(2):
            for h, (first, second) in enumerate(HALVES):
                for i in range(self.size(first)):
                    for j in range(self.size(second)):
                        for d in range(half):
                            near = {first: i, second: j}
                            at = h * half + d
                            rows.append((core, 0 if around else at, near["a"], near["b"]))
                            hops.append(at)
        return self.natural(rows) + (self.around(hops) * self.n_ctx if around else 0)

    def around(self, hops):
        ring = jnp.asarray(np.array(self.ring, np.int32))
        return ring[(self.d - np.array(hops, np.int32)) % self.n_dp]

    def ring_order(self):
        rows, hops = [], []
        for core in range(2):
            for d in range(self.n_dp):
                for b in range(self.n_b):
                    for a in range(self.n_a):
                        rows.append((core, 0, a, b))
                        hops.append(d)
        return self.natural(rows) + self.around(hops) * self.n_ctx

    def ctx_order(self):
        rows = [
            (c, 0, a, b) for c in range(2) for b in range(self.n_b) for a in range(self.n_a)
        ]
        return self.natural(rows)

    def value_places(self):
        cells = [(c, b, a) for c in range(2) for b in range(self.n_b) for a in range(self.n_a)]
        return tuple((c * self.n_a + a) * self.n_b + b for c, b, a in cells)


HALVES = (("b", "a"), ("a", "b"))


def turn_kernel(order_ref, x_ref, o_ref, held, *, blk):
    tokens, width = x_ref.shape
    for i in range(width // WIDE):
        held[i * WIDE : (i + 1) * WIDE, :] = x_ref[:, i * WIDE : (i + 1) * WIDE].T

    def move(i, _):
        source = pl.multiple_of(order_ref[i] * blk, blk)
        target = pl.multiple_of(i * blk, blk)
        o_ref[pl.ds(target, blk), :] = held[pl.ds(source, blk), :]
        return 0

    lax.fori_loop(0, width // blk, move, 0)


def turned(x, order):
    tokens, width = x.shape
    blk = width // order.shape[0]
    if blk % 16:
        blocks = jnp.take(x.T.reshape(order.shape[0], blk, tokens), order, axis=0)
        return blocks.reshape(width, tokens)
    return pl.pallas_call(
        functools.partial(turn_kernel, blk=blk),
        out_shape=jax.ShapeDtypeStruct((width, tokens), x.dtype),
        in_specs=[
            pl.BlockSpec(memory_space=pltpu.SMEM),
            pl.BlockSpec(memory_space=pltpu.VMEM),
        ],
        out_specs=pl.BlockSpec(memory_space=pltpu.VMEM),
        scratch_shapes=[pltpu.VMEM((width, tokens), x.dtype)],
        compiler_params=pltpu.CompilerParams(vmem_limit_bytes=32 << 20),
        cost_estimate=pl.CostEstimate(flops=0, bytes_accessed=4 * x.size, transcendentals=0),
        name="turned",
    )(order, x)


def reduce_term(grid, left, right, extra=None, around=False):
    rows = left.shape[0]
    mine = rows // 2

    def term(start, size):
        part = mm(left[start : start + size], right, NN)
        if extra is not None:
            part = jnp.concatenate([part, extra[start : start + size].astype(F32)], 1)
        return part

    (arrived,) = yield [grid.next(term(mine, mine).astype(BF16), "c")]
    held = []
    for h, axes in enumerate(HALVES):
        start = h * (mine // 2)
        count = grid.size(axes[0])
        size = mine // 2 // count
        held.append(
            [
                (term(at, size) + arrived[at : at + size].astype(F32)).astype(BF16)
                for at in range(start, start + count * size, size)
            ]
        )
    for step in range(2):
        totals = [None, None]
        counts = [grid.size(axes[step]) for axes in HALVES]
        for k in range(1, max(counts)):
            live = [h for h in range(2) if k < counts[h]]
            sent = [
                grid.next(held[h][1] if k == 1 else totals[h], HALVES[h][step]) for h in live
            ]
            came = yield sent
            for h, part in zip(live, came):
                own = held[h][(k + 1) % counts[h]]
                totals[h] = (part.astype(F32) + own.astype(F32)).astype(BF16)
        if step == 0:
            held = []
            for h, total in enumerate(totals):
                count = grid.size(HALVES[h][1])
                size = total.shape[0] // count
                held.append([total[j * size : (j + 1) * size] for j in range(count)])
    if not around:
        joined = jnp.concatenate(totals, 0)
        (share,) = yield [lax.psum_scatter(joined, "dp", scatter_dimension=0, tiled=True)]
        return share.astype(F32)
    half = grid.n_dp // 2
    size = totals[0].shape[0] // half
    held = [t[at : at + size] for t in totals for at in range(0, half * size, size)]
    total = held[1]
    for k in range(1, grid.n_dp):
        (came,) = yield [grid.next(total, "d")]
        total = came.astype(F32) + held[(k + 1) % grid.n_dp].astype(F32)
        total = total if k == grid.n_dp - 1 else total.astype(BF16)
    return total


def place_kernel(order_ref, *refs, sources, slots):
    pieces = refs[: -(3 + 1)]
    out_ref, held, in_sem, out_sem = refs[-4:]
    count = len(sources)

    def fetch(i):
        piece, place = sources[i]
        return pltpu.make_async_copy(
            pieces[piece].at[place], held.at[i % slots], in_sem.at[i % slots]
        )

    def store(i):
        return pltpu.make_async_copy(
            held.at[i % slots], out_ref.at[order_ref[i]], out_sem.at[i % slots]
        )

    ahead = slots // 2
    for i in range(min(ahead, count)):
        fetch(i).start()
    for i in range(count):
        fetch(i).wait()
        store(i).start()
        later = i + ahead
        if later < count:
            if later >= slots:
                store(later - slots).wait()
            fetch(later).start()
    for i in range(max(0, count - slots), count):
        store(i).wait()


def placed(order, pieces):
    blk, width = pieces[0].shape[-2:]
    flat = [p.reshape((-1, blk, width)) for p in pieces]
    sources = [(n, j) for n, p in enumerate(flat) for j in range(p.shape[0])]
    slots = 8
    whole = pl.pallas_call(
        functools.partial(place_kernel, sources=sources, slots=slots),
        out_shape=jax.ShapeDtypeStruct((len(sources), blk, width), flat[0].dtype),
        in_specs=[pl.BlockSpec(memory_space=pltpu.SMEM)]
        + [pl.BlockSpec(memory_space=pl.ANY)] * len(flat),
        out_specs=pl.BlockSpec(memory_space=pl.ANY),
        scratch_shapes=[
            pltpu.VMEM((slots, blk, width), flat[0].dtype),
            pltpu.SemaphoreType.DMA((slots,)),
            pltpu.SemaphoreType.DMA((slots,)),
        ],
        compiler_params=pltpu.CompilerParams(vmem_limit_bytes=16 << 20),
        cost_estimate=pl.CostEstimate(
            flops=0, bytes_accessed=4 * len(sources) * blk * width, transcendentals=0
        ),
        name="placed",
    )(order, *flat)
    return whole.reshape(len(sources) * blk, width)


def gather_weight(grid, weight, around=False):
    half = grid.n_dp // 2
    if around:
        column = [weight]
        for _ in range(grid.n_dp - 1):
            (came,) = yield [grid.next(column[-1], "d")]
            column.append(came)
        parts = [jnp.stack(column[:half]), jnp.stack(column[half:])]
    else:
        (column,) = yield [lax.all_gather(weight, "dp", axis=0)]
        parts = [column[:half], column[half:]]
    steps = [[parts[0]], [parts[1]]]
    for stage in (1, 0):
        counts = [grid.size(axes[stage]) for axes in HALVES]
        for k in range(1, max(counts)):
            live = [h for h in range(2) if k < counts[h]]
            came = yield [grid.next(steps[h][-1], HALVES[h][stage]) for h in live]
            for h, part in zip(live, came):
                steps[h].append(part)
        if stage == 1:
            steps = [[jnp.stack(s)] for s in steps]
    near = jnp.concatenate([p.reshape((-1,) + p.shape[-2:]) for p in steps[0] + steps[1]], 0)
    (far,) = yield [grid.next(near, "c")]
    return placed(grid.block_order(around), [near, far])


def gather_ring(grid, weight):
    part = weight
    for axis in ("a", "b"):
        steps = [part]
        for _ in range(grid.size(axis) - 1):
            (came,) = yield [grid.next(steps[-1], axis)]
            steps.append(came)
        part = jnp.stack(steps)
    near, far = [part], []
    waiting = [part]
    for k in range(grid.n_dp - 1):
        sent = [grid.next(near[-1], "d")]
        early = k == grid.n_dp // 2 - 1
        if early:
            sent.append(grid.next(jnp.stack(waiting), "c"))
            waiting = []
        came = yield sent
        if early:
            far.append(came[1])
        near.append(came[0])
        waiting.append(came[0])
    (other,) = yield [grid.next(jnp.stack(waiting), "c")]
    return placed(grid.ring_order(), near + far + [other])


def reduce_ring(grid, left, right):
    mine = left.shape[0] // 2
    (arrived,) = yield [grid.next(mm(left[mine:], right, NN).astype(BF16), "c")]
    size = mine // grid.n_dp
    held = [
        (mm(left[at : at + size], right, NN) + arrived[at : at + size].astype(F32)).astype(BF16)
        for at in range(0, mine, size)
    ]
    for axis in ("d", "b", "a"):
        count = grid.size(axis)
        total = held[1]
        for k in range(1, count):
            (came,) = yield [grid.next(total, axis)]
            total = (came.astype(F32) + held[(k + 1) % count].astype(F32)).astype(BF16)
        following = {"d": grid.n_b, "b": grid.n_a, "a": 1}[axis]
        size = total.shape[0] // following
        held = [total[at : at + size] for at in range(0, total.shape[0], size)]
    return held[0].astype(F32)


def gather_keys(grid, own):
    width = own.shape[1] // 2
    steps = [[own[:, :width]], [own[:, width:]]]
    for stage in (1, 0):
        counts = [grid.size(axes[stage]) for axes in HALVES]
        for k in range(1, max(counts)):
            live = [h for h in range(2) if k < counts[h]]
            came = yield [grid.next(steps[h][-1], HALVES[h][stage]) for h in live]
            for h, part in zip(live, came):
                steps[h].append(part)
        steps = [[jnp.stack(s)] for s in steps]
    near = [s[0] for s in steps]
    far = yield [grid.next(part, "c") for part in near]
    return tuple(
        jnp.stack([one, two]).reshape(-1, width) for one, two in zip(near, far)
    )


def reduce_keys(grid, terms):
    mine = terms.shape[0] // 2
    (came,) = yield [grid.next(terms[mine:], "c")]
    total = (terms[:mine].astype(F32) + came.astype(F32)).astype(BF16)
    for axis in ("b", "a"):
        count = grid.size(axis)
        size = total.shape[0] // count
        held = [total[at : at + size] for at in range(0, count * size, size)]
        total = held[1]
        for k in range(1, count):
            (came,) = yield [grid.next(total, axis)]
            total = (came.astype(F32) + held[(k + 1) % count].astype(F32)).astype(BF16)
    return total


class Chain:
    def __init__(self, generator):
        self.generator, self.done, self.result = generator, False, None
        self.flight = next(generator)

    def advance(self, arrived):
        try:
            self.flight = self.generator.send(arrived)
        except StopIteration as stop:
            self.done, self.result, self.flight = True, stop.value, []


def meet(main, *chains, hold=()):
    chains = [c for c in chains if not c.done]
    both = chains + [c for c in hold if not c.done]
    main, flights = lax.optimization_barrier((main, [list(c.flight) for c in both]))
    for i, (chain, flight) in enumerate(zip(both, flights)):
        chain.flight = flight
        if i < len(chains):
            chain.advance(flight)
    return main


def finish(chain):
    while not chain.done:
        chain.advance(chain.flight)
    return chain.result


def angles(positions):
    lane = jnp.arange(WIDE)
    freq = 10000.0 ** (-((lane % (HD // 2)).astype(F32) * 2.0 / HD))
    turn = positions.astype(F32)[:, None] * freq[None, :]
    sign = jnp.where(lane % HD < HD // 2, -1.0, 1.0)
    return jnp.cos(turn), jnp.sin(turn) * sign[None, :]


def normalize(rows):
    factor = lax.rsqrt(jnp.mean(rows * rows, -1, keepdims=True) + EPS)
    return (rows * factor, factor)


def norm_back(upstream, normed, factor, gain):
    scaled = upstream * gain
    inner = jnp.mean(scaled * normed, -1, keepdims=True)
    return (factor * (scaled - normed * inner), jnp.sum(upstream * normed, 0))


def body(
    n_dp,
    n_ctx,
    layer_in,
    positions,
    attn_gain,
    query_proj,
    key_proj,
    value_proj,
    merge_proj,
    ffn_gain,
    gate_proj,
    up_proj,
    down_proj,
    out_grad,
):
    _, rows, model = layer_in.shape
    kv_width = key_proj.shape[1]
    kv_heads = kv_width // HD
    width = query_proj.shape[1]
    run = rows // 2
    positions = positions[0]
    grid = Grid(n_dp, n_ctx)
    order, sum_order = grid.block_order(False), grid.block_order(True)
    ring_order, ctx_order = grid.ring_order(), grid.ctx_order()
    places = grid.value_places()

    gains = jnp.stack([attn_gain, ffn_gain], -1)
    gains = jnp.concatenate([gains, jnp.zeros((gains.shape[0], WIDE - 2), BF16)], 1)
    packed = jnp.concatenate([query_proj, key_proj, value_proj, gains], 1)
    down_chain = Chain(gather_weight(grid, down_proj))
    gate_chain = Chain(gather_weight(grid, gate_proj))
    merge_chain = Chain(gather_weight(grid, merge_proj))
    first_chain = Chain(gather_weight(grid, packed, True))
    up_chain = Chain(gather_ring(grid, up_proj))
    all_pos = lax.all_gather(positions[::run], "ctx", axis=0, tiled=True)
    cosine, sine = angles(positions)
    rows_in = layer_in.reshape(rows, model).astype(F32)
    normed_one, factor_one = normalize(rows_in)
    all_pos, factor_one = meet((all_pos, factor_one), first_chain, up_chain)
    factor_one = meet(factor_one, first_chain)
    cosine, sine = meet((cosine, sine), first_chain, up_chain)
    cosine = meet(cosine, first_chain, down_chain)
    first_weights = finish(first_chain)
    attn_all = first_weights[:, : width + 2 * kv_width]
    gain_one = first_weights[:, width + 2 * kv_width].astype(F32)
    gain_two = first_weights[:, width + 2 * kv_width + 1].astype(F32)

    first_in = (normed_one * gain_one).astype(BF16)
    first_in = meet(first_in, hold=(down_chain,))
    raw = mm(first_in, attn_all, NN)
    queries, own_kv = rotated(raw, cosine, sine, kv_width)
    kv_chain = Chain(gather_keys(grid, own_kv))
    later = all_pos.reshape(n_ctx, 2)[ctx_order].reshape(2 * n_ctx, 1)
    later = later > jnp.repeat(positions[::run], run)[None, :]
    bias = jnp.where(later, MASKED, 0.0).astype(F32)
    bias = meet(bias, kv_chain)
    bias = meet(bias, kv_chain)
    bias = meet(bias, kv_chain, down_chain, hold=(gate_chain,))
    all_keys, all_values = finish(kv_chain)
    kt, vt = all_keys.T, all_values.T

    grad_rows = out_grad.reshape(rows, model)
    plan = (
        ((gate_chain,), ()),
        ((down_chain, up_chain), ()),
        ((down_chain, merge_chain, up_chain), (gate_chain,)),
        ((merge_chain, gate_chain, up_chain), ()),
    )
    outs, log_sums = [], []
    for group in range(kv_heads):
        out, log_sum = attend(group, places, bias, queries, all_keys, vt)
        on, hold = plan[group % 4]
        queries, out, grad_rows = meet((queries, out, grad_rows), *on, hold=hold)
        if group == 2:
            down_all = finish(down_chain)
            queries, down_all = meet((queries, down_all), merge_chain, gate_chain)
            grad_hidden = mm(grad_rows, down_all, NT)
            queries, grad_hidden = lax.optimization_barrier((queries, grad_hidden))
        outs.append(out)
        log_sums.append(log_sum)
    mixed = jnp.concatenate([out.astype(BF16) for out in outs], 1)
    mixed = meet(mixed, merge_chain)
    merge_all = finish(merge_chain)
    middle = rows_in + mm(mixed, merge_all, NN)
    normed_two, factor_two = normalize(middle)
    second_in = (normed_two * gain_two).astype(BF16)
    up_all = finish(up_chain)
    lift = mm(second_in, up_all, NN)
    lift = meet(lift, gate_chain)
    gate_all = finish(gate_chain)
    gate = mm(second_in, gate_all, NN)
    sigma = jax.nn.sigmoid(gate)
    activated = gate * sigma
    hidden = (activated * lift).astype(BF16)
    grad_gate = (grad_hidden * lift * sigma * (1.0 + gate * (1.0 - sigma))).astype(BF16)
    grad_lift = (grad_hidden * activated).astype(BF16)
    hidden, grad_gate, grad_lift = lax.optimization_barrier((hidden, grad_gate, grad_lift))
    second_turned = turned(second_in, order)
    gate_sum = Chain(reduce_term(grid, second_turned, grad_gate))
    up_sum = Chain(reduce_term(grid, second_turned, grad_lift))
    down_sum = Chain(reduce_ring(grid, turned(hidden, ring_order), grad_rows))
    grad_second = mm(grad_gate, gate_all, NT)
    grad_second, grad_lift = meet((grad_second, grad_lift), gate_sum)
    grad_second = grad_second + mm(grad_lift, up_all, NT)
    grad_norm_two, gain_two_term = norm_back(grad_second, normed_two, factor_two, gain_two)
    grad_middle = grad_rows.astype(F32) + grad_norm_two
    grad_branch = grad_middle.astype(BF16)
    grad_mixed = mm(grad_branch, merge_all, NT).astype(BF16)
    grad_mixed, grad_branch = meet((grad_mixed, grad_branch), down_sum, up_sum)
    first_turned = turned(first_in, order)
    mixed_turned = turned(mixed, order)

    dqs, dkvs = [], []
    for group in range(kv_heads):
        dq, dkv = attend_back(
            group, places, bias, log_sums[group], outs[group], queries, grad_mixed,
            all_keys, all_values, kt,
        )
        dqs.append(dq)
        dkvs.append(dkv)
        if group == kv_heads - 4:
            grad_mixed, dkv = meet((grad_mixed, dkv), gate_sum, down_sum)
        elif group == kv_heads - 3:
            grad_mixed, dkv, grad_branch = meet(
                (grad_mixed, dkv, grad_branch), up_sum, down_sum, hold=(gate_sum,)
            )
            merge_sum = Chain(reduce_term(grid, mixed_turned, grad_branch))
        elif group == kv_heads - 2:
            grad_mixed, dkvs = meet((grad_mixed, dkvs), gate_sum, up_sum, merge_sum, down_sum)
            keys_sum = Chain(reduce_keys(grid, jnp.concatenate(dkvs, 1)))
    dqs, dkv = meet((dqs, dkv), keys_sum, gate_sum, merge_sum, hold=(down_sum,))
    last_keys = Chain(reduce_keys(grid, dkv))
    query_grads = unrotated(unrotate_queries_kernel, dqs, cosine, sine)
    query_sum = Chain(reduce_term(grid, first_turned, query_grads))
    grad_first = mm(query_grads, attn_all[:, :width], NT)
    grad_first = meet(grad_first, last_keys, keys_sum, down_sum, hold=(query_sum,))
    grad_first = meet(grad_first, last_keys, keys_sum, merge_sum)
    grad_first = meet(grad_first, last_keys, query_sum, down_sum)
    wide = finish(keys_sum)
    dkv_parts = [wide[:, at : at + WIDE] for at in range(0, wide.shape[1], WIDE)]
    dkv_parts.append(finish(last_keys))
    kv_grads = unrotated(unrotate_keys_kernel, dkv_parts, cosine, sine)
    grad_first = grad_first + mm(kv_grads, attn_all[:, width:], NT)
    grad_norm_one, gain_one_term = norm_back(grad_first, normed_one, factor_one, gain_one)
    gain_terms = jnp.stack([gain_one_term, gain_two_term], 0)
    gain_terms = jnp.concatenate([gain_terms, jnp.zeros((WIDE - 2, model), F32)], 0)
    gain_columns = turned(gain_terms.astype(BF16), sum_order)
    last_turned = turned(first_in, sum_order)
    last = Chain(reduce_term(grid, last_turned, kv_grads, gain_columns, around=True))
    input_grad = (grad_middle + grad_norm_one).astype(BF16).reshape(layer_in.shape)
    last.flight, input_grad = lax.optimization_barrier((last.flight, input_grad))
    input_grad = meet(input_grad, last, query_sum, up_sum, down_sum)
    input_grad, hidden = meet((input_grad, hidden), last, query_sum)
    result = middle + mm(hidden, down_all, NN)
    layer_out = result.astype(BF16).reshape(layer_in.shape)
    input_grad = meet(input_grad, last)
    input_grad, layer_out = meet((input_grad, layer_out), last, merge_sum)
    while not last.done:
        input_grad = meet(input_grad, last)
    query_share, last_share = finish(query_sum), finish(last)
    merge_share, gate_share = finish(merge_sum), finish(gate_sum)
    up_share, down_share = finish(up_sum), finish(down_sum)
    return (
        layer_out,
        input_grad,
        last_share[:, 2 * kv_width],
        query_share,
        last_share[:, :kv_width],
        last_share[:, kv_width : 2 * kv_width],
        merge_share,
        last_share[:, 2 * kv_width + 1],
        gate_share,
        up_share,
        down_share,
    )


def solution(mesh):
    acts = P("dp", "ctx", None)
    rows = P(BOTH, None)
    flat = P(BOTH)
    return jax.shard_map(
        functools.partial(body, mesh.shape["dp"], mesh.shape["ctx"]),
        mesh=mesh,
        in_specs=(acts, P("dp", "ctx"), flat, rows, rows, rows, rows, flat, rows, rows, rows, acts),
        out_specs=(acts, acts, flat, rows, rows, rows, rows, flat, rows, rows, rows),
        check_vma=False,
    )
```

```python
import functools

import jax
import jax.numpy as jnp
import numpy as np
from jax import lax
from jax.experimental import pallas as pl
from jax.experimental.pallas import tpu as pltpu
from jax.sharding import PartitionSpec as P

HD = 64
EPS = 1e-05
WIDE = 128
MASKED = -1e30
SCALE = HD**-0.5
LOG2E = 1.4426950408889634
TO_LOG2 = SCALE * LOG2E
BRIEF = pl.CostEstimate(flops=1 << 20, bytes_accessed=1 << 16, transcendentals=0)
F32 = jnp.float32
BF16 = jnp.bfloat16
NT = (((1,), (1,)), ((), ()))
NN = (((1,), (0,)), ((), ()))


def mm(left, right, dims):
    return lax.dot_general(left, right, dims, preferred_element_type=F32)


def same_run_later(keys, rows):
    run = rows // 2
    key = lax.broadcasted_iota(jnp.int32, (keys, rows), 0)
    query = lax.broadcasted_iota(jnp.int32, (keys, rows), 1)
    return (key > query) & ((key // run) == (query // run))


def split_heads(pair_ref, which, low_ref, high_ref):
    both = pair_ref[...]
    turned = pltpu.roll(both.astype(F32), HD, 1).astype(BF16)
    lane = lax.broadcasted_iota(jnp.int32, both.shape, 1)
    zero = jnp.zeros_like(both)
    first, second = (both, turned) if which == 0 else (turned, both)
    low_ref[...] = jnp.where(lane < HD, first, zero)
    high_ref[...] = jnp.where(lane < HD, zero, second)


def biased(scores, bias_ref, block, rows):
    run = rows // 2
    start = pl.multiple_of(block * rows, rows)
    parts = [
        scores[i * run : (i + 1) * run] + bias_ref[pl.ds(block * 2 + i, 1), :]
        for i in range(2)
    ]
    return jnp.concatenate(parts, 0)


def attend_kernel(
    bias_ref, q_ref, kp_ref, vt_ref, o_ref, lse_ref, low, high, vx, turned, *, which, places
):
    rows, width = q_ref.shape
    length = kp_ref.shape[0]
    blocks = length // rows
    split_heads(kp_ref, which, low, high)
    vx[:HD, :] = vt_ref[...]
    top_row = lax.broadcasted_iota(jnp.int32, (16, length), 0) == 0
    vx[HD:, :] = top_row.astype(F32).astype(BF16)

    def scores(key, pair, block):
        start = pl.multiple_of(block * rows, rows)
        column = pl.multiple_of(pair * WIDE, WIDE)
        s = mm(key[pl.ds(start, rows), :], q_ref[:, pl.ds(column, WIDE)], NT) * TO_LOG2
        return biased(s, bias_ref, block, rows)

    def weigh(probs, block):
        start = places[block] * rows
        return mm(vx[:, start : start + rows], probs.astype(BF16), NN)

    def one_pair(pair, _):
        blocked = same_run_later(rows, rows)
        state = []
        for key in (low, high):
            s = jnp.where(blocked, MASKED, scores(key, pair, 0))
            top = jnp.max(s, 0, keepdims=True)
            state.append((top, weigh(jnp.exp2(s - top), 0)))

        def step(block, state):
            raw = [scores(key, pair, block) for key in (low, high)]
            result = []
            for (top, total), s in zip(state, raw):
                new_top = jnp.maximum(top, jnp.max(s, 0, keepdims=True))
                probs = jnp.exp2(s - new_top)
                result.append((new_top, total * jnp.exp2(top - new_top) + weigh(probs, block)))
            return result

        for block in range(1, blocks):
            state = step(block, state)
        for i, (top, total) in enumerate(state):
            weight_sum = total[HD : HD + 1, :]
            turned[i * HD : (i + 1) * HD, :] = total[:HD] / weight_sum
            lse_ref[pl.ds(pair * 2 + i, 1), :] = top + jnp.log2(weight_sum)
        column = pl.multiple_of(pair * WIDE, WIDE)
        o_ref[:, pl.ds(column, WIDE)] = turned[...].T
        return 0

    lax.fori_loop(0, width // WIDE, one_pair, 0)


def attend(group, places, bias, q, keys, vt):
    rows, width = q.shape
    length = keys.shape[0]
    kv_heads = vt.shape[0] // HD
    mine = width // kv_heads
    heads = mine // HD
    return pl.pallas_call(
        functools.partial(attend_kernel, which=group % 2, places=places),
        grid=(1,),
        out_shape=(
            jax.ShapeDtypeStruct((rows, mine), F32),
            jax.ShapeDtypeStruct((heads, rows), F32),
        ),
        in_specs=[
            pl.BlockSpec(bias.shape, lambda i: (0, 0)),
            pl.BlockSpec((rows, mine), lambda i: (0, group)),
            pl.BlockSpec((length, WIDE), lambda i: (0, group // 2)),
            pl.BlockSpec((HD, length), lambda i: (group, 0)),
        ],
        out_specs=(
            pl.BlockSpec((rows, mine), lambda i: (0, 0)),
            pl.BlockSpec((heads, rows), lambda i: (0, 0)),
        ),
        scratch_shapes=[
            pltpu.VMEM((length, WIDE), BF16),
            pltpu.VMEM((length, WIDE), BF16),
            pltpu.VMEM((HD + 16, length), BF16),
            pltpu.VMEM((WIDE, rows), F32),
        ],
        compiler_params=pltpu.CompilerParams(vmem_limit_bytes=40 << 20),
        cost_estimate=BRIEF,
        name="attend",
    )(bias, q, keys, vt)


def attend_back_kernel(
    place_ref, bias_ref, lse_ref, o_ref, q_ref, g_ref, kp_ref, vp_ref, kt_ref,
    dq_ref, dkv_ref, k_low, k_high, v_low, v_high, dqt, delta_ref, *, which, unroll
):
    rows, width = q_ref.shape
    length = kp_ref.shape[0]
    blocks = length // rows
    pairs = width // WIDE
    split_heads(kp_ref, which, k_low, k_high)
    split_heads(vp_ref, which, v_low, v_high)
    row = lax.broadcasted_iota(jnp.int32, (16, WIDE), 0)
    lane = lax.broadcasted_iota(jnp.int32, (16, WIDE), 1)
    chosen = (row == lane // HD).astype(F32).astype(BF16)
    for pair in range(pairs):
        column = pl.ds(pair * WIDE, WIDE)
        product = g_ref[:, column].astype(F32) * o_ref[:, column]
        main = product.astype(BF16)
        rest = (product - main.astype(F32)).astype(BF16)
        both = mm(chosen, main, NT) + mm(chosen, rest, NT)
        delta_ref[2 * pair : 2 * pair + 2, :] = both[:2]

    def block(index, diagonal):
        start = pl.multiple_of(index * rows, rows)
        value_start = pl.multiple_of(place_ref[index] * rows, rows)

        def some_heads(i, sums):
            sums = list(sums)
            work = []
            for t in range(unroll):
                pair = i * unroll + t
                column = pl.multiple_of(pair * WIDE, WIDE)
                query = q_ref[:, pl.ds(column, WIDE)]
                grad = g_ref[:, pl.ds(column, WIDE)]
                for side, (key, value) in enumerate(((k_low, v_low), (k_high, v_high))):
                    head = pair * 2 + side
                    shift = -lse_ref[pl.ds(head, 1), :]
                    run = rows // 2
                    s = mm(key[pl.ds(start, rows), :], query, NT) * TO_LOG2
                    s = jnp.concatenate(
                        [
                            s[r * run : (r + 1) * run]
                            + (bias_ref[pl.ds(index * 2 + r, 1), :] + shift)
                            for r in range(2)
                        ],
                        0,
                    )
                    p = jnp.exp2(s)
                    if diagonal:
                        p = jnp.where(same_run_later(rows, rows), 0.0, p)
                    slope = mm(value[pl.ds(value_start, rows), :], grad, NT)
                    d = (p * (slope - delta_ref[pl.ds(head, 1), :])).astype(BF16)
                    work.append((side, pair, query, grad, p.astype(BF16), d))
            for side, pair, query, grad, p, d in work:
                sums[side] = sums[side] + mm(d, query, NN)
                sums[2 + side] = sums[2 + side] + mm(p, grad, NN)
                term = mm(kt_ref[:, pl.ds(start, rows)], d, NN)
                row = pl.multiple_of(pair * WIDE + side * HD, HD)
                if diagonal:
                    dqt[pl.ds(row, HD), :] = term
                else:
                    dqt[pl.ds(row, HD), :] += term
            return tuple(sums)

        zero = jnp.zeros((rows, WIDE), F32)
        sums = lax.fori_loop(0, pairs // unroll, some_heads, (zero,) * 4)
        lane = lax.broadcasted_iota(jnp.int32, (rows, WIDE), 1)
        key_sum = sums[0] + pltpu.roll(sums[1], HD, 1)
        value_sum = pltpu.roll(sums[2], HD, 1) + sums[3]
        dkv_ref[pl.ds(start, rows), :] = jnp.where(
            lane < HD, key_sum * SCALE, value_sum
        ).astype(BF16)

    block(0, True)

    def rest(j, _):
        block(j, False)
        return 0

    lax.fori_loop(1, blocks, rest, 0)
    for pair in range(pairs):
        dq_ref[:, pair * WIDE : (pair + 1) * WIDE] = (
            dqt[pair * WIDE : (pair + 1) * WIDE, :] * SCALE
        ).T


def attend_back(group, places, bias, lse, out, q, g, keys, values, kt, unroll=2):
    rows, width = q.shape
    length = keys.shape[0]
    kv_heads = kt.shape[0] // HD
    mine = width // kv_heads
    heads = mine // HD
    return pl.pallas_call(
        functools.partial(attend_back_kernel, which=group % 2, unroll=unroll),
        grid=(1,),
        out_shape=(
            jax.ShapeDtypeStruct((rows, mine), F32),
            jax.ShapeDtypeStruct((length, WIDE), BF16),
        ),
        in_specs=[
            pl.BlockSpec(memory_space=pltpu.SMEM),
            pl.BlockSpec(bias.shape, lambda i: (0, 0)),
            pl.BlockSpec((heads, rows), lambda i: (0, 0)),
            pl.BlockSpec((rows, mine), lambda i: (0, 0)),
            pl.BlockSpec((rows, mine), lambda i: (0, group)),
            pl.BlockSpec((rows, mine), lambda i: (0, group)),
            pl.BlockSpec((length, WIDE), lambda i: (0, group // 2)),
            pl.BlockSpec((length, WIDE), lambda i: (0, group // 2)),
            pl.BlockSpec((HD, length), lambda i: (group, 0)),
        ],
        out_specs=(
            pl.BlockSpec((rows, mine), lambda i: (0, 0)),
            pl.BlockSpec((length, WIDE), lambda i: (0, 0)),
        ),
        scratch_shapes=[pltpu.VMEM((length, WIDE), BF16)] * 4
        + [pltpu.VMEM((mine, rows), F32), pltpu.VMEM((heads, rows), F32)],
        compiler_params=pltpu.CompilerParams(vmem_limit_bytes=48 << 20),
        cost_estimate=BRIEF,
        name="attend_back",
    )(jnp.array(places, jnp.int32), bias, lse, out, q, g, keys, values, kt)


def turn_pairs(x, cosine, sine):
    lane = lax.broadcasted_iota(jnp.int32, x.shape, 1)
    swapped = jnp.where(
        lane % HD < HD // 2, pltpu.roll(x, WIDE - HD // 2, 1), pltpu.roll(x, HD // 2, 1)
    )
    return x * cosine + swapped * sine


def rotate_kernel(cos_ref, sin_ref, raw_ref, q_ref, kv_ref, *, kv_width):
    cosine, sine = cos_ref[...], sin_ref[...]
    width = q_ref.shape[1]
    for at in range(0, width, WIDE):
        q_ref[:, at : at + WIDE] = turn_pairs(raw_ref[:, at : at + WIDE], cosine, sine).astype(BF16)
    for at in range(0, kv_width, WIDE):
        column = slice(width + at, width + at + WIDE)
        kv_ref[:, at : at + WIDE] = turn_pairs(raw_ref[:, column], cosine, sine).astype(BF16)
    kv_ref[:, kv_width:] = raw_ref[:, width + kv_width :].astype(BF16)


def rotated(raw, cosine, sine, kv_width):
    rows, total = raw.shape
    return pl.pallas_call(
        functools.partial(rotate_kernel, kv_width=kv_width),
        out_shape=(
            jax.ShapeDtypeStruct((rows, total - 2 * kv_width), BF16),
            jax.ShapeDtypeStruct((rows, 2 * kv_width), BF16),
        ),
        in_specs=[pl.BlockSpec(memory_space=pltpu.VMEM)] * 3,
        out_specs=(pl.BlockSpec(memory_space=pltpu.VMEM),) * 2,
        compiler_params=pltpu.CompilerParams(vmem_limit_bytes=32 << 20),
        cost_estimate=pl.CostEstimate(
            flops=8 * raw.size, bytes_accessed=6 * raw.size, transcendentals=0
        ),
        name="rotated",
    )(cosine, sine, raw)


def unrotate_queries_kernel(cos_ref, sin_ref, *refs):
    cosine, sine = cos_ref[...], -sin_ref[...]
    out_ref = refs[-1]
    mine = refs[0].shape[1]
    for n, ref in enumerate(refs[:-1]):
        for at in range(0, mine, WIDE):
            turned = turn_pairs(ref[:, at : at + WIDE], cosine, sine)
            out_ref[:, n * mine + at : n * mine + at + WIDE] = turned.astype(BF16)


def unrotate_keys_kernel(cos_ref, sin_ref, *refs):
    cosine, sine = cos_ref[...], -sin_ref[...]
    out_ref = refs[-1]
    count = len(refs) - 1
    lane = lax.broadcasted_iota(jnp.int32, cosine.shape, 1)
    for i in range(count // 2):
        first, second = refs[2 * i][...].astype(F32), refs[2 * i + 1][...].astype(F32)
        keys = jnp.where(lane < HD, first, pltpu.roll(second, HD, 1))
        values = jnp.where(lane < HD, pltpu.roll(first, HD, 1), second)
        at = i * WIDE
        out_ref[:, at : at + WIDE] = turn_pairs(keys, cosine, sine).astype(BF16)
        at = count * HD + i * WIDE
        out_ref[:, at : at + WIDE] = values.astype(BF16)


def unrotated(kernel, parts, cosine, sine):
    rows, mine = parts[0].shape
    total = len(parts) * mine
    return pl.pallas_call(
        kernel,
        out_shape=jax.ShapeDtypeStruct((rows, total), BF16),
        in_specs=[pl.BlockSpec(memory_space=pltpu.VMEM)] * (2 + len(parts)),
        out_specs=pl.BlockSpec(memory_space=pltpu.VMEM),
        compiler_params=pltpu.CompilerParams(vmem_limit_bytes=32 << 20),
        cost_estimate=pl.CostEstimate(
            flops=8 * rows * total, bytes_accessed=6 * rows * total, transcendentals=0
        ),
        name="unrotated",
    )(cosine, sine, *parts)


BOTH = ("dp", "ctx")


class Grid:
    def __init__(self, n_dp, n_ctx):
        self.n_dp, self.n_a, self.n_b = n_dp, 2, n_ctx // 4
        self.n_ctx = n_ctx
        self.ring = [0, 1, 3, 2] if n_dp == 4 else list(range(n_dp))
        own = lax.axis_index("ctx").astype(jnp.int32)
        self.a = own // (2 * self.n_b)
        self.b = (own // 2) % self.n_b
        self.c = own % 2
        places = np.argsort(np.array(self.ring)).astype(np.int32)
        self.d = jnp.asarray(places)[lax.axis_index("dp")]

    def size(self, axis):
        return {"a": self.n_a, "b": self.n_b, "c": 2, "d": self.n_dp}[axis]

    def next(self, values, axis):
        if axis == "d":
            around = self.ring[1:] + self.ring[:1]
            return lax.ppermute(values, "dp", list(zip(self.ring, around)))
        pairs = []
        for i in range(self.n_ctx):
            a, b, c = i // (2 * self.n_b), (i // 2) % self.n_b, i % 2
            if axis == "a":
                a = (a + 1) % self.n_a
            elif axis == "b":
                b = (b + 1) % self.n_b
            else:
                c = 1 - c
            pairs.append((i, (a * self.n_b + b) * 2 + c))
        return lax.ppermute(values, "ctx", pairs)

    def natural(self, rows):
        rows = np.array(rows, np.int32)
        a = (self.a - rows[:, 2]) % self.n_a
        b = (self.b - rows[:, 3]) % self.n_b
        c = (self.c - rows[:, 0]) % 2
        return ((rows[:, 1] * self.n_a + a) * self.n_b + b) * 2 + c

    def block_order(self, around):
        half = self.n_dp // 2
        rows, hops = [], []
        for core in range(2):
            for h, (first, second) in enumerate(HALVES):
                for i in range(self.size(first)):
                    for j in range(self.size(second)):
                        for d in range(half):
                            near = {first: i, second: j}
                            at = h * half + d
                            rows.append((core, 0 if around else at, near["a"], near["b"]))
                            hops.append(at)
        return self.natural(rows) + (self.around(hops) * self.n_ctx if around else 0)

    def around(self, hops):
        ring = jnp.asarray(np.array(self.ring, np.int32))
        return ring[(self.d - np.array(hops, np.int32)) % self.n_dp]

    def ring_order(self):
        rows, hops = [], []
        for core in range(2):
            for d in range(self.n_dp):
                for b in range(self.n_b):
                    for a in range(self.n_a):
                        rows.append((core, 0, a, b))
                        hops.append(d)
        return self.natural(rows) + self.around(hops) * self.n_ctx

    def ctx_order(self):
        rows = [
            (c, 0, a, b) for c in range(2) for b in range(self.n_b) for a in range(self.n_a)
        ]
        return self.natural(rows)

    def value_places(self):
        cells = [(c, b, a) for c in range(2) for b in range(self.n_b) for a in range(self.n_a)]
        return tuple((c * self.n_a + a) * self.n_b + b for c, b, a in cells)


HALVES = (("b", "a"), ("a", "b"))


def turn_kernel(order_ref, x_ref, o_ref, held, *, blk):
    tokens, width = x_ref.shape
    for i in range(width // WIDE):
        held[i * WIDE : (i + 1) * WIDE, :] = x_ref[:, i * WIDE : (i + 1) * WIDE].T

    def move(i, _):
        source = pl.multiple_of(order_ref[i] * blk, blk)
        target = pl.multiple_of(i * blk, blk)
        o_ref[pl.ds(target, blk), :] = held[pl.ds(source, blk), :]
        return 0

    lax.fori_loop(0, width // blk, move, 0)


def turned(x, order):
    tokens, width = x.shape
    blk = width // order.shape[0]
    if blk % 16:
        blocks = jnp.take(x.T.reshape(order.shape[0], blk, tokens), order, axis=0)
        return blocks.reshape(width, tokens)
    return pl.pallas_call(
        functools.partial(turn_kernel, blk=blk),
        out_shape=jax.ShapeDtypeStruct((width, tokens), x.dtype),
        in_specs=[
            pl.BlockSpec(memory_space=pltpu.SMEM),
            pl.BlockSpec(memory_space=pltpu.VMEM),
        ],
        out_specs=pl.BlockSpec(memory_space=pltpu.VMEM),
        scratch_shapes=[pltpu.VMEM((width, tokens), x.dtype)],
        compiler_params=pltpu.CompilerParams(vmem_limit_bytes=32 << 20),
        cost_estimate=pl.CostEstimate(flops=0, bytes_accessed=4 * x.size, transcendentals=0),
        name="turned",
    )(order, x)


def reduce_term(grid, left, right, extra=None, around=False):
    rows = left.shape[0]
    mine = rows // 2

    def term(start, size):
        part = mm(left[start : start + size], right, NN)
        if extra is not None:
            part = jnp.concatenate([part, extra[start : start + size].astype(F32)], 1)
        return part

    (arrived,) = yield [grid.next(term(mine, mine).astype(BF16), "c")]
    held = []
    for h, axes in enumerate(HALVES):
        start = h * (mine // 2)
        count = grid.size(axes[0])
        size = mine // 2 // count
        held.append(
            [
                (term(at, size) + arrived[at : at + size].astype(F32)).astype(BF16)
                for at in range(start, start + count * size, size)
            ]
        )
    for step in range(2):
        totals = [None, None]
        counts = [grid.size(axes[step]) for axes in HALVES]
        for k in range(1, max(counts)):
            live = [h for h in range(2) if k < counts[h]]
            sent = [
                grid.next(held[h][1] if k == 1 else totals[h], HALVES[h][step]) for h in live
            ]
            came = yield sent
            for h, part in zip(live, came):
                own = held[h][(k + 1) % counts[h]]
                totals[h] = (part.astype(F32) + own.astype(F32)).astype(BF16)
        if step == 0:
            held = []
            for h, total in enumerate(totals):
                count = grid.size(HALVES[h][1])
                size = total.shape[0] // count
                held.append([total[j * size : (j + 1) * size] for j in range(count)])
    if not around:
        joined = jnp.concatenate(totals, 0)
        (share,) = yield [lax.psum_scatter(joined, "dp", scatter_dimension=0, tiled=True)]
        return share.astype(F32)
    half = grid.n_dp // 2
    size = totals[0].shape[0] // half
    held = [t[at : at + size] for t in totals for at in range(0, half * size, size)]
    total = held[1]
    for k in range(1, grid.n_dp):
        (came,) = yield [grid.next(total, "d")]
        total = came.astype(F32) + held[(k + 1) % grid.n_dp].astype(F32)
        total = total if k == grid.n_dp - 1 else total.astype(BF16)
    return total


def place_kernel(order_ref, *refs, sources, slots):
    pieces = refs[: -(3 + 1)]
    out_ref, held, in_sem, out_sem = refs[-4:]
    count = len(sources)

    def fetch(i):
        piece, place = sources[i]
        return pltpu.make_async_copy(
            pieces[piece].at[place], held.at[i % slots], in_sem.at[i % slots]
        )

    def store(i):
        return pltpu.make_async_copy(
            held.at[i % slots], out_ref.at[order_ref[i]], out_sem.at[i % slots]
        )

    ahead = slots // 2
    for i in range(min(ahead, count)):
        fetch(i).start()
    for i in range(count):
        fetch(i).wait()
        store(i).start()
        later = i + ahead
        if later < count:
            if later >= slots:
                store(later - slots).wait()
            fetch(later).start()
    for i in range(max(0, count - slots), count):
        store(i).wait()


def placed(order, pieces):
    blk, width = pieces[0].shape[-2:]
    flat = [p.reshape((-1, blk, width)) for p in pieces]
    sources = [(n, j) for n, p in enumerate(flat) for j in range(p.shape[0])]
    slots = 8
    whole = pl.pallas_call(
        functools.partial(place_kernel, sources=sources, slots=slots),
        out_shape=jax.ShapeDtypeStruct((len(sources), blk, width), flat[0].dtype),
        in_specs=[pl.BlockSpec(memory_space=pltpu.SMEM)]
        + [pl.BlockSpec(memory_space=pl.ANY)] * len(flat),
        out_specs=pl.BlockSpec(memory_space=pl.ANY),
        scratch_shapes=[
            pltpu.VMEM((slots, blk, width), flat[0].dtype),
            pltpu.SemaphoreType.DMA((slots,)),
            pltpu.SemaphoreType.DMA((slots,)),
        ],
        compiler_params=pltpu.CompilerParams(vmem_limit_bytes=16 << 20),
        cost_estimate=pl.CostEstimate(
            flops=0, bytes_accessed=4 * len(sources) * blk * width, transcendentals=0
        ),
        name="placed",
    )(order, *flat)
    return whole.reshape(len(sources) * blk, width)


def gather_weight(grid, weight, around=False):
    half = grid.n_dp // 2
    if around:
        column = [weight]
        for _ in range(grid.n_dp - 1):
            (came,) = yield [grid.next(column[-1], "d")]
            column.append(came)
        parts = [jnp.stack(column[:half]), jnp.stack(column[half:])]
    else:
        (column,) = yield [lax.all_gather(weight, "dp", axis=0)]
        parts = [column[:half], column[half:]]
    steps = [[parts[0]], [parts[1]]]
    for stage in (1, 0):
        counts = [grid.size(axes[stage]) for axes in HALVES]
        for k in range(1, max(counts)):
            live = [h for h in range(2) if k < counts[h]]
            came = yield [grid.next(steps[h][-1], HALVES[h][stage]) for h in live]
            for h, part in zip(live, came):
                steps[h].append(part)
        if stage == 1:
            steps = [[jnp.stack(s)] for s in steps]
    near = jnp.concatenate([p.reshape((-1,) + p.shape[-2:]) for p in steps[0] + steps[1]], 0)
    (far,) = yield [grid.next(near, "c")]
    return placed(grid.block_order(around), [near, far])


def gather_ring(grid, weight):
    part = weight
    for axis in ("a", "b"):
        steps = [part]
        for _ in range(grid.size(axis) - 1):
            (came,) = yield [grid.next(steps[-1], axis)]
            steps.append(came)
        part = jnp.stack(steps)
    near, far = [part], []
    waiting = [part]
    for k in range(grid.n_dp - 1):
        sent = [grid.next(near[-1], "d")]
        early = k == grid.n_dp - 2
        if early:
            sent.append(grid.next(jnp.stack(waiting[:-1]), "c"))
            waiting = waiting[-1:]
        came = yield sent
        if early:
            far.append(came[1])
        near.append(came[0])
        waiting.append(came[0])
    (other,) = yield [grid.next(jnp.stack(waiting), "c")]
    return placed(grid.ring_order(), near + far + [other])


def reduce_ring(grid, left, right):
    mine = left.shape[0] // 2
    (arrived,) = yield [grid.next(mm(left[mine:], right, NN).astype(BF16), "c")]
    size = mine // grid.n_dp
    held = [
        (mm(left[at : at + size], right, NN) + arrived[at : at + size].astype(F32)).astype(BF16)
        for at in range(0, mine, size)
    ]
    for axis in ("d", "b", "a"):
        count = grid.size(axis)
        total = held[1]
        for k in range(1, count):
            (came,) = yield [grid.next(total, axis)]
            total = (came.astype(F32) + held[(k + 1) % count].astype(F32)).astype(BF16)
        following = {"d": grid.n_b, "b": grid.n_a, "a": 1}[axis]
        size = total.shape[0] // following
        held = [total[at : at + size] for at in range(0, total.shape[0], size)]
    return held[0].astype(F32)


def gather_keys(grid, own):
    width = own.shape[1] // 2
    steps = [[own[:, :width]], [own[:, width:]]]
    for stage in (1, 0):
        counts = [grid.size(axes[stage]) for axes in HALVES]
        for k in range(1, max(counts)):
            live = [h for h in range(2) if k < counts[h]]
            came = yield [grid.next(steps[h][-1], HALVES[h][stage]) for h in live]
            for h, part in zip(live, came):
                steps[h].append(part)
        steps = [[jnp.stack(s)] for s in steps]
    near = [s[0] for s in steps]
    far = yield [grid.next(part, "c") for part in near]
    return tuple(
        jnp.stack([one, two]).reshape(-1, width) for one, two in zip(near, far)
    )


def reduce_keys(grid, terms):
    mine = terms.shape[0] // 2
    (came,) = yield [grid.next(terms[mine:], "c")]
    total = (terms[:mine].astype(F32) + came.astype(F32)).astype(BF16)
    for axis in ("b", "a"):
        count = grid.size(axis)
        size = total.shape[0] // count
        held = [total[at : at + size] for at in range(0, count * size, size)]
        total = held[1]
        for k in range(1, count):
            (came,) = yield [grid.next(total, axis)]
            total = (came.astype(F32) + held[(k + 1) % count].astype(F32)).astype(BF16)
    return total


class Chain:
    def __init__(self, generator):
        self.generator, self.done, self.result = generator, False, None
        self.flight = next(generator)

    def advance(self, arrived):
        try:
            self.flight = self.generator.send(arrived)
        except StopIteration as stop:
            self.done, self.result, self.flight = True, stop.value, []


def meet(main, *chains, hold=()):
    chains = [c for c in chains if not c.done]
    both = chains + [c for c in hold if not c.done]
    main, flights = lax.optimization_barrier((main, [list(c.flight) for c in both]))
    for i, (chain, flight) in enumerate(zip(both, flights)):
        chain.flight = flight
        if i < len(chains):
            chain.advance(flight)
    return main


def finish(chain):
    while not chain.done:
        chain.advance(chain.flight)
    return chain.result


def angles(positions):
    lane = jnp.arange(WIDE)
    freq = 10000.0 ** (-((lane % (HD // 2)).astype(F32) * 2.0 / HD))
    turn = positions.astype(F32)[:, None] * freq[None, :]
    sign = jnp.where(lane % HD < HD // 2, -1.0, 1.0)
    return jnp.cos(turn), jnp.sin(turn) * sign[None, :]


def normalize(rows):
    factor = lax.rsqrt(jnp.mean(rows * rows, -1, keepdims=True) + EPS)
    return (rows * factor, factor)


def norm_back(upstream, normed, factor, gain):
    scaled = upstream * gain
    inner = jnp.mean(scaled * normed, -1, keepdims=True)
    return (factor * (scaled - normed * inner), jnp.sum(upstream * normed, 0))


def body(
    n_dp,
    n_ctx,
    layer_in,
    positions,
    attn_gain,
    query_proj,
    key_proj,
    value_proj,
    merge_proj,
    ffn_gain,
    gate_proj,
    up_proj,
    down_proj,
    out_grad,
):
    _, rows, model = layer_in.shape
    kv_width = key_proj.shape[1]
    kv_heads = kv_width // HD
    width = query_proj.shape[1]
    run = rows // 2
    positions = positions[0]
    grid = Grid(n_dp, n_ctx)
    order, sum_order = grid.block_order(False), grid.block_order(True)
    ring_order, ctx_order = grid.ring_order(), grid.ctx_order()
    places = grid.value_places()

    gains = jnp.stack([attn_gain, ffn_gain], -1)
    gains = jnp.concatenate([gains, jnp.zeros((gains.shape[0], WIDE - 2), BF16)], 1)
    packed = jnp.concatenate([query_proj, key_proj, value_proj, gains], 1)
    down_chain = Chain(gather_weight(grid, down_proj))
    gate_chain = Chain(gather_weight(grid, gate_proj))
    merge_chain = Chain(gather_weight(grid, merge_proj))
    first_chain = Chain(gather_weight(grid, packed, True))
    up_chain = Chain(gather_ring(grid, up_proj))
    all_pos = lax.all_gather(positions[::run], "ctx", axis=0, tiled=True)
    cosine, sine = angles(positions)
    rows_in = layer_in.reshape(rows, model).astype(F32)
    normed_one, factor_one = normalize(rows_in)
    all_pos, factor_one = meet((all_pos, factor_one), first_chain, up_chain)
    factor_one = meet(factor_one, first_chain)
    cosine, sine = meet((cosine, sine), first_chain, up_chain)
    cosine = meet(cosine, first_chain, down_chain)
    first_weights = finish(first_chain)
    attn_all = first_weights[:, : width + 2 * kv_width]
    gain_one = first_weights[:, width + 2 * kv_width].astype(F32)
    gain_two = first_weights[:, width + 2 * kv_width + 1].astype(F32)

    first_in = (normed_one * gain_one).astype(BF16)
    first_in = meet(first_in, down_chain)
    raw = mm(first_in, attn_all, NN)
    queries, own_kv = rotated(raw, cosine, sine, kv_width)
    kv_chain = Chain(gather_keys(grid, own_kv))
    later = all_pos.reshape(n_ctx, 2)[ctx_order].reshape(2 * n_ctx, 1)
    later = later > jnp.repeat(positions[::run], run)[None, :]
    bias = jnp.where(later, MASKED, 0.0).astype(F32)
    bias = meet(bias, kv_chain)
    bias = meet(bias, kv_chain)
    bias = meet(bias, kv_chain, gate_chain, up_chain)
    all_keys, all_values = finish(kv_chain)
    kt, vt = all_keys.T, all_values.T

    grad_rows = out_grad.reshape(rows, model)
    plan = (
        ((), ()),
        ((down_chain, merge_chain, up_chain), (gate_chain,)),
        ((down_chain, merge_chain, gate_chain), ()),
        ((merge_chain, gate_chain, up_chain), ()),
    )
    outs, log_sums = [], []
    for group in range(kv_heads):
        out, log_sum = attend(group, places, bias, queries, all_keys, vt)
        on, hold = plan[group % 4]
        queries, out, grad_rows = meet((queries, out, grad_rows), *on, hold=hold)
        if group == 2:
            down_all = finish(down_chain)
            grad_hidden = mm(grad_rows, down_all, NT)
            queries, grad_hidden = lax.optimization_barrier((queries, grad_hidden))
        outs.append(out)
        log_sums.append(log_sum)
    mixed = jnp.concatenate([out.astype(BF16) for out in outs], 1)
    mixed = meet(mixed, merge_chain)
    merge_all = finish(merge_chain)
    middle = rows_in + mm(mixed, merge_all, NN)
    normed_two, factor_two = normalize(middle)
    second_in = (normed_two * gain_two).astype(BF16)
    second_in = meet(second_in, up_chain)
    up_all = finish(up_chain)
    lift = mm(second_in, up_all, NN)
    lift = meet(lift, gate_chain)
    gate_all = finish(gate_chain)
    gate = mm(second_in, gate_all, NN)
    sigma = jax.nn.sigmoid(gate)
    activated = gate * sigma
    hidden = (activated * lift).astype(BF16)
    grad_gate = (grad_hidden * lift * sigma * (1.0 + gate * (1.0 - sigma))).astype(BF16)
    grad_lift = (grad_hidden * activated).astype(BF16)
    hidden, grad_gate, grad_lift = lax.optimization_barrier((hidden, grad_gate, grad_lift))
    second_turned = turned(second_in, order)
    gate_sum = Chain(reduce_term(grid, second_turned, grad_gate))
    up_sum = Chain(reduce_term(grid, second_turned, grad_lift))
    down_sum = Chain(reduce_ring(grid, turned(hidden, ring_order), grad_rows))
    grad_second = mm(grad_gate, gate_all, NT)
    grad_second, grad_lift = meet((grad_second, grad_lift), gate_sum)
    grad_second = grad_second + mm(grad_lift, up_all, NT)
    grad_norm_two, gain_two_term = norm_back(grad_second, normed_two, factor_two, gain_two)
    grad_middle = grad_rows.astype(F32) + grad_norm_two
    grad_branch = grad_middle.astype(BF16)
    grad_mixed = mm(grad_branch, merge_all, NT).astype(BF16)
    grad_mixed, grad_branch = meet((grad_mixed, grad_branch), down_sum, up_sum)
    first_turned = turned(first_in, order)
    mixed_turned = turned(mixed, order)

    dqs, dkvs = [], []
    for group in range(kv_heads):
        dq, dkv = attend_back(
            group, places, bias, log_sums[group], outs[group], queries, grad_mixed,
            all_keys, all_values, kt,
        )
        dqs.append(dq)
        dkvs.append(dkv)
        if group == kv_heads - 4:
            grad_mixed, dkv = meet((grad_mixed, dkv), gate_sum, down_sum)
        elif group == kv_heads - 3:
            grad_mixed, dkv, grad_branch = meet(
                (grad_mixed, dkv, grad_branch), up_sum, down_sum, hold=(gate_sum,)
            )
            merge_sum = Chain(reduce_term(grid, mixed_turned, grad_branch))
        elif group == kv_heads - 2:
            grad_mixed, dkvs = meet((grad_mixed, dkvs), gate_sum, up_sum, merge_sum, down_sum)
            keys_sum = Chain(reduce_keys(grid, jnp.concatenate(dkvs, 1)))
    dqs, dkv = meet((dqs, dkv), keys_sum, gate_sum, merge_sum, hold=(down_sum,))
    last_keys = Chain(reduce_keys(grid, dkv))
    query_grads = unrotated(unrotate_queries_kernel, dqs, cosine, sine)
    query_sum = Chain(reduce_term(grid, first_turned, query_grads))
    grad_first = mm(query_grads, attn_all[:, :width], NT)
    grad_first = meet(grad_first, last_keys, keys_sum, query_sum, merge_sum)
    grad_first = meet(grad_first, last_keys, keys_sum, down_sum)
    grad_first = meet(grad_first, last_keys, query_sum, hold=(merge_sum,))
    wide = finish(keys_sum)
    dkv_parts = [wide[:, at : at + WIDE] for at in range(0, wide.shape[1], WIDE)]
    dkv_parts.append(finish(last_keys))
    kv_grads = unrotated(unrotate_keys_kernel, dkv_parts, cosine, sine)
    grad_first = grad_first + mm(kv_grads, attn_all[:, width:], NT)
    grad_norm_one, gain_one_term = norm_back(grad_first, normed_one, factor_one, gain_one)
    gain_terms = jnp.stack([gain_one_term, gain_two_term], 0)
    gain_terms = jnp.concatenate([gain_terms, jnp.zeros((WIDE - 2, model), F32)], 0)
    gain_columns = turned(gain_terms.astype(BF16), sum_order)
    last_turned = turned(first_in, sum_order)
    last = Chain(reduce_term(grid, last_turned, kv_grads, gain_columns, around=True))
    input_grad = (grad_middle + grad_norm_one).astype(BF16).reshape(layer_in.shape)
    last.flight, input_grad = lax.optimization_barrier((last.flight, input_grad))
    input_grad = meet(input_grad, last, query_sum, up_sum, down_sum)
    input_grad, hidden = meet((input_grad, hidden), last)
    result = middle + mm(hidden, down_all, NN)
    layer_out = result.astype(BF16).reshape(layer_in.shape)
    input_grad = meet(input_grad, last, query_sum)
    input_grad, layer_out = meet((input_grad, layer_out), last, merge_sum)
    while not last.done:
        input_grad = meet(input_grad, last)
    query_share, last_share = finish(query_sum), finish(last)
    merge_share, gate_share = finish(merge_sum), finish(gate_sum)
    up_share, down_share = finish(up_sum), finish(down_sum)
    return (
        layer_out,
        input_grad,
        last_share[:, 2 * kv_width],
        query_share,
        last_share[:, :kv_width],
        last_share[:, kv_width : 2 * kv_width],
        merge_share,
        last_share[:, 2 * kv_width + 1],
        gate_share,
        up_share,
        down_share,
    )


def solution(mesh):
    acts = P("dp", "ctx", None)
    rows = P(BOTH, None)
    flat = P(BOTH)
    return jax.shard_map(
        functools.partial(body, mesh.shape["dp"], mesh.shape["ctx"]),
        mesh=mesh,
        in_specs=(acts, P("dp", "ctx"), flat, rows, rows, rows, rows, flat, rows, rows, rows, acts),
        out_specs=(acts, acts, flat, rows, rows, rows, rows, flat, rows, rows, rows),
        check_vma=False,
    )
```
